32 devices in a mesh: row: 8 (over y, x, core), col: 4 (over z).
Axes of the slice: x: 2, y: 2, z: 4, core: 2. Of those that a mesh axis runs over, the one named last changes fastest.
Arguments:
- object_field: float32 [2, 2048, 1024], P(None, 'row', 'col'), may hold values from -5 to 5
- probe_field: float32 [2, 128, 128], replicated, may hold values from -5 to 5
- intensities: int32 [8, 4, 4, 128, 128], P('row', 'col'), may hold values from 0 to 2047
- off_rows: int32 [8, 4, 4], P('row', 'col'), may hold values from 0 to 255
- off_cols: int32 [8, 4, 4], P('row', 'col'), may hold values from 0 to 255
- counts: int32 [8, 4], P('row', 'col'), may hold values from 0 to 4, as said below
Outputs:
- object_out: float32 [2, 2048, 1024], P(None, 'row', 'col')
- probe_out: float32 [2, 128, 128], replicated
The draws below stay inside these ranges and needn't reach their ends.
Inputs may be any that keep to these rules, and one draw needn't show every extreme that they name: The counts of tile (r, c) and of tile (r + 4, c) add up to exactly 4; some tile owns 4 positions.
All inputs are finite; a program needn't handle non-finite values.
Results may differ from the reference program's by a relative error of at most 0.0003.
Values sent between devices are 32-bit elements; how exact they have to be, the bound alone decides.
No kernel may reach another device: no remote copies, remote signals or barrier semaphores. Data moves between devices by JAX's collectives and lax.ppermute only.
A program may use at most 64 MiB of HBM per device.

```python
import jax
import jax.numpy as jnp
from jax import lax

P_SIZE = 128
TY = 256
TX = 256
SLOTS = 4
ITERS = 2
GRID_ROWS = 8
GRID_COLS = 4
OY = 2048
OX = 1024


def draw_counts(key, part):
    upper_counts = jax.random.randint(key, (GRID_ROWS // 2, GRID_COLS), 0, SLOTS + 1, dtype=jnp.int32)
    upper_counts = upper_counts.at[0, 0].set(0)
    return jnp.concatenate([upper_counts, SLOTS - upper_counts], axis=0)


def plant(array, stream_key, least, largest):
    dims = array.shape
    index_at = [jax.random.randint(jax.random.fold_in(stream_key, axis), (), 0, dims[axis]) for axis in range(len(dims))]
    array = array.at[tuple(index_at)].set(least)
    longest = dims.index(max(dims))
    index_at[longest] = (index_at[longest] + 1) % dims[longest]
    return array.at[tuple(index_at)].set(largest)


def levels(rng, extent, cuts, smallest, largest):
    level = 1.0
    for dim, parts in cuts:
        heights = jax.random.uniform(jax.random.fold_in(jax.random.fold_in(rng, 6), dim), (parts,), jnp.float32, smallest / len(cuts), largest / len(cuts))
        level = level * jnp.repeat(jnp.exp(heights), extent[dim] // parts).reshape((-1,) + (1,) * (len(extent) - 1 - dim))
    return level


def normal_values(rng, extent, spread, most, shards=(), kind=jnp.bfloat16):
    drawn = spread * jax.random.normal(rng, extent, jnp.float32)
    if shards:
        drawn = drawn * levels(rng, extent, shards, -0.22, 0.18)
    return jnp.clip(drawn, -most, most).astype(kind)


def setup_inputs(seed: int = 0) -> dict:
    seeds = jax.random.split(jax.random.key(seed), 7)
    object_field = normal_values(seeds[0], (2, OY, OX), 0.7, 5.0, ((1, 8), (2, 4)), jnp.float32)
    probe_field = normal_values(seeds[1], (2, P_SIZE, P_SIZE), 0.7, 5.0, (), jnp.float32)
    intensities = plant(jax.random.randint(seeds[2], (GRID_ROWS, GRID_COLS, SLOTS, P_SIZE, P_SIZE), 0, 2048), jax.random.fold_in(seeds[2], 1), 0, 2047).astype(jnp.int32)
    off_rows = plant(jax.random.randint(seeds[3], (GRID_ROWS, GRID_COLS, SLOTS), 0, TY), jax.random.fold_in(seeds[3], 1), 0, TY - 1).astype(jnp.int32)
    off_cols = plant(jax.random.randint(seeds[4], (GRID_ROWS, GRID_COLS, SLOTS), 0, TX), jax.random.fold_in(seeds[4], 1), 0, TX - 1).astype(jnp.int32)
    counts = draw_counts(jax.random.fold_in(seeds[6], 71), 0)
    return {"object_field": object_field, "probe_field": probe_field, "intensities": intensities, "off_rows": off_rows, "off_cols": off_cols, "counts": counts}


STEP_SIZE = 0.25
PROBE_STEP = 1.0
REGULARIZER = 1.0
COUNT_SCALE = 1.0 / 1024.0


def reference(object_field, probe_field, intensities, off_rows, off_cols, counts):
    grid_rows, grid_cols, slots = off_rows.shape
    length = probe_field.shape[1]
    height = object_field.shape[1]
    width = object_field.shape[2]
    tile_rows = height // grid_rows
    tile_cols = width // grid_cols
    slot_index = jnp.arange(slots, dtype=jnp.int32)[None, None, :]
    upper_half = (jnp.arange(grid_rows, dtype=jnp.int32) < grid_rows // 2)[:, None, None]
    count_grid = counts[:, :, None]
    valid_mask = jnp.where(upper_half, slot_index < count_grid, slot_index >= slots - count_grid)
    valid_mask = valid_mask.astype(jnp.float32).reshape(-1)
    row_list = (off_rows + (jnp.arange(grid_rows, dtype=jnp.int32) * tile_rows)[:, None, None]).reshape(-1).astype(jnp.int32)
    col_list = (off_cols + (jnp.arange(grid_cols, dtype=jnp.int32) * tile_cols)[None, :, None]).reshape(-1).astype(jnp.int32)
    measured = intensities.reshape(-1, length, length)
    field_now = object_field
    probe_now = probe_field
    for step in range(ITERS):
        extended = jnp.pad(field_now, ((0, 0), (0, length), (0, length)))
        probe_complex = probe_now[0] + 1j * probe_now[1]
        probe_power = probe_now[0] * probe_now[0] + probe_now[1] * probe_now[1]

        def visit(index, carry):
            totals, grad_sum, light_sum = carry
            anchor = (jnp.int32(0), row_list[index], col_list[index])
            patches = lax.dynamic_slice(extended, anchor, (2, length, length))
            object_complex = patches[0] + 1j * patches[1]
            spectrum = jnp.fft.fft2(probe_complex * object_complex, norm="ortho")
            residual = jnp.real(spectrum) ** 2 + jnp.imag(spectrum) ** 2 - COUNT_SCALE * measured[index].astype(jnp.float32)
            weight = valid_mask[index]
            update = jnp.fft.ifft2(residual * spectrum, norm="ortho") * weight
            object_term = jnp.conj(probe_complex) * update
            probe_term = jnp.conj(object_complex) * update
            piece = jnp.stack([jnp.real(object_term), jnp.imag(object_term), weight * probe_power])
            current = lax.dynamic_slice(totals, (jnp.int32(0), anchor[1], anchor[2]), (3, length, length))
            totals = lax.dynamic_update_slice(totals, current + piece, (jnp.int32(0), anchor[1], anchor[2]))
            grad_sum = grad_sum + jnp.stack([jnp.real(probe_term), jnp.imag(probe_term)])
            light_sum = light_sum + weight * (patches[0] * patches[0] + patches[1] * patches[1])
            return totals, grad_sum, light_sum

        start = (jnp.zeros((3, height + length, width + length), jnp.float32),
                 jnp.zeros((2, length, length), jnp.float32),
                 jnp.zeros((length, length), jnp.float32))
        totals, grad_sum, light_sum = lax.fori_loop(0, row_list.shape[0], visit, start)
        field_now = field_now - STEP_SIZE * totals[:2, :height, :width] / (totals[2, :height, :width] + REGULARIZER)
        probe_now = probe_now - PROBE_STEP * grad_sum / (light_sum + REGULARIZER)
    return field_now, probe_now
```

```python
import math

import jax
import jax.numpy as jnp
import numpy as np
from jax import lax
from jax.experimental import pallas as pl
from jax.experimental.pallas import tpu as pltpu
from jax.sharding import PartitionSpec as P

STEP_SIZE = 0.25
PROBE_STEP = 1.0
REGULARIZER = 1.0
COUNT_SCALE = 1.0 / 1024.0
LANES = 128
VMEM_BYTES = 24 * 1024 * 1024


def dft_parts(length):
    points = np.arange(length)
    angles = (points[:, None] * points[None, :] % length) * (2.0 * math.pi / length)
    cosine = np.cos(angles) / math.sqrt(length)
    sine = np.sin(angles) / math.sqrt(length)
    forward = np.block([[cosine, -sine], [sine, cosine]]).astype(np.float32)
    parts = []
    for table in (forward, forward.T):
        high = table.astype(jnp.bfloat16)
        low = (table - high.astype(np.float32)).astype(jnp.bfloat16)
        parts += [high, low]
    return np.stack(parts)


def split(values):
    high = values.astype(jnp.bfloat16)
    low = (values - high.astype(jnp.float32)).astype(jnp.bfloat16)
    return high, low


def dot(left, right):
    return jnp.dot(left, right, preferred_element_type=jnp.float32)


def right_table(values, table_high, table_low):
    high, low = split(values)
    return dot(high, table_high) + (dot(high, table_low) + dot(low, table_high))


def left_table(table_high, table_low, values):
    high, low = split(values)
    return dot(table_high, high) + (dot(table_low, high) + dot(table_high, low))


def slot_weight(counts_ref, slot, slots):
    count = counts_ref[0, 0]
    upper = lax.axis_index("row") < lax.axis_size("row") // 2
    inside = jnp.where(upper, slot < count, slot >= slots - count)
    return jnp.where(inside, 1.0, 0.0).astype(jnp.float32)


def lane_index(length):
    return lax.broadcasted_iota(jnp.int32, (length, LANES), 1)


def take_patch(ext_ref, channel, row, col, length):
    block = col // LANES
    shift = col % LANES
    turn = (LANES - shift) % LANES
    first = pltpu.roll(ext_ref[channel, block, pl.ds(row, length), :], turn, 1)
    second = pltpu.roll(ext_ref[channel, block + 1, pl.ds(row, length), :], turn, 1)
    return jnp.where(lane_index(length) < LANES - shift, first, second)


def add_patch(dep_ref, channel, row, col, values, length):
    block = col // LANES
    shift = col % LANES
    turned = pltpu.roll(values, shift, 1)
    late = lane_index(length) >= shift
    window = pl.ds(row, length)
    dep_ref[block, channel, window, :] += jnp.where(late, turned, 0.0)
    dep_ref[block + 1, channel, window, :] += jnp.where(late, 0.0, turned)


def position_terms(patches, probe_real, probe_imag, measured_ref, tables_ref, weights, slots, length):
    forward_high, forward_low = tables_ref[0], tables_ref[1]
    backward_high, backward_low = tables_ref[2], tables_ref[3]
    exits = []
    for patch_real, patch_imag in patches:
        exits.append(
            jnp.concatenate(
                [
                    probe_real * patch_real - probe_imag * patch_imag,
                    probe_real * patch_imag + probe_imag * patch_real,
                ],
                axis=1,
            )
        )
    mid = right_table(jnp.concatenate(exits, axis=0), forward_high, forward_low)
    mid = jnp.concatenate(
        [
            jnp.concatenate(
                [
                    mid[s * length : (s + 1) * length, :length],
                    mid[s * length : (s + 1) * length, length:],
                ],
                axis=0,
            )
            for s in range(slots)
        ],
        axis=1,
    )
    freq = left_table(backward_high, backward_low, mid)
    scaled = []
    for s in range(slots):
        freq_real = freq[:length, s * length : (s + 1) * length]
        freq_imag = freq[length:, s * length : (s + 1) * length]
        measured = measured_ref[s].astype(jnp.float32)
        residual = freq_real * freq_real + freq_imag * freq_imag - COUNT_SCALE * measured
        scaled.append(jnp.concatenate([residual * freq_real, residual * freq_imag], axis=0))
    mid = left_table(forward_high, forward_low, jnp.concatenate(scaled, axis=1))
    mid = jnp.concatenate(
        [
            jnp.concatenate(
                [
                    mid[:length, s * length : (s + 1) * length],
                    mid[length:, s * length : (s + 1) * length],
                ],
                axis=1,
            )
            for s in range(slots)
        ],
        axis=0,
    )
    back = right_table(mid, backward_high, backward_low)
    updates = []
    for s in range(slots):
        rows = slice(s * length, (s + 1) * length)
        updates.append((back[rows, :length] * weights[s], back[rows, length:] * weights[s]))
    return updates


def finish_terms(
    patches, updates, probe_real, probe_imag, weights, rows_ref, cols_ref, keep_ref, send_ref, dep_ref, sum_ref, length
):
    slots = len(patches)
    grad_real = jnp.zeros((length, length), jnp.float32)
    grad_imag = grad_real
    light = grad_real
    for s in range(slots):
        (patch_real, patch_imag), (back_real, back_imag) = patches[s], updates[s]
        grad_real += patch_real * back_real + patch_imag * back_imag
        grad_imag += patch_real * back_imag - patch_imag * back_real
        light += weights[s] * (patch_real * patch_real + patch_imag * patch_imag)
    sum_ref[0] = grad_real
    sum_ref[1] = grad_imag
    sum_ref[2] = light
    half = length // 2
    side = lax.axis_index("row") % 2
    keep_ref[...] = sum_ref[:, pl.ds(pl.multiple_of(side * half, half), half), :]
    send_ref[...] = sum_ref[:, pl.ds(pl.multiple_of((1 - side) * half, half), half), :]
    power = probe_real * probe_real + probe_imag * probe_imag
    dep_ref[...] = jnp.zeros_like(dep_ref)
    for s in range(slots):
        back_real, back_imag = updates[s]
        row, col = rows_ref[0, 0, s], cols_ref[0, 0, s]
        add_patch(dep_ref, 0, row, col, probe_real * back_real + probe_imag * back_imag, length)
        add_patch(dep_ref, 1, row, col, probe_real * back_imag - probe_imag * back_real, length)
        add_patch(dep_ref, 2, row, col, weights[s] * power, length)


def first_kernel(
    rows_ref, cols_ref, counts_ref, tile_ref, right_ref, below_ref, corner_ref, probe_ref, measured_ref, tables_ref,
    ext_ref, keep_ref, send_ref, left_out, middle_out, right_out, dep_ref, sum_ref,
):
    length = probe_ref.shape[1]
    slots = measured_ref.shape[0]
    tall = tile_ref.shape[1]
    blocks = tile_ref.shape[2] // LANES
    for channel in range(2):
        for block in range(blocks):
            lanes = slice(block * LANES, (block + 1) * LANES)
            ext_ref[channel, block, :tall, :] = tile_ref[channel, :, lanes]
            ext_ref[channel, block, tall:, :] = below_ref[channel, :, lanes]
        ext_ref[channel, blocks, :tall, :] = right_ref[channel]
        ext_ref[channel, blocks, tall:, :] = corner_ref[channel]
    probe_real, probe_imag = probe_ref[0], probe_ref[1]
    weights = [slot_weight(counts_ref, s, slots) for s in range(slots)]
    patches = [
        [take_patch(ext_ref, channel, rows_ref[0, 0, s], cols_ref[0, 0, s], length) for channel in range(2)]
        for s in range(slots)
    ]
    updates = position_terms(
        patches, probe_real, probe_imag, measured_ref, tables_ref, weights, slots, length
    )
    finish_terms(
        patches, updates, probe_real, probe_imag, weights, rows_ref, cols_ref, keep_ref, send_ref, dep_ref, sum_ref, length
    )
    left_out[...] = dep_ref[0]
    middle_out[...] = dep_ref[1]
    right_out[...] = dep_ref[2]


def strips_kernel(left_ref, middle_ref, right_ref, from_left, from_right, left_out, right_out, top_out, bottom_out):
    left_out[...] = left_ref[...] + from_left[...]
    right_out[...] = right_ref[...] + from_right[...]
    length = top_out.shape[2]
    tall = left_ref.shape[1] - length
    for index, part in enumerate((left_out, middle_ref, right_out)):
        top_out[index] = part[:, :length, :]
        bottom_out[index] = part[:, tall:, :]


def object_kernel(
    rows_ref, cols_ref, ext_ref, left_ref, middle_ref, right_ref, from_above, from_below, tile_out, patches_out, new_ref
):
    length = patches_out.shape[2]
    slots = patches_out.shape[0]
    tall = ext_ref.shape[2] - length
    blocks = tile_out.shape[1]
    inside_row = jnp.where(lax.axis_index("row") < lax.axis_size("row") - 1, 1.0, 0.0).astype(jnp.float32)
    inside_col = jnp.where(lax.axis_index("col") < lax.axis_size("col") - 1, 1.0, 0.0).astype(jnp.float32)
    for block, part in enumerate((left_ref, middle_ref, right_ref)):
        for piece, start, stop in ((0, 0, length), (1, length, tall), (2, tall, tall + length)):
            if start == stop:
                continue
            totals = [part[channel, start:stop, :] for channel in range(3)]
            if piece == 0:
                totals = [totals[channel] + from_above[block, channel] for channel in range(3)]
            if piece == 2:
                totals = [totals[channel] + from_below[block, channel] for channel in range(3)]
            scale = STEP_SIZE / (totals[2] + REGULARIZER)
            if piece == 2:
                scale = scale * inside_row
            if block == blocks:
                scale = scale * inside_col
            for channel in range(2):
                new_ref[channel, block, start:stop, :] = (
                    ext_ref[channel, block, start:stop, :] - scale * totals[channel]
                )
    for channel in range(2):
        tile_out[channel] = new_ref[channel, :blocks, :tall, :]
        for s in range(slots):
            patches_out[s, channel] = take_patch(new_ref, channel, rows_ref[0, 0, s], cols_ref[0, 0, s], length)


def assemble_probe(half_ref, other_ref, side):
    first = side == 0
    return [
        jnp.concatenate(
            [
                jnp.where(first, half_ref[channel], other_ref[channel]),
                jnp.where(first, other_ref[channel], half_ref[channel]),
            ],
            axis=0,
        )
        for channel in range(2)
    ]


def second_kernel(
    rows_ref, cols_ref, counts_ref, patches_ref, half_ref, other_ref, measured_ref, tables_ref,
    keep_ref, send_ref, left_out, middle_out, right_out, dep_ref, sum_ref,
):
    slots = measured_ref.shape[0]
    length = measured_ref.shape[1]
    probe_real, probe_imag = assemble_probe(half_ref, other_ref, lax.axis_index("row") % 2)
    weights = [slot_weight(counts_ref, s, slots) for s in range(slots)]
    patches = [[patches_ref[s, channel] for channel in range(2)] for s in range(slots)]
    updates = position_terms(
        patches, probe_real, probe_imag, measured_ref, tables_ref, weights, slots, length
    )
    finish_terms(
        patches, updates, probe_real, probe_imag, weights, rows_ref, cols_ref, keep_ref, send_ref, dep_ref, sum_ref, length
    )
    left_out[...] = dep_ref[0]
    middle_out[...] = dep_ref[1]
    right_out[...] = dep_ref[2]


def final_kernel(tile_ref, left_ref, middle_ref, from_left, from_above, object_out):
    tall = tile_ref.shape[2]
    length = from_above.shape[2]
    for block in range(tile_ref.shape[1]):
        for start, stop in ((0, length), (length, tall)):
            if block == 0:
                totals = [left_ref[channel, start:stop, :] + from_left[channel, start:stop, :] for channel in range(3)]
            else:
                totals = [middle_ref[channel, start:stop, :] for channel in range(3)]
            if start == 0:
                totals = [totals[channel] + from_above[block, channel] for channel in range(3)]
            scale = STEP_SIZE / (totals[2] + REGULARIZER)
            for channel in range(2):
                object_out[channel, start:stop, block * LANES : (block + 1) * LANES] = (
                    tile_ref[channel, block, start:stop, :] - scale * totals[channel]
                )


def shift(value, axis, steps):
    count = lax.axis_size(axis)
    pairs = [(source, source + steps) for source in range(count) if 0 <= source + steps < count]
    return lax.ppermute(value, axis, pairs)


def flip(value, axis, mask):
    count = lax.axis_size(axis)
    return lax.ppermute(value, axis, [(source, source ^ mask) for source in range(count)])


def sum_over(value, axis, bit):
    count = lax.axis_size(axis)
    while bit < count:
        if 2 * bit < count:
            one, two, three = (flip(value, axis, mask * bit) for mask in (1, 2, 3))
            value = (value + one) + (two + three)
            bit *= 4
        else:
            value = value + flip(value, axis, bit)
            bit *= 2
    return value


def probe_half(half, keep, send):
    total = keep + flip(send, "row", 1)
    total = sum_over(total, "row", 2)
    total = sum_over(total, "col", 1)
    return half - PROBE_STEP * total[:2] / (total[2] + REGULARIZER)


def call(kernel, outs, scratch, args, scalars):
    vmem = pl.BlockSpec(memory_space=pltpu.VMEM)
    smem = pl.BlockSpec(memory_space=pltpu.SMEM)
    return pl.pallas_call(
        kernel,
        out_shape=[jax.ShapeDtypeStruct(shape, jnp.float32) for shape in outs],
        in_specs=[smem] * scalars + [vmem] * (len(args) - scalars),
        out_specs=[vmem] * len(outs),
        scratch_shapes=[pltpu.VMEM(shape, jnp.float32) for shape in scratch],
        compiler_params=pltpu.CompilerParams(vmem_limit_bytes=VMEM_BYTES),
    )(*args)


def local(object_field, probe_field, intensities, off_rows, off_cols, counts):
    tall, wide = object_field.shape[1:]
    length = probe_field.shape[1]
    slots = off_rows.shape[2]
    half = length // 2
    high = tall + length
    blocks = wide // LANES
    tables = jnp.asarray(dft_parts(length))
    measured = intensities.reshape(slots, length, length)
    count_rows, count_cols = lax.axis_size("row"), lax.axis_size("col")

    below = shift(object_field[:, :length, :], "row", -1)
    right = shift(object_field[:, :, :length], "col", -1)
    corner = lax.ppermute(
        object_field[:, :length, :length],
        ("row", "col"),
        [
            ((r + 1) * count_cols + c + 1, r * count_cols + c)
            for r in range(count_rows - 1)
            for c in range(count_cols - 1)
        ],
    )
    strip = (3, high, LANES)
    partial = (3, half, length)
    ext, keep, send, left_part, middle_part, right_part = call(
        first_kernel,
        [(2, blocks + 1, high, LANES), partial, partial, strip, strip, strip],
        [(blocks + 1, 3, high, LANES), (3, length, length)],
        [off_rows, off_cols, counts, object_field, right, below, corner, probe_field, measured, tables],
        3,
    )
    side = lax.axis_index("row") % 2
    own = lax.dynamic_slice(probe_field, (jnp.int32(0), side * half, jnp.int32(0)), (2, half, length))
    new_half = probe_half(own, keep, send)
    new_other = flip(new_half, "row", 1)
    from_right = shift(left_part, "col", -1)
    from_left = shift(right_part, "col", 1)
    edge = (blocks + 1, 3, length, LANES)
    left_part, right_part, top, bottom = call(
        strips_kernel,
        [strip, strip, edge, edge],
        [],
        [left_part, middle_part, right_part, from_left, from_right],
        0,
    )
    from_below = shift(top, "row", -1)
    from_above = shift(bottom, "row", 1)
    tile, patches = call(
        object_kernel,
        [(2, blocks, tall, LANES), (slots, 2, length, length)],
        [(2, blocks + 1, high, LANES)],
        [off_rows, off_cols, ext, left_part, middle_part, right_part, from_above, from_below],
        2,
    )
    keep, send, left_part, middle_part, right_part = call(
        second_kernel,
        [partial, partial, strip, strip, strip],
        [(blocks + 1, 3, high, LANES), (3, length, length)],
        [off_rows, off_cols, counts, patches, new_half, new_other, measured, tables],
        3,
    )
    last_half = probe_half(new_half, keep, send)
    last_other = flip(last_half, "row", 1)
    from_left = shift(right_part, "col", 1)
    bottom = jnp.stack([left_part[:, tall:, :] + from_left[:, tall:, :], middle_part[:, tall:, :]])
    from_above = shift(bottom, "row", 1)
    (object_out,) = call(
        final_kernel,
        [(2, tall, wide)],
        [],
        [tile, left_part, middle_part, from_left, from_above],
        0,
    )
    first = side == 0
    probe_out = jnp.concatenate(
        [jnp.where(first, last_half, last_other), jnp.where(first, last_other, last_half)], axis=1
    )
    return object_out, probe_out


def solution(mesh):
    placed = (
        P(None, "row", "col"),
        P(),
        P("row", "col", None, None, None),
        P("row", "col", None),
        P("row", "col", None),
        P("row", "col"),
    )
    return jax.shard_map(
        local, mesh=mesh, in_specs=placed, out_specs=(P(None, "row", "col"), P()), check_vma=False
    )
```

```python
import functools
import math

import jax
import jax.numpy as jnp
import numpy as np
from jax import lax
from jax.experimental import pallas as pl
from jax.experimental.pallas import tpu as pltpu
from jax.sharding import PartitionSpec as P

STEP_SIZE = 0.25
PROBE_STEP = 1.0
REGULARIZER = 1.0
COUNT_SCALE = 1.0 / 1024.0
LANES = 128
INFO = 8
VMEM_BYTES = 12 * 1024 * 1024


def dft_parts(length):
    points = np.arange(length)
    angles = (points[:, None] * points[None, :] % length) * (2.0 * math.pi / length)
    cosine = np.cos(angles) / math.sqrt(length)
    sine = np.sin(angles) / math.sqrt(length)
    forward = np.block([[cosine, -sine], [sine, cosine]]).astype(np.float32)
    parts = []
    for table in (forward, forward.T):
        high = table.astype(jnp.bfloat16)
        low = (table - high.astype(np.float32)).astype(jnp.bfloat16)
        parts += [high, low]
    return np.stack(parts)


def split(values):
    high = values.astype(jnp.bfloat16)
    low = (values - high.astype(jnp.float32)).astype(jnp.bfloat16)
    return high, low


def dot(left, right):
    return jnp.dot(left, right, preferred_element_type=jnp.float32)


def right_table(values, table_high, table_low):
    high, low = split(values)
    return dot(high, table_high) + (dot(high, table_low) + dot(low, table_high))


def left_table(table_high, table_low, values):
    high, low = split(values)
    return dot(table_high, high) + (dot(table_low, high) + dot(table_high, low))


def parity(axis):
    return lax.axis_index(axis) % 2


def slot_place(info_ref, index, slot, slots):
    row = info_ref[index, 0, slot].astype(jnp.int32)
    col = info_ref[index, 0, slots + slot].astype(jnp.int32)
    return row, col, info_ref[index, 0, 2 * slots + slot]


def lane_index(length):
    return lax.broadcasted_iota(jnp.int32, (length, LANES), 1)


def take_patch(ext_ref, channel, row, col, length):
    block = col // LANES
    shift = col % LANES
    turn = (LANES - shift) % LANES
    first = pltpu.roll(ext_ref[channel, block, pl.ds(row, length), :], turn, 1)
    second = pltpu.roll(ext_ref[channel, block + 1, pl.ds(row, length), :], turn, 1)
    return jnp.where(lane_index(length) < LANES - shift, first, second)


def add_patch(acc_ref, row, col, values, length):
    block = col // LANES
    shift = col % LANES
    turned = pltpu.roll(values, shift, 1)
    late = lane_index(length) >= shift
    window = pl.ds(row, length)
    acc_ref[block, window, :] += jnp.where(late, turned, 0.0)
    acc_ref[block + 1, window, :] += jnp.where(late, 0.0, turned)


def add_light(light_ref, power_ref, row, col, weight, length):
    row, col = row + length, col + length
    inside = (row > 0) & (row < light_ref.shape[1] - length) & (col > 0) & (col < (light_ref.shape[0] - 1) * LANES)

    @pl.when(inside & (weight > 0.0))
    def _():
        add_patch(light_ref, row, col, power_ref[...], length)


def all_light(light_ref, power_ref, info_ref, tall, wide, slots, length):
    across = 1 - 2 * parity("col")
    down = 1 - 2 * parity("row")
    places = [(0, 0), (0, across), (0, -across)]
    places += [(down, step) for step in (-1, 0, 1)] + [(-down, step) for step in (-1, 0, 1)]
    for index, (row_step, col_step) in enumerate(places):
        for s in range(slots):
            row, col, weight = slot_place(info_ref, index, s, slots)
            add_light(light_ref, power_ref, row + row_step * tall, col + col_step * wide, weight, length)


def fill_info(rows_ref, cols_ref, counts_ref, slots):
    lanes = lax.broadcasted_iota(jnp.int32, (INFO, LANES), 1)
    info = jnp.zeros((INFO, LANES), jnp.float32)
    count = counts_ref[0, 0]
    upper = lax.axis_index("row") < lax.axis_size("row") // 2
    for s in range(slots):
        inside = jnp.where(upper, s < count, s >= slots - count)
        weight = jnp.where(inside, 1.0, 0.0).astype(jnp.float32)
        info = jnp.where(lanes == s, rows_ref[0, 0, s].astype(jnp.float32), info)
        info = jnp.where(lanes == slots + s, cols_ref[0, 0, s].astype(jnp.float32), info)
        info = jnp.where(lanes == 2 * slots + s, weight, info)
    return info


def position_terms(patches, probe_real, probe_imag, measured_ref, tables_ref, weights, slots, length):
    forward_high, forward_low = tables_ref[0], tables_ref[1]
    backward_high, backward_low = tables_ref[2], tables_ref[3]
    exits = []
    for patch_real, patch_imag in patches:
        exits.append(
            jnp.concatenate(
                [
                    probe_real * patch_real - probe_imag * patch_imag,
                    probe_real * patch_imag + probe_imag * patch_real,
                ],
                axis=1,
            )
        )
    mid = right_table(jnp.concatenate(exits, axis=0), forward_high, forward_low)
    mid = jnp.concatenate(
        [
            jnp.concatenate(
                [
                    mid[s * length : (s + 1) * length, :length],
                    mid[s * length : (s + 1) * length, length:],
                ],
                axis=0,
            )
            for s in range(slots)
        ],
        axis=1,
    )
    freq = left_table(backward_high, backward_low, mid)
    scaled = []
    for s in range(slots):
        freq_real = freq[:length, s * length : (s + 1) * length]
        freq_imag = freq[length:, s * length : (s + 1) * length]
        measured = measured_ref[s].astype(jnp.float32)
        residual = freq_real * freq_real + freq_imag * freq_imag - COUNT_SCALE * measured
        scaled.append(jnp.concatenate([residual * freq_real, residual * freq_imag], axis=0))
    mid = left_table(forward_high, forward_low, jnp.concatenate(scaled, axis=1))
    mid = jnp.concatenate(
        [
            jnp.concatenate(
                [
                    mid[:length, s * length : (s + 1) * length],
                    mid[length:, s * length : (s + 1) * length],
                ],
                axis=1,
            )
            for s in range(slots)
        ],
        axis=0,
    )
    back = right_table(mid, backward_high, backward_low)
    updates = []
    for s in range(slots):
        rows = slice(s * length, (s + 1) * length)
        updates.append((back[rows, :length] * weights[s], back[rows, length:] * weights[s]))
    return updates


def finish_terms(patches, updates, probe_real, probe_imag, places, keep_ref, send_ref, dep_ref, sum_ref, length):
    slots = len(patches)
    grad_real = jnp.zeros((length, length), jnp.float32)
    grad_imag = grad_real
    light = grad_real
    for s in range(slots):
        (patch_real, patch_imag), (back_real, back_imag) = patches[s], updates[s]
        grad_real += patch_real * back_real + patch_imag * back_imag
        grad_imag += patch_real * back_imag - patch_imag * back_real
        light += places[s][2] * (patch_real * patch_real + patch_imag * patch_imag)
    sum_ref[0] = grad_real
    sum_ref[1] = grad_imag
    sum_ref[2] = light
    half = length // 2
    side = parity("row")
    keep_ref[...] = sum_ref[:, pl.ds(pl.multiple_of(side * half, half), half), :]
    send_ref[...] = sum_ref[:, pl.ds(pl.multiple_of((1 - side) * half, half), half), :]
    dep_ref[...] = jnp.zeros_like(dep_ref)
    high = dep_ref.shape[1] // 2
    for s in range(slots):
        back_real, back_imag = updates[s]
        row, col, _ = places[s]
        add_patch(dep_ref, row, col, probe_real * back_real + probe_imag * back_imag, length)
        add_patch(dep_ref, row + high, col, probe_real * back_imag - probe_imag * back_real, length)


def start_all(pairs, sems):
    copies = [pltpu.make_async_copy(source, target, sems.at[i]) for i, (source, target) in enumerate(pairs)]
    for copy in copies:
        copy.start()
    return copies


def wait_all(copies):
    for copy in copies:
        copy.wait()


def halo_kernel(
    field_ref, probe_ref, measured_ref, tables_ref, rows_ref, cols_ref, counts_ref,
    ext_ref, right_out, below_out, corner_out, probe_out, half_out, measured_out, tables_out, info_out,
    rows_at, cols_at, counts_at, sems,
):
    length = corner_out.shape[1]
    half = half_out.shape[1]
    blocks = ext_ref.shape[1] - 1
    tall = field_ref.shape[1]
    start = pl.multiple_of(parity("row") * half, half)
    pairs = [
        (rows_ref, rows_at),
        (cols_ref, cols_at),
        (counts_ref, counts_at),
        (field_ref.at[:, :, pl.ds(0, length)], right_out),
        (field_ref.at[:, pl.ds(0, length), :], below_out),
        (field_ref.at[:, pl.ds(0, length), pl.ds(0, length)], corner_out),
        (probe_ref, probe_out),
        (probe_ref.at[:, pl.ds(start, half), :], half_out),
        (measured_ref, measured_out),
        (tables_ref, tables_out),
    ]
    for block in range(blocks):
        for channel in range(2):
            pairs.append(
                (
                    field_ref.at[channel, :, pl.ds(block * LANES, LANES)],
                    ext_ref.at[channel, block, pl.ds(0, tall), :],
                )
            )
    copies = start_all(pairs, sems)
    wait_all(copies[:3])
    info_out[...] = fill_info(rows_at, cols_at, counts_at, rows_at.shape[2])
    wait_all(copies[3:])


def split_sides(inner_out, outer_out, dep_ref):
    size = dep_ref.shape[1]
    side = parity("col")
    inner_out[:size] = dep_ref[2 - 2 * side]
    outer_out[:size] = dep_ref[2 * side]


def first_kernel(
    start_ref, right_ref, below_ref, corner_ref, probe_ref, measured_ref, tables_ref, info_ref,
    ext_ref, keep_ref, send_ref, inner_out, middle_out, outer_out, dep_ref, sum_ref, info_at, sems,
):
    copies = start_all([(info_ref, info_at.at[0])], sems)
    length = probe_ref.shape[1]
    slots = measured_ref.shape[0]
    tall = right_ref.shape[1]
    blocks = below_ref.shape[2] // LANES
    for channel in range(2):
        for block in range(blocks):
            lanes = slice(block * LANES, (block + 1) * LANES)
            ext_ref[channel, block, tall:, :] = below_ref[channel, :, lanes]
        ext_ref[channel, blocks, :tall, :] = right_ref[channel]
        ext_ref[channel, blocks, tall:, :] = corner_ref[channel]
    probe_real, probe_imag = probe_ref[0], probe_ref[1]
    wait_all(copies)
    places = [slot_place(info_at, 0, s, slots) for s in range(slots)]
    patches = [
        [take_patch(ext_ref, channel, places[s][0], places[s][1], length) for channel in range(2)] for s in range(slots)
    ]
    weights = [place[2] for place in places]
    updates = position_terms(
        patches, probe_real, probe_imag, measured_ref, tables_ref, weights, slots, length
    )
    finish_terms(patches, updates, probe_real, probe_imag, places, keep_ref, send_ref, dep_ref, sum_ref, length)
    size = dep_ref.shape[1]
    middle_out[...] = dep_ref[1]
    split_sides(inner_out, outer_out, dep_ref)
    inner_out[size:] = info_ref[...]
    outer_out[size:] = info_ref[...]


def strips_kernel(
    inner_ref, middle_ref, outer_ref, from_inner, from_outer, total_out, inner_out, outer_out, infos_out
):
    size = middle_ref.shape[0]
    high = size // 2
    length = (inner_out.shape[0] - 3 * INFO) // 6
    tall = high - length
    side = parity("col")
    total_out[2 - 2 * side] = inner_ref[:size] + from_inner[:size]
    total_out[1] = middle_ref[...]
    total_out[2 * side] = outer_ref[:size] + from_outer[:size]
    side_row = parity("row")
    for block in range(3):
        for channel in range(2):
            rows = slice((2 * block + channel) * length, (2 * block + channel + 1) * length)
            start = channel * high + tall - side_row * tall
            inner_out[rows] = total_out[block, pl.ds(pl.multiple_of(start, 8), length), :]
            start = channel * high + side_row * tall
            outer_out[rows] = total_out[block, pl.ds(pl.multiple_of(start, 8), length), :]
    own, inner, outer = inner_ref[size:], from_inner[size:], from_outer[size:]
    infos_out[0], infos_out[1], infos_out[2] = own, inner, outer
    left = jnp.where(side == 0, outer, inner)
    right = jnp.where(side == 0, inner, outer)
    for index, info in enumerate((left, own, right)):
        rows = slice(6 * length + index * INFO, 6 * length + (index + 1) * INFO)
        inner_out[rows] = info
        outer_out[rows] = info


def object_kernel(
    ext_ref, probe_ref, total_ref, infos_ref, from_inner, from_outer,
    tile_out, patches_out, info_out, new_ref, light_ref, power_ref, info_at, sems,
):
    length = patches_out.shape[2]
    slots = patches_out.shape[0]
    high = ext_ref.shape[2]
    tall = high - length
    blocks = tile_out.shape[1]
    edge = 6 * length
    info_out[0:3] = infos_ref[...]
    for index in range(3):
        info_out[3 + index] = from_inner[edge + index * INFO : edge + (index + 1) * INFO]
        info_out[6 + index] = from_outer[edge + index * INFO : edge + (index + 1) * INFO]
    copies = start_all([(info_out, info_at)], sems)
    power_ref[...] = probe_ref[0] * probe_ref[0] + probe_ref[1] * probe_ref[1]
    light_ref[...] = jnp.zeros_like(light_ref)
    wait_all(copies)
    all_light(light_ref, power_ref, info_at, tall, blocks * LANES, slots, length)
    inside_row = jnp.where(lax.axis_index("row") < lax.axis_size("row") - 1, 1.0, 0.0).astype(jnp.float32)
    inside_col = jnp.where(lax.axis_index("col") < lax.axis_size("col") - 1, 1.0, 0.0).astype(jnp.float32)
    even = parity("row") == 0
    for block in range(blocks + 1):
        for piece, start, stop in ((0, 0, length), (1, length, tall), (2, tall, high)):
            light = light_ref[block + 1, start + length : stop + length, :]
            scale = STEP_SIZE / (light + REGULARIZER)
            if piece == 2:
                scale = scale * inside_row
            if block == blocks:
                scale = scale * inside_col
            for channel in range(2):
                total = total_ref[block, channel * high + start : channel * high + stop]
                rows = slice((2 * block + channel) * length, (2 * block + channel + 1) * length)
                if piece == 0:
                    total = total + jnp.where(even, from_outer[rows], from_inner[rows])
                if piece == 2:
                    total = total + jnp.where(even, from_inner[rows], from_outer[rows])
                new_ref[channel, block, start:stop, :] = ext_ref[channel, block, start:stop, :] - scale * total
    for channel in range(2):
        tile_out[channel] = new_ref[channel, :blocks, :tall, :]
    for s in range(slots):
        row, col, _ = slot_place(info_at, 0, s, slots)
        for channel in range(2):
            patches_out[s, channel] = take_patch(new_ref, channel, row, col, length)


def assemble_probe(half_ref, other_ref, side):
    first = side == 0
    return [
        jnp.concatenate(
            [
                jnp.where(first, half_ref[channel], other_ref[channel]),
                jnp.where(first, other_ref[channel], half_ref[channel]),
            ],
            axis=0,
        )
        for channel in range(2)
    ]


def second_kernel(
    patches_ref, half_ref, other_ref, measured_ref, tables_ref, info_ref,
    keep_ref, send_ref, left_out, middle_out, right_out, dep_ref, sum_ref, info_at, sems,
):
    copies = start_all([(info_ref, info_at.at[0])], sems)
    slots = measured_ref.shape[0]
    length = measured_ref.shape[1]
    probe_real, probe_imag = assemble_probe(half_ref, other_ref, parity("row"))
    patches = [[patches_ref[s, channel] for channel in range(2)] for s in range(slots)]
    wait_all(copies)
    places = [slot_place(info_at, 0, s, slots) for s in range(slots)]
    weights = [place[2] for place in places]
    updates = position_terms(
        patches, probe_real, probe_imag, measured_ref, tables_ref, weights, slots, length
    )
    finish_terms(patches, updates, probe_real, probe_imag, places, keep_ref, send_ref, dep_ref, sum_ref, length)
    left_out[...] = dep_ref[0]
    middle_out[...] = dep_ref[1]
    right_out[...] = dep_ref[2]


def light_kernel(slots, infos_ref, half_ref, other_ref, light_out, light_ref, power_ref, info_at, sems):
    copies = start_all([(infos_ref, info_at)], sems)
    length = power_ref.shape[0]
    tall = light_out.shape[1]
    blocks = light_out.shape[0]
    probe_real, probe_imag = assemble_probe(half_ref, other_ref, parity("row"))
    power_ref[...] = probe_real * probe_real + probe_imag * probe_imag
    light_ref[...] = jnp.zeros_like(light_ref)
    wait_all(copies)
    all_light(light_ref, power_ref, info_at, tall, blocks * LANES, slots, length)
    light_out[...] = STEP_SIZE / (light_ref[1 : 1 + blocks, length : length + tall, :] + REGULARIZER)


def push_kernel(left_ref, middle_ref, from_left, left_out, bottom_out):
    size = middle_ref.shape[0]
    high = size // 2
    length = bottom_out.shape[1] // 2
    tall = high - length
    left_out[...] = left_ref[...] + from_left[...]
    for block, part in enumerate((left_out, middle_ref)):
        for channel in range(2):
            bottom_out[block, channel * length : (channel + 1) * length] = part[
                channel * high + tall : (channel + 1) * high
            ]


def final_kernel(tile_ref, light_ref, left_ref, middle_ref, from_above, half_ref, other_ref, object_out, probe_out):
    tall = tile_ref.shape[2]
    length = from_above.shape[1] // 2
    high = tall + length
    for block, part in enumerate((left_ref, middle_ref)):
        lanes = slice(block * LANES, (block + 1) * LANES)
        for channel in range(2):
            for start, stop in ((0, length), (length, tall)):
                total = part[channel * high + start : channel * high + stop]
                if start == 0:
                    total = total + from_above[block, channel * length : (channel + 1) * length]
                object_out[channel, start:stop, lanes] = (
                    tile_ref[channel, block, start:stop, :] - light_ref[block, start:stop, :] * total
                )
    probe_out[0], probe_out[1] = assemble_probe(half_ref, other_ref, parity("row"))


def shift(value, axis, steps):
    count = lax.axis_size(axis)
    pairs = [(source, source + steps) for source in range(count) if 0 <= source + steps < count]
    return lax.ppermute(value, axis, pairs)


def swap(value, axis, first):
    count = lax.axis_size(axis)
    pairs = []
    for low in range(first, count - 1, 2):
        pairs += [(low, low + 1), (low + 1, low)]
    return lax.ppermute(value, axis, pairs)


def flip(value, axis, mask):
    count = lax.axis_size(axis)
    return lax.ppermute(value, axis, [(source, source ^ mask) for source in range(count)])


def sum_over(value, axis, bit):
    count = lax.axis_size(axis)
    while bit < count:
        value = value + flip(value, axis, bit)
        bit *= 2
    return value


def probe_half(half, keep, send, *gates):
    total = keep + flip(send, "row", 1)
    total = sum_over(total, "row", 2)
    total = sum_over(total, "col", 1)
    return half - PROBE_STEP * total[:2] / (total[2] + REGULARIZER), *gates


def shape_of(spec):
    return spec if isinstance(spec, jax.ShapeDtypeStruct) else jax.ShapeDtypeStruct(spec, jnp.float32)


def call(kernel, outs, scratch, args, aliases={}, space=pltpu.VMEM):
    vmem = pl.BlockSpec(memory_space=pltpu.VMEM)
    return pl.pallas_call(
        kernel,
        out_shape=[shape_of(spec) for spec in outs],
        in_specs=[pl.BlockSpec(memory_space=space)] * len(args),
        out_specs=[vmem] * len(outs),
        scratch_shapes=[pltpu.VMEM(shape, jnp.float32) if isinstance(shape, tuple) else shape for shape in scratch],
        compiler_params=pltpu.CompilerParams(vmem_limit_bytes=VMEM_BYTES),
        input_output_aliases=aliases,
    )(*args)


def local(object_field, probe_field, intensities, off_rows, off_cols, counts):
    tall, wide = object_field.shape[1:]
    length = probe_field.shape[1]
    slots = off_rows.shape[2]
    half = length // 2
    high = tall + length
    blocks = wide // LANES
    tables = jnp.asarray(dft_parts(length))
    measured = intensities.reshape(slots, length, length)
    count_rows, count_cols = lax.axis_size("row"), lax.axis_size("col")

    def info_space(tiles):
        return [pltpu.SMEM((tiles, INFO, LANES), jnp.float32), pltpu.SemaphoreType.DMA((1,))]

    extended = (2, blocks + 1, high, LANES)
    ext, right, below, corner, probe_now, own, measured, tables, info = call(
        halo_kernel,
        [
            extended,
            (2, tall, length),
            (2, length, wide),
            (2, length, length),
            (2, length, length),
            (2, half, length),
            jax.ShapeDtypeStruct(measured.shape, measured.dtype),
            jax.ShapeDtypeStruct(tables.shape, tables.dtype),
            (INFO, LANES),
        ],
        [
            pltpu.SMEM(off_rows.shape, jnp.int32),
            pltpu.SMEM(off_cols.shape, jnp.int32),
            pltpu.SMEM(counts.shape, jnp.int32),
            pltpu.SemaphoreType.DMA((10 + 2 * blocks,)),
        ],
        [object_field, probe_field, measured, tables, off_rows, off_cols, counts],
        space=pltpu.HBM,
    )
    right = shift(right, "col", -1)
    corner = lax.ppermute(
        corner,
        ("row", "col"),
        [
            ((r + 1) * count_cols + c + 1, r * count_cols + c)
            for r in range(count_rows - 1)
            for c in range(count_cols - 1)
        ],
    )
    below = shift(below, "row", -1)
    size = 2 * high
    strip = (size + INFO, LANES)
    partial = (3, half, length)
    deposits = [(blocks + 1, size, LANES), (3, length, length)] + info_space(1)
    ext, keep, send, inner, middle, outer = call(
        first_kernel,
        [extended, partial, partial, strip, (size, LANES), strip],
        deposits,
        [ext, right, below, corner, probe_now, measured, tables, info],
        aliases={0: 0},
    )
    from_inner = swap(inner, "col", 0)
    from_outer = swap(outer, "col", 1)
    new_half, from_inner, from_outer = probe_half(own, keep, send, from_inner, from_outer)
    new_other = flip(new_half, "row", 1)
    edge = (2 * (blocks + 1) * length + 3 * INFO, LANES)
    total, inner, outer, infos = call(
        strips_kernel,
        [(blocks + 1, size, LANES), edge, edge, (3, INFO, LANES)],
        [],
        [inner, middle, outer, from_inner, from_outer],
    )
    from_inner = swap(inner, "row", 0)
    from_outer = swap(outer, "row", 1)
    padded = (blocks + 3, high + 2 * length, LANES)
    tile, patches, infos = call(
        object_kernel,
        [(2, blocks, tall, LANES), (slots, 2, length, length), (9, INFO, LANES)],
        [extended, padded, (length, length)] + info_space(9),
        [ext, probe_now, total, infos, from_inner, from_outer],
    )
    keep, send, left, middle, right = call(
        second_kernel,
        [partial, partial, (size, LANES), (size, LANES), (size, LANES)],
        deposits,
        [patches, new_half, new_other, measured, tables, info],
    )
    from_left = shift(right, "col", 1)
    padded = (blocks + 2, tall + 2 * length, LANES)
    (light,) = call(
        functools.partial(light_kernel, slots),
        [(blocks, tall, LANES)],
        [padded, (length, length)] + info_space(9),
        [infos, new_half, new_other],
    )
    last_half, from_left = probe_half(new_half, keep, send, from_left)
    last_other = flip(last_half, "row", 1)
    left, bottom = call(
        push_kernel, [(size, LANES), (blocks, 2 * length, LANES)], [], [left, middle, from_left]
    )
    from_above = shift(bottom, "row", 1)
    return call(
        final_kernel,
        [(2, tall, wide), (2, length, length)],
        [],
        [tile, light, left, middle, from_above, last_half, last_other],
    )


def solution(mesh):
    placed = (
        P(None, "row", "col"),
        P(),
        P("row", "col", None, None, None),
        P("row", "col", None),
        P("row", "col", None),
        P("row", "col"),
    )
    return jax.shard_map(
        local, mesh=mesh, in_specs=placed, out_specs=(P(None, "row", "col"), P()), check_vma=False
    )
```

```python
import functools
import math

import jax
import jax.numpy as jnp
import numpy as np
from jax import lax
from jax.experimental import pallas as pl
from jax.experimental.pallas import tpu as pltpu
from jax.sharding import PartitionSpec as P

STEP_SIZE = 0.25
PROBE_STEP = 1.0
REGULARIZER = 1.0
COUNT_SCALE = 1.0 / 1024.0
LANES = 128
INFO = 8
VMEM_BYTES = 12 * 1024 * 1024


def dft_parts(length):
    points = np.arange(length)
    angles = (points[:, None] * points[None, :] % length) * (2.0 * math.pi / length)
    cosine = np.cos(angles) / math.sqrt(length)
    sine = np.sin(angles) / math.sqrt(length)
    forward = np.block([[cosine, -sine], [sine, cosine]]).astype(np.float32)
    parts = []
    for table in (forward, forward.T):
        high = table.astype(jnp.bfloat16)
        low = (table - high.astype(np.float32)).astype(jnp.bfloat16)
        parts += [high, low]
    return np.stack(parts)


def split(values):
    high = values.astype(jnp.bfloat16)
    low = (values - high.astype(jnp.float32)).astype(jnp.bfloat16)
    return high, low


def dot(left, right):
    return jnp.dot(left, right, preferred_element_type=jnp.float32)


def right_table(values, table_high, table_low):
    high, low = split(values)
    return dot(high, table_high) + (dot(high, table_low) + dot(low, table_high))


def left_table(table_high, table_low, values):
    high, low = split(values)
    return dot(table_high, high) + (dot(table_low, high) + dot(table_high, low))


def parity(axis):
    return lax.axis_index(axis) % 2


def slot_place(info_ref, index, slot, slots):
    row = info_ref[index, 0, slot].astype(jnp.int32)
    col = info_ref[index, 0, slots + slot].astype(jnp.int32)
    return row, col, info_ref[index, 0, 2 * slots + slot]


def lane_index(length):
    return lax.broadcasted_iota(jnp.int32, (length, LANES), 1)


def take_patch(ext_ref, channel, row, col, length):
    block = col // LANES
    shift = col % LANES
    turn = (LANES - shift) % LANES
    first = pltpu.roll(ext_ref[channel, block, pl.ds(row, length), :], turn, 1)
    second = pltpu.roll(ext_ref[channel, block + 1, pl.ds(row, length), :], turn, 1)
    return jnp.where(lane_index(length) < LANES - shift, first, second)


def add_patch(acc_ref, row, col, values, length):
    block = col // LANES
    shift = col % LANES
    turned = pltpu.roll(values, shift, 1)
    late = lane_index(length) >= shift
    window = pl.ds(row, length)
    acc_ref[block, window, :] += jnp.where(late, turned, 0.0)
    acc_ref[block + 1, window, :] += jnp.where(late, 0.0, turned)


def add_light(light_ref, power_ref, row, col, weight, length):
    row, col = row + length, col + length
    inside = (row > 0) & (row < light_ref.shape[1] - length) & (col > 0) & (col < (light_ref.shape[0] - 1) * LANES)

    @pl.when(inside & (weight > 0.0))
    def _():
        add_patch(light_ref, row, col, power_ref[...], length)


def all_light(light_ref, power_ref, info_ref, tall, wide, slots, length):
    across = 1 - 2 * parity("col")
    down = 1 - 2 * parity("row")
    places = [(0, 0), (0, across), (0, -across)]
    places += [(down, step) for step in (-1, 0, 1)] + [(-down, step) for step in (-1, 0, 1)]
    for index, (row_step, col_step) in enumerate(places):
        for s in range(slots):
            row, col, weight = slot_place(info_ref, index, s, slots)
            add_light(light_ref, power_ref, row + row_step * tall, col + col_step * wide, weight, length)


def fill_info(rows_ref, cols_ref, counts_ref, slots):
    lanes = lax.broadcasted_iota(jnp.int32, (INFO, LANES), 1)
    info = jnp.zeros((INFO, LANES), jnp.float32)
    count = counts_ref[0, 0]
    upper = lax.axis_index("row") < lax.axis_size("row") // 2
    for s in range(slots):
        inside = jnp.where(upper, s < count, s >= slots - count)
        weight = jnp.where(inside, 1.0, 0.0).astype(jnp.float32)
        info = jnp.where(lanes == s, rows_ref[0, 0, s].astype(jnp.float32), info)
        info = jnp.where(lanes == slots + s, cols_ref[0, 0, s].astype(jnp.float32), info)
        info = jnp.where(lanes == 2 * slots + s, weight, info)
    return info


def position_terms(patches, probe_real, probe_imag, measured_ref, tables_ref, weights, slots, length):
    forward_high, forward_low = tables_ref[0], tables_ref[1]
    backward_high, backward_low = tables_ref[2], tables_ref[3]
    exits = []
    for patch_real, patch_imag in patches:
        exits.append(
            jnp.concatenate(
                [
                    probe_real * patch_real - probe_imag * patch_imag,
                    probe_real * patch_imag + probe_imag * patch_real,
                ],
                axis=1,
            )
        )
    mid = right_table(jnp.concatenate(exits, axis=0), forward_high, forward_low)
    mid = jnp.concatenate(
        [
            jnp.concatenate(
                [
                    mid[s * length : (s + 1) * length, :length],
                    mid[s * length : (s + 1) * length, length:],
                ],
                axis=0,
            )
            for s in range(slots)
        ],
        axis=1,
    )
    freq = left_table(backward_high, backward_low, mid)
    scaled = []
    for s in range(slots):
        freq_real = freq[:length, s * length : (s + 1) * length]
        freq_imag = freq[length:, s * length : (s + 1) * length]
        measured = measured_ref[s].astype(jnp.float32)
        residual = freq_real * freq_real + freq_imag * freq_imag - COUNT_SCALE * measured
        scaled.append(jnp.concatenate([residual * freq_real, residual * freq_imag], axis=0))
    mid = left_table(forward_high, forward_low, jnp.concatenate(scaled, axis=1))
    mid = jnp.concatenate(
        [
            jnp.concatenate(
                [
                    mid[:length, s * length : (s + 1) * length],
                    mid[length:, s * length : (s + 1) * length],
                ],
                axis=1,
            )
            for s in range(slots)
        ],
        axis=0,
    )
    back = right_table(mid, backward_high, backward_low)
    updates = []
    for s in range(slots):
        rows = slice(s * length, (s + 1) * length)
        updates.append((back[rows, :length] * weights[s], back[rows, length:] * weights[s]))
    return updates


def finish_terms(patches, updates, probe_real, probe_imag, places, keep_ref, send_ref, dep_ref, sum_ref, length):
    slots = len(patches)
    grad_real = jnp.zeros((length, length), jnp.float32)
    grad_imag = grad_real
    light = grad_real
    for s in range(slots):
        (patch_real, patch_imag), (back_real, back_imag) = patches[s], updates[s]
        grad_real += patch_real * back_real + patch_imag * back_imag
        grad_imag += patch_real * back_imag - patch_imag * back_real
        light += places[s][2] * (patch_real * patch_real + patch_imag * patch_imag)
    sum_ref[0] = grad_real
    sum_ref[1] = grad_imag
    sum_ref[2] = light
    half = length // 2
    side = parity("row")
    keep_ref[...] = sum_ref[:, pl.ds(pl.multiple_of(side * half, half), half), :]
    send_ref[...] = sum_ref[:, pl.ds(pl.multiple_of((1 - side) * half, half), half), :]
    dep_ref[...] = jnp.zeros_like(dep_ref)
    high = dep_ref.shape[1] // 2
    for s in range(slots):
        back_real, back_imag = updates[s]
        row, col, _ = places[s]
        add_patch(dep_ref, row, col, probe_real * back_real + probe_imag * back_imag, length)
        add_patch(dep_ref, row + high, col, probe_real * back_imag - probe_imag * back_real, length)


def start_all(pairs, sems):
    copies = [pltpu.make_async_copy(source, target, sems.at[i]) for i, (source, target) in enumerate(pairs)]
    for copy in copies:
        copy.start()
    return copies


def wait_all(copies):
    for copy in copies:
        copy.wait()


def halo_kernel(field_ref, ext_ref, right_out, below_out, corner_out, sems):
    length = corner_out.shape[1]
    blocks = ext_ref.shape[1] - 1
    tall = field_ref.shape[1]
    pairs = [
        (field_ref.at[:, :, pl.ds(0, length)], right_out),
        (field_ref.at[:, pl.ds(0, length), :], below_out),
        (field_ref.at[:, pl.ds(0, length), pl.ds(0, length)], corner_out),
    ]
    for block in range(blocks):
        for channel in range(2):
            pairs.append(
                (
                    field_ref.at[channel, :, pl.ds(block * LANES, LANES)],
                    ext_ref.at[channel, block, pl.ds(0, tall), :],
                )
            )
    wait_all(start_all(pairs, sems))


def load_kernel(
    probe_ref, measured_ref, tables_ref, rows_ref, cols_ref, counts_ref,
    probe_out, half_out, measured_out, tables_out, info_out, rows_at, cols_at, counts_at, sems,
):
    half = half_out.shape[1]
    start = pl.multiple_of(parity("row") * half, half)
    pairs = [
        (rows_ref, rows_at),
        (cols_ref, cols_at),
        (counts_ref, counts_at),
        (probe_ref, probe_out),
        (probe_ref.at[:, pl.ds(start, half), :], half_out),
        (measured_ref, measured_out),
        (tables_ref, tables_out),
    ]
    copies = start_all(pairs, sems)
    wait_all(copies[:3])
    info_out[...] = fill_info(rows_at, cols_at, counts_at, rows_at.shape[2])
    wait_all(copies[3:])


def split_sides(inner_out, outer_out, dep_ref):
    size = dep_ref.shape[1]
    side = parity("col")
    inner_out[:size] = dep_ref[2 - 2 * side]
    outer_out[:size] = dep_ref[2 * side]


def first_kernel(
    start_ref, right_ref, below_ref, corner_ref, probe_ref, measured_ref, tables_ref, info_ref,
    ext_ref, keep_ref, send_ref, inner_out, middle_out, outer_out, dep_ref, sum_ref, info_at, sems,
):
    copies = start_all([(info_ref, info_at.at[0])], sems)
    length = probe_ref.shape[1]
    slots = measured_ref.shape[0]
    tall = right_ref.shape[1]
    blocks = below_ref.shape[2] // LANES
    for channel in range(2):
        for block in range(blocks):
            lanes = slice(block * LANES, (block + 1) * LANES)
            ext_ref[channel, block, tall:, :] = below_ref[channel, :, lanes]
        ext_ref[channel, blocks, :tall, :] = right_ref[channel]
        ext_ref[channel, blocks, tall:, :] = corner_ref[channel]
    probe_real, probe_imag = probe_ref[0], probe_ref[1]
    wait_all(copies)
    places = [slot_place(info_at, 0, s, slots) for s in range(slots)]
    patches = [
        [take_patch(ext_ref, channel, places[s][0], places[s][1], length) for channel in range(2)] for s in range(slots)
    ]
    weights = [place[2] for place in places]
    updates = position_terms(
        patches, probe_real, probe_imag, measured_ref, tables_ref, weights, slots, length
    )
    finish_terms(patches, updates, probe_real, probe_imag, places, keep_ref, send_ref, dep_ref, sum_ref, length)
    size = dep_ref.shape[1]
    middle_out[...] = dep_ref[1]
    split_sides(inner_out, outer_out, dep_ref)
    inner_out[size:] = info_ref[...]
    outer_out[size:] = info_ref[...]


def strips_kernel(
    inner_ref, middle_ref, outer_ref, from_inner, from_outer, total_out, inner_out, outer_out, infos_out
):
    size = middle_ref.shape[0]
    high = size // 2
    length = (inner_out.shape[0] - 3 * INFO) // 6
    tall = high - length
    side = parity("col")
    total_out[2 - 2 * side] = inner_ref[:size] + from_inner[:size]
    total_out[1] = middle_ref[...]
    total_out[2 * side] = outer_ref[:size] + from_outer[:size]
    side_row = parity("row")
    for block in range(3):
        for channel in range(2):
            rows = slice((2 * block + channel) * length, (2 * block + channel + 1) * length)
            start = channel * high + tall - side_row * tall
            inner_out[rows] = total_out[block, pl.ds(pl.multiple_of(start, 8), length), :]
            start = channel * high + side_row * tall
            outer_out[rows] = total_out[block, pl.ds(pl.multiple_of(start, 8), length), :]
    own, inner, outer = inner_ref[size:], from_inner[size:], from_outer[size:]
    infos_out[0], infos_out[1], infos_out[2] = own, inner, outer
    left = jnp.where(side == 0, outer, inner)
    right = jnp.where(side == 0, inner, outer)
    for index, info in enumerate((left, own, right)):
        rows = slice(6 * length + index * INFO, 6 * length + (index + 1) * INFO)
        inner_out[rows] = info
        outer_out[rows] = info


def object_kernel(
    ext_ref, probe_ref, total_ref, infos_ref, from_inner, from_outer,
    tile_out, patches_out, info_out, new_ref, light_ref, power_ref, info_at, sems,
):
    length = patches_out.shape[2]
    slots = patches_out.shape[0]
    high = ext_ref.shape[2]
    tall = high - length
    blocks = tile_out.shape[1]
    edge = 6 * length
    info_out[0:3] = infos_ref[...]
    for index in range(3):
        info_out[3 + index] = from_inner[edge + index * INFO : edge + (index + 1) * INFO]
        info_out[6 + index] = from_outer[edge + index * INFO : edge + (index + 1) * INFO]
    copies = start_all([(info_out, info_at)], sems)
    power_ref[...] = probe_ref[0] * probe_ref[0] + probe_ref[1] * probe_ref[1]
    light_ref[...] = jnp.zeros_like(light_ref)
    wait_all(copies)
    all_light(light_ref, power_ref, info_at, tall, blocks * LANES, slots, length)
    inside_row = jnp.where(lax.axis_index("row") < lax.axis_size("row") - 1, 1.0, 0.0).astype(jnp.float32)
    inside_col = jnp.where(lax.axis_index("col") < lax.axis_size("col") - 1, 1.0, 0.0).astype(jnp.float32)
    even = parity("row") == 0
    for block in range(blocks + 1):
        for piece, start, stop in ((0, 0, length), (1, length, tall), (2, tall, high)):
            light = light_ref[block + 1, start + length : stop + length, :]
            scale = STEP_SIZE / (light + REGULARIZER)
            if piece == 2:
                scale = scale * inside_row
            if block == blocks:
                scale = scale * inside_col
            for channel in range(2):
                total = total_ref[block, channel * high + start : channel * high + stop]
                rows = slice((2 * block + channel) * length, (2 * block + channel + 1) * length)
                if piece == 0:
                    total = total + jnp.where(even, from_outer[rows], from_inner[rows])
                if piece == 2:
                    total = total + jnp.where(even, from_inner[rows], from_outer[rows])
                new_ref[channel, block, start:stop, :] = ext_ref[channel, block, start:stop, :] - scale * total
    for channel in range(2):
        tile_out[channel] = new_ref[channel, :blocks, :tall, :]
    for s in range(slots):
        row, col, _ = slot_place(info_at, 0, s, slots)
        for channel in range(2):
            patches_out[s, channel] = take_patch(new_ref, channel, row, col, length)


def assemble_probe(half_ref, other_ref, side):
    first = side == 0
    return [
        jnp.concatenate(
            [
                jnp.where(first, half_ref[channel], other_ref[channel]),
                jnp.where(first, other_ref[channel], half_ref[channel]),
            ],
            axis=0,
        )
        for channel in range(2)
    ]


def second_kernel(
    patches_ref, half_ref, other_ref, measured_ref, tables_ref, info_ref,
    keep_ref, send_ref, left_out, middle_out, right_out, dep_ref, sum_ref, info_at, sems,
):
    copies = start_all([(info_ref, info_at.at[0])], sems)
    slots = measured_ref.shape[0]
    length = measured_ref.shape[1]
    probe_real, probe_imag = assemble_probe(half_ref, other_ref, parity("row"))
    patches = [[patches_ref[s, channel] for channel in range(2)] for s in range(slots)]
    wait_all(copies)
    places = [slot_place(info_at, 0, s, slots) for s in range(slots)]
    weights = [place[2] for place in places]
    updates = position_terms(
        patches, probe_real, probe_imag, measured_ref, tables_ref, weights, slots, length
    )
    finish_terms(patches, updates, probe_real, probe_imag, places, keep_ref, send_ref, dep_ref, sum_ref, length)
    left_out[...] = dep_ref[0]
    middle_out[...] = dep_ref[1]
    right_out[...] = dep_ref[2]


def light_kernel(slots, infos_ref, half_ref, other_ref, light_out, light_ref, power_ref, info_at, sems):
    copies = start_all([(infos_ref, info_at)], sems)
    length = power_ref.shape[0]
    tall = light_out.shape[1]
    blocks = light_out.shape[0]
    probe_real, probe_imag = assemble_probe(half_ref, other_ref, parity("row"))
    power_ref[...] = probe_real * probe_real + probe_imag * probe_imag
    light_ref[...] = jnp.zeros_like(light_ref)
    wait_all(copies)
    all_light(light_ref, power_ref, info_at, tall, blocks * LANES, slots, length)
    light_out[...] = STEP_SIZE / (light_ref[1 : 1 + blocks, length : length + tall, :] + REGULARIZER)


def push_kernel(left_ref, middle_ref, from_left, left_out, bottom_out):
    size = middle_ref.shape[0]
    high = size // 2
    length = bottom_out.shape[1] // 2
    tall = high - length
    left_out[...] = left_ref[...] + from_left[...]
    for block, part in enumerate((left_out, middle_ref)):
        for channel in range(2):
            bottom_out[block, channel * length : (channel + 1) * length] = part[
                channel * high + tall : (channel + 1) * high
            ]


def final_kernel(tile_ref, light_ref, left_ref, middle_ref, from_above, half_ref, other_ref, object_out, probe_out):
    tall = tile_ref.shape[2]
    length = from_above.shape[1] // 2
    high = tall + length
    for block, part in enumerate((left_ref, middle_ref)):
        lanes = slice(block * LANES, (block + 1) * LANES)
        for channel in range(2):
            for start, stop in ((0, length), (length, tall)):
                total = part[channel * high + start : channel * high + stop]
                if start == 0:
                    total = total + from_above[block, channel * length : (channel + 1) * length]
                object_out[channel, start:stop, lanes] = (
                    tile_ref[channel, block, start:stop, :] - light_ref[block, start:stop, :] * total
                )
    probe_out[0], probe_out[1] = assemble_probe(half_ref, other_ref, parity("row"))


def shift(value, axis, steps):
    count = lax.axis_size(axis)
    pairs = [(source, source + steps) for source in range(count) if 0 <= source + steps < count]
    return lax.ppermute(value, axis, pairs)


def swap(value, axis, first):
    count = lax.axis_size(axis)
    pairs = []
    for low in range(first, count - 1, 2):
        pairs += [(low, low + 1), (low + 1, low)]
    return lax.ppermute(value, axis, pairs)


def flip(value, axis, mask):
    count = lax.axis_size(axis)
    return lax.ppermute(value, axis, [(source, source ^ mask) for source in range(count)])


def tie(*values):
    return lax.optimization_barrier(values)


def butterfly(total, axis, first, stop=None):
    bit = first
    while bit < (stop or lax.axis_size(axis)):
        total = total + flip(total, axis, bit)
        bit *= 2
    return total


def stepped(half, total):
    return half - PROBE_STEP * total[:2] / (total[2] + REGULARIZER)


def shape_of(spec):
    return spec if isinstance(spec, jax.ShapeDtypeStruct) else jax.ShapeDtypeStruct(spec, jnp.float32)


def call(kernel, outs, scratch, args, aliases={}, space=pltpu.VMEM):
    vmem = pl.BlockSpec(memory_space=pltpu.VMEM)
    return pl.pallas_call(
        kernel,
        out_shape=[shape_of(spec) for spec in outs],
        in_specs=[pl.BlockSpec(memory_space=space)] * len(args),
        out_specs=[vmem] * len(outs),
        scratch_shapes=[pltpu.VMEM(shape, jnp.float32) if isinstance(shape, tuple) else shape for shape in scratch],
        compiler_params=pltpu.CompilerParams(vmem_limit_bytes=VMEM_BYTES),
        input_output_aliases=aliases,
    )(*args)


def local(object_field, probe_field, intensities, off_rows, off_cols, counts):
    tall, wide = object_field.shape[1:]
    length = probe_field.shape[1]
    slots = off_rows.shape[2]
    half = length // 2
    high = tall + length
    blocks = wide // LANES
    tables = jnp.asarray(dft_parts(length))
    measured = intensities.reshape(slots, length, length)
    count_rows, count_cols = lax.axis_size("row"), lax.axis_size("col")

    def info_space(tiles):
        return [pltpu.SMEM((tiles, INFO, LANES), jnp.float32), pltpu.SemaphoreType.DMA((1,))]

    extended = (2, blocks + 1, high, LANES)
    ext, right, below, corner = call(
        halo_kernel,
        [extended, (2, tall, length), (2, length, wide), (2, length, length)],
        [pltpu.SemaphoreType.DMA((3 + 2 * blocks,))],
        [object_field],
        space=pl.ANY,
    )
    probe_now, own, measured, tables, info = call(
        load_kernel,
        [
            (2, length, length),
            (2, half, length),
            jax.ShapeDtypeStruct(measured.shape, measured.dtype),
            jax.ShapeDtypeStruct(tables.shape, tables.dtype),
            (INFO, LANES),
        ],
        [
            pltpu.SMEM(off_rows.shape, jnp.int32),
            pltpu.SMEM(off_cols.shape, jnp.int32),
            pltpu.SMEM(counts.shape, jnp.int32),
            pltpu.SemaphoreType.DMA((7,)),
        ],
        [probe_field, measured, tables, off_rows, off_cols, counts],
        space=pl.ANY,
    )
    right = shift(right, "col", -1)
    corner = lax.ppermute(
        corner,
        ("row", "col"),
        [
            ((r + 1) * count_cols + c + 1, r * count_cols + c)
            for r in range(count_rows - 1)
            for c in range(count_cols - 1)
        ],
    )
    below = shift(below, "row", -1)
    size = 2 * high
    strip = (size + INFO, LANES)
    partial = (3, half, length)
    deposits = [(blocks + 1, size, LANES), (3, length, length)] + info_space(1)
    ext, keep, send, inner, middle, outer = call(
        first_kernel,
        [extended, partial, partial, strip, (size, LANES), strip],
        deposits,
        [ext, right, below, corner, probe_now, measured, tables, info],
        aliases={0: 0},
    )
    last_row, last_col = count_rows // 2, count_cols // 2
    edge = (2 * (blocks + 1) * length + 3 * INFO, LANES)
    padded = (blocks + 3, high + 2 * length, LANES)

    from_inner = swap(inner, "col", 0)
    from_outer = swap(outer, "col", 1)
    part = keep + flip(send, "row", 1)
    part = butterfly(part, "row", 2, last_row)
    part = butterfly(part, "row", last_row)
    total, inner, outer, infos = call(
        strips_kernel,
        [(blocks + 1, size, LANES), edge, edge, (3, INFO, LANES)],
        [],
        [inner, middle, outer, from_inner, from_outer],
    )
    from_inner = swap(inner, "row", 0)
    from_outer = swap(outer, "row", 1)
    part = butterfly(part, "col", 1, last_col)
    part = butterfly(part, "col", last_col)
    new_half = stepped(own, part)
    tile, patches, infos = call(
        object_kernel,
        [(2, blocks, tall, LANES), (slots, 2, length, length), (9, INFO, LANES)],
        [extended, padded, (length, length)] + info_space(9),
        [ext, probe_now, total, infos, from_inner, from_outer],
    )
    new_other = flip(new_half, "row", 1)

    keep, send, left, middle, right = call(
        second_kernel,
        [partial, partial, (size, LANES), (size, LANES), (size, LANES)],
        deposits,
        [patches, new_half, new_other, measured, tables, info],
    )
    padded = (blocks + 2, tall + 2 * length, LANES)
    (light,) = call(
        functools.partial(light_kernel, slots),
        [(blocks, tall, LANES)],
        [padded, (length, length)] + info_space(9),
        [infos, new_half, new_other],
    )
    from_left = shift(right, "col", 1)
    part = keep + flip(send, "row", 1)
    part = butterfly(part, "row", 2, last_row)
    part = butterfly(part, "row", last_row)
    left, bottom = call(
        push_kernel, [(size, LANES), (blocks, 2 * length, LANES)], [], [left, middle, from_left]
    )
    from_above = shift(bottom, "row", 1)
    part = butterfly(part, "col", 1, last_col)
    part = butterfly(part, "col", last_col)
    last_half = stepped(new_half, part)
    last_other = flip(last_half, "row", 1)
    return call(
        final_kernel,
        [(2, tall, wide), (2, length, length)],
        [],
        [tile, light, left, middle, from_above, last_half, last_other],
    )


def solution(mesh):
    placed = (
        P(None, "row", "col"),
        P(),
        P("row", "col", None, None, None),
        P("row", "col", None),
        P("row", "col", None),
        P("row", "col"),
    )
    return jax.shard_map(
        local, mesh=mesh, in_specs=placed, out_specs=(P(None, "row", "col"), P()), check_vma=False
    )
```

```python
import functools
import math

import jax
import jax.numpy as jnp
import numpy as np
from jax import lax
from jax.experimental import pallas as pl
from jax.experimental.pallas import tpu as pltpu
from jax.sharding import PartitionSpec as P

STEP_SIZE = 0.25
PROBE_STEP = 1.0
REGULARIZER = 1.0
COUNT_SCALE = 1.0 / 1024.0
LANES = 128
INFO = 8
VMEM_BYTES = 12 * 1024 * 1024


def dft_parts(length):
    points = np.arange(length)
    angles = (points[:, None] * points[None, :] % length) * (2.0 * math.pi / length)
    cosine = np.cos(angles) / math.sqrt(length)
    sine = np.sin(angles) / math.sqrt(length)
    forward = np.block([[cosine, -sine], [sine, cosine]]).astype(np.float32)
    parts = []
    for table in (forward, forward.T):
        high = table.astype(jnp.bfloat16)
        low = (table - high.astype(np.float32)).astype(jnp.bfloat16)
        parts += [high, low]
    return np.stack(parts)


def split(values):
    high = values.astype(jnp.bfloat16)
    low = (values - high.astype(jnp.float32)).astype(jnp.bfloat16)
    return high, low


def dot(left, right):
    return jnp.dot(left, right, preferred_element_type=jnp.float32)


def right_table(values, table_high, table_low):
    high, low = split(values)
    return dot(high, table_high) + (dot(high, table_low) + dot(low, table_high))


def left_table(table_high, table_low, values):
    high, low = split(values)
    return dot(table_high, high) + (dot(table_low, high) + dot(table_high, low))


def parity(axis):
    return lax.axis_index(axis) % 2


def slot_place(info_ref, index, slot, slots):
    row = info_ref[index, 0, slot].astype(jnp.int32)
    col = info_ref[index, 0, slots + slot].astype(jnp.int32)
    return row, col, info_ref[index, 0, 2 * slots + slot]


def lane_index(length):
    return lax.broadcasted_iota(jnp.int32, (length, LANES), 1)


def take_patch(ext_ref, channel, row, col, length):
    block = col // LANES
    shift = col % LANES
    turn = (LANES - shift) % LANES
    first = pltpu.roll(ext_ref[channel, block, pl.ds(row, length), :], turn, 1)
    second = pltpu.roll(ext_ref[channel, block + 1, pl.ds(row, length), :], turn, 1)
    return jnp.where(lane_index(length) < LANES - shift, first, second)


def add_patch(acc_ref, row, col, values, length):
    block = col // LANES
    shift = col % LANES
    turned = pltpu.roll(values, shift, 1)
    late = lane_index(length) >= shift
    window = pl.ds(row, length)
    acc_ref[block, window, :] += jnp.where(late, turned, 0.0)
    acc_ref[block + 1, window, :] += jnp.where(late, 0.0, turned)


def add_light(light_ref, power_ref, row, col, weight, length):
    row, col = row + length, col + length
    inside = (row > 0) & (row < light_ref.shape[1] - length) & (col > 0) & (col < (light_ref.shape[0] - 1) * LANES)

    @pl.when(inside & (weight > 0.0))
    def _():
        add_patch(light_ref, row, col, power_ref[...], length)


def all_light(light_ref, power_ref, info_ref, tall, wide, slots, length):
    across = 1 - 2 * parity("col")
    down = 1 - 2 * parity("row")
    places = [(0, 0), (0, across), (0, -across)]
    places += [(down, step) for step in (-1, 0, 1)] + [(-down, step) for step in (-1, 0, 1)]
    for index, (row_step, col_step) in enumerate(places):
        for s in range(slots):
            row, col, weight = slot_place(info_ref, index, s, slots)
            add_light(light_ref, power_ref, row + row_step * tall, col + col_step * wide, weight, length)


def fill_info(rows_ref, cols_ref, counts_ref, slots):
    lanes = lax.broadcasted_iota(jnp.int32, (INFO, LANES), 1)
    info = jnp.zeros((INFO, LANES), jnp.float32)
    count = counts_ref[0, 0]
    upper = lax.axis_index("row") < lax.axis_size("row") // 2
    for s in range(slots):
        inside = jnp.where(upper, s < count, s >= slots - count)
        weight = jnp.where(inside, 1.0, 0.0).astype(jnp.float32)
        info = jnp.where(lanes == s, rows_ref[0, 0, s].astype(jnp.float32), info)
        info = jnp.where(lanes == slots + s, cols_ref[0, 0, s].astype(jnp.float32), info)
        info = jnp.where(lanes == 2 * slots + s, weight, info)
    return info


def position_terms(patches, probe_real, probe_imag, measured_ref, tables_ref, weights, slots, length):
    forward_high, forward_low = tables_ref[0], tables_ref[1]
    backward_high, backward_low = tables_ref[2], tables_ref[3]
    exits = []
    for patch_real, patch_imag in patches:
        exits.append(
            jnp.concatenate(
                [
                    probe_real * patch_real - probe_imag * patch_imag,
                    probe_real * patch_imag + probe_imag * patch_real,
                ],
                axis=1,
            )
        )
    mid = right_table(jnp.concatenate(exits, axis=0), forward_high, forward_low)
    mid = jnp.concatenate(
        [
            jnp.concatenate(
                [
                    mid[s * length : (s + 1) * length, :length],
                    mid[s * length : (s + 1) * length, length:],
                ],
                axis=0,
            )
            for s in range(slots)
        ],
        axis=1,
    )
    freq = left_table(backward_high, backward_low, mid)
    scaled = []
    for s in range(slots):
        freq_real = freq[:length, s * length : (s + 1) * length]
        freq_imag = freq[length:, s * length : (s + 1) * length]
        measured = measured_ref[s].astype(jnp.float32)
        residual = freq_real * freq_real + freq_imag * freq_imag - COUNT_SCALE * measured
        scaled.append(jnp.concatenate([residual * freq_real, residual * freq_imag], axis=0))
    mid = left_table(forward_high, forward_low, jnp.concatenate(scaled, axis=1))
    mid = jnp.concatenate(
        [
            jnp.concatenate(
                [
                    mid[:length, s * length : (s + 1) * length],
                    mid[length:, s * length : (s + 1) * length],
                ],
                axis=1,
            )
            for s in range(slots)
        ],
        axis=0,
    )
    back = right_table(mid, backward_high, backward_low)
    updates = []
    for s in range(slots):
        rows = slice(s * length, (s + 1) * length)
        updates.append((back[rows, :length] * weights[s], back[rows, length:] * weights[s]))
    return updates


def finish_terms(patches, updates, probe_real, probe_imag, places, keep_ref, send_ref, dep_ref, sum_ref, length):
    slots = len(patches)
    grad_real = jnp.zeros((length, length), jnp.float32)
    grad_imag = grad_real
    light = grad_real
    for s in range(slots):
        (patch_real, patch_imag), (back_real, back_imag) = patches[s], updates[s]
        grad_real += patch_real * back_real + patch_imag * back_imag
        grad_imag += patch_real * back_imag - patch_imag * back_real
        light += places[s][2] * (patch_real * patch_real + patch_imag * patch_imag)
    sum_ref[0] = grad_real
    sum_ref[1] = grad_imag
    sum_ref[2] = light
    half = length // 2
    side = parity("row")
    keep_ref[...] = sum_ref[:, pl.ds(pl.multiple_of(side * half, half), half), :]
    send_ref[...] = sum_ref[:, pl.ds(pl.multiple_of((1 - side) * half, half), half), :]
    dep_ref[...] = jnp.zeros_like(dep_ref)
    high = dep_ref.shape[1] // 2
    for s in range(slots):
        back_real, back_imag = updates[s]
        row, col, _ = places[s]
        add_patch(dep_ref, row, col, probe_real * back_real + probe_imag * back_imag, length)
        add_patch(dep_ref, row + high, col, probe_real * back_imag - probe_imag * back_real, length)


def start_all(pairs, sems):
    copies = [pltpu.make_async_copy(source, target, sems.at[i]) for i, (source, target) in enumerate(pairs)]
    for copy in copies:
        copy.start()
    return copies


def wait_all(copies):
    for copy in copies:
        copy.wait()


def halo_kernel(field_ref, ext_ref, right_out, below_out, corner_out, sems):
    length = corner_out.shape[1]
    blocks = ext_ref.shape[1] - 1
    tall = field_ref.shape[1]
    pairs = [
        (field_ref.at[:, :, pl.ds(0, length)], right_out),
        (field_ref.at[:, pl.ds(0, length), :], below_out),
        (field_ref.at[:, pl.ds(0, length), pl.ds(0, length)], corner_out),
    ]
    for block in range(blocks):
        for channel in range(2):
            pairs.append(
                (
                    field_ref.at[channel, :, pl.ds(block * LANES, LANES)],
                    ext_ref.at[channel, block, pl.ds(0, tall), :],
                )
            )
    wait_all(start_all(pairs, sems))


def load_kernel(
    probe_ref, measured_ref, tables_ref, rows_ref, cols_ref, counts_ref,
    probe_out, half_out, measured_out, tables_out, info_out, rows_at, cols_at, counts_at, sems,
):
    half = half_out.shape[1]
    start = pl.multiple_of(parity("row") * half, half)
    pairs = [
        (rows_ref, rows_at),
        (cols_ref, cols_at),
        (counts_ref, counts_at),
        (probe_ref, probe_out),
        (probe_ref.at[:, pl.ds(start, half), :], half_out),
        (measured_ref, measured_out),
        (tables_ref, tables_out),
    ]
    copies = start_all(pairs, sems)
    wait_all(copies[:3])
    info_out[...] = fill_info(rows_at, cols_at, counts_at, rows_at.shape[2])
    wait_all(copies[3:])


def split_sides(inner_out, outer_out, dep_ref):
    size = dep_ref.shape[1]
    side = parity("col")
    inner_out[:size] = dep_ref[2 - 2 * side]
    outer_out[:size] = dep_ref[2 * side]


def first_kernel(
    start_ref, right_ref, below_ref, corner_ref, probe_ref, measured_ref, tables_ref, info_ref,
    ext_ref, keep_ref, send_ref, inner_out, middle_out, outer_out, dep_ref, sum_ref, info_at, sems,
):
    copies = start_all([(info_ref, info_at.at[0])], sems)
    length = probe_ref.shape[1]
    slots = measured_ref.shape[0]
    tall = right_ref.shape[1]
    blocks = below_ref.shape[2] // LANES
    for channel in range(2):
        for block in range(blocks):
            lanes = slice(block * LANES, (block + 1) * LANES)
            ext_ref[channel, block, tall:, :] = below_ref[channel, :, lanes]
        ext_ref[channel, blocks, :tall, :] = right_ref[channel]
        ext_ref[channel, blocks, tall:, :] = corner_ref[channel]
    probe_real, probe_imag = probe_ref[0], probe_ref[1]
    wait_all(copies)
    places = [slot_place(info_at, 0, s, slots) for s in range(slots)]
    patches = [
        [take_patch(ext_ref, channel, places[s][0], places[s][1], length) for channel in range(2)] for s in range(slots)
    ]
    weights = [place[2] for place in places]
    updates = position_terms(
        patches, probe_real, probe_imag, measured_ref, tables_ref, weights, slots, length
    )
    finish_terms(patches, updates, probe_real, probe_imag, places, keep_ref, send_ref, dep_ref, sum_ref, length)
    size = dep_ref.shape[1]
    middle_out[...] = dep_ref[1]
    split_sides(inner_out, outer_out, dep_ref)
    inner_out[size:] = info_ref[...]
    outer_out[size:] = info_ref[...]


def strips_kernel(
    inner_ref, middle_ref, outer_ref, from_inner, from_outer, total_out, inner_out, outer_out, infos_out
):
    size = middle_ref.shape[0]
    high = size // 2
    length = (inner_out.shape[0] - 3 * INFO) // 6
    tall = high - length
    side = parity("col")
    total_out[2 - 2 * side] = inner_ref[:size] + from_inner[:size]
    total_out[1] = middle_ref[...]
    total_out[2 * side] = outer_ref[:size] + from_outer[:size]
    side_row = parity("row")
    for block in range(3):
        for channel in range(2):
            rows = slice((2 * block + channel) * length, (2 * block + channel + 1) * length)
            start = channel * high + tall - side_row * tall
            inner_out[rows] = total_out[block, pl.ds(pl.multiple_of(start, 8), length), :]
            start = channel * high + side_row * tall
            outer_out[rows] = total_out[block, pl.ds(pl.multiple_of(start, 8), length), :]
    own, inner, outer = inner_ref[size:], from_inner[size:], from_outer[size:]
    infos_out[0], infos_out[1], infos_out[2] = own, inner, outer
    left = jnp.where(side == 0, outer, inner)
    right = jnp.where(side == 0, inner, outer)
    for index, info in enumerate((left, own, right)):
        rows = slice(6 * length + index * INFO, 6 * length + (index + 1) * INFO)
        inner_out[rows] = info
        outer_out[rows] = info


def object_kernel(
    ext_ref, probe_ref, total_ref, infos_ref, from_inner, from_outer,
    tile_out, patches_out, info_out, new_ref, light_ref, power_ref, info_at, sems,
):
    length = patches_out.shape[2]
    slots = patches_out.shape[0]
    high = ext_ref.shape[2]
    tall = high - length
    blocks = tile_out.shape[1]
    edge = 6 * length
    info_out[0:3] = infos_ref[...]
    for index in range(3):
        info_out[3 + index] = from_inner[edge + index * INFO : edge + (index + 1) * INFO]
        info_out[6 + index] = from_outer[edge + index * INFO : edge + (index + 1) * INFO]
    copies = start_all([(info_out, info_at)], sems)
    power_ref[...] = probe_ref[0] * probe_ref[0] + probe_ref[1] * probe_ref[1]
    light_ref[...] = jnp.zeros_like(light_ref)
    wait_all(copies)
    all_light(light_ref, power_ref, info_at, tall, blocks * LANES, slots, length)
    inside_row = jnp.where(lax.axis_index("row") < lax.axis_size("row") - 1, 1.0, 0.0).astype(jnp.float32)
    inside_col = jnp.where(lax.axis_index("col") < lax.axis_size("col") - 1, 1.0, 0.0).astype(jnp.float32)
    even = parity("row") == 0
    for block in range(blocks + 1):
        for piece, start, stop in ((0, 0, length), (1, length, tall), (2, tall, high)):
            light = light_ref[block + 1, start + length : stop + length, :]
            scale = STEP_SIZE / (light + REGULARIZER)
            if piece == 2:
                scale = scale * inside_row
            if block == blocks:
                scale = scale * inside_col
            for channel in range(2):
                total = total_ref[block, channel * high + start : channel * high + stop]
                rows = slice((2 * block + channel) * length, (2 * block + channel + 1) * length)
                if piece == 0:
                    total = total + jnp.where(even, from_outer[rows], from_inner[rows])
                if piece == 2:
                    total = total + jnp.where(even, from_inner[rows], from_outer[rows])
                new_ref[channel, block, start:stop, :] = ext_ref[channel, block, start:stop, :] - scale * total
    for channel in range(2):
        tile_out[channel] = new_ref[channel, :blocks, :tall, :]
    for s in range(slots):
        row, col, _ = slot_place(info_at, 0, s, slots)
        for channel in range(2):
            patches_out[s, channel] = take_patch(new_ref, channel, row, col, length)


def assemble_probe(half_ref, other_ref, side):
    first = side == 0
    return [
        jnp.concatenate(
            [
                jnp.where(first, half_ref[channel], other_ref[channel]),
                jnp.where(first, other_ref[channel], half_ref[channel]),
            ],
            axis=0,
        )
        for channel in range(2)
    ]


def second_kernel(
    patches_ref, half_ref, other_ref, measured_ref, tables_ref, info_ref,
    keep_ref, send_ref, left_out, middle_out, right_out, dep_ref, sum_ref, info_at, sems,
):
    copies = start_all([(info_ref, info_at.at[0])], sems)
    slots = measured_ref.shape[0]
    length = measured_ref.shape[1]
    probe_real, probe_imag = assemble_probe(half_ref, other_ref, parity("row"))
    patches = [[patches_ref[s, channel] for channel in range(2)] for s in range(slots)]
    wait_all(copies)
    places = [slot_place(info_at, 0, s, slots) for s in range(slots)]
    weights = [place[2] for place in places]
    updates = position_terms(
        patches, probe_real, probe_imag, measured_ref, tables_ref, weights, slots, length
    )
    finish_terms(patches, updates, probe_real, probe_imag, places, keep_ref, send_ref, dep_ref, sum_ref, length)
    left_out[...] = dep_ref[0]
    middle_out[...] = dep_ref[1]
    right_out[...] = dep_ref[2]


def light_kernel(slots, infos_ref, half_ref, other_ref, light_out, light_ref, power_ref, info_at, sems):
    copies = start_all([(infos_ref, info_at)], sems)
    length = power_ref.shape[0]
    tall = light_out.shape[1]
    blocks = light_out.shape[0]
    probe_real, probe_imag = assemble_probe(half_ref, other_ref, parity("row"))
    power_ref[...] = probe_real * probe_real + probe_imag * probe_imag
    light_ref[...] = jnp.zeros_like(light_ref)
    wait_all(copies)
    all_light(light_ref, power_ref, info_at, tall, blocks * LANES, slots, length)
    light_out[...] = STEP_SIZE / (light_ref[1 : 1 + blocks, length : length + tall, :] + REGULARIZER)


def push_kernel(left_ref, middle_ref, from_left, left_out, bottom_out):
    size = middle_ref.shape[0]
    high = size // 2
    length = bottom_out.shape[1] // 2
    tall = high - length
    left_out[...] = left_ref[...] + from_left[...]
    for block, part in enumerate((left_out, middle_ref)):
        for channel in range(2):
            bottom_out[block, channel * length : (channel + 1) * length] = part[
                channel * high + tall : (channel + 1) * high
            ]


def final_kernel(tile_ref, light_ref, left_ref, middle_ref, from_above, half_ref, other_ref, object_out, probe_out):
    tall = tile_ref.shape[2]
    length = from_above.shape[1] // 2
    high = tall + length
    for block, part in enumerate((left_ref, middle_ref)):
        lanes = slice(block * LANES, (block + 1) * LANES)
        for channel in range(2):
            for start, stop in ((0, length), (length, tall)):
                total = part[channel * high + start : channel * high + stop]
                if start == 0:
                    total = total + from_above[block, channel * length : (channel + 1) * length]
                object_out[channel, start:stop, lanes] = (
                    tile_ref[channel, block, start:stop, :] - light_ref[block, start:stop, :] * total
                )
    probe_out[0], probe_out[1] = assemble_probe(half_ref, other_ref, parity("row"))


def shift(value, axis, steps):
    count = lax.axis_size(axis)
    pairs = [(source, source + steps) for source in range(count) if 0 <= source + steps < count]
    return lax.ppermute(value, axis, pairs)


def swap(value, axis, first):
    count = lax.axis_size(axis)
    pairs = []
    for low in range(first, count - 1, 2):
        pairs += [(low, low + 1), (low + 1, low)]
    return lax.ppermute(value, axis, pairs)


def flip(value, axis, mask):
    count = lax.axis_size(axis)
    return lax.ppermute(value, axis, [(source, source ^ mask) for source in range(count)])


def tie(*values):
    return lax.optimization_barrier(values)


def butterfly(total, axis, first, stop=None):
    bit = first
    while bit < (stop or lax.axis_size(axis)):
        total = total + flip(total, axis, bit)
        bit *= 2
    return total


def quad(total, axis, first):
    bit = first
    while 2 * bit < lax.axis_size(axis):
        one, two, three = (flip(total, axis, bit * mask) for mask in (1, 2, 3))
        total = (total + one) + (two + three)
        bit *= 4
    return butterfly(total, axis, bit)


def stepped(half, total):
    return half - PROBE_STEP * total[:2] / (total[2] + REGULARIZER)


def shape_of(spec):
    return spec if isinstance(spec, jax.ShapeDtypeStruct) else jax.ShapeDtypeStruct(spec, jnp.float32)


def call(kernel, outs, scratch, args, aliases={}, space=pltpu.VMEM):
    vmem = pl.BlockSpec(memory_space=pltpu.VMEM)
    return pl.pallas_call(
        kernel,
        out_shape=[shape_of(spec) for spec in outs],
        in_specs=[pl.BlockSpec(memory_space=space)] * len(args),
        out_specs=[vmem] * len(outs),
        scratch_shapes=[pltpu.VMEM(shape, jnp.float32) if isinstance(shape, tuple) else shape for shape in scratch],
        compiler_params=pltpu.CompilerParams(vmem_limit_bytes=VMEM_BYTES),
        input_output_aliases=aliases,
    )(*args)


def local(object_field, probe_field, intensities, off_rows, off_cols, counts):
    tall, wide = object_field.shape[1:]
    length = probe_field.shape[1]
    slots = off_rows.shape[2]
    half = length // 2
    high = tall + length
    blocks = wide // LANES
    tables = jnp.asarray(dft_parts(length))
    measured = intensities.reshape(slots, length, length)
    count_rows, count_cols = lax.axis_size("row"), lax.axis_size("col")

    def info_space(tiles):
        return [pltpu.SMEM((tiles, INFO, LANES), jnp.float32), pltpu.SemaphoreType.DMA((1,))]

    extended = (2, blocks + 1, high, LANES)
    ext, right, below, corner = call(
        halo_kernel,
        [extended, (2, tall, length), (2, length, wide), (2, length, length)],
        [pltpu.SemaphoreType.DMA((3 + 2 * blocks,))],
        [object_field],
        space=pl.ANY,
    )
    probe_now, own, measured, tables, info = call(
        load_kernel,
        [
            (2, length, length),
            (2, half, length),
            jax.ShapeDtypeStruct(measured.shape, measured.dtype),
            jax.ShapeDtypeStruct(tables.shape, tables.dtype),
            (INFO, LANES),
        ],
        [
            pltpu.SMEM(off_rows.shape, jnp.int32),
            pltpu.SMEM(off_cols.shape, jnp.int32),
            pltpu.SMEM(counts.shape, jnp.int32),
            pltpu.SemaphoreType.DMA((7,)),
        ],
        [probe_field, measured, tables, off_rows, off_cols, counts],
        space=pl.ANY,
    )
    right = shift(right, "col", -1)
    corner = lax.ppermute(
        corner,
        ("row", "col"),
        [
            ((r + 1) * count_cols + c + 1, r * count_cols + c)
            for r in range(count_rows - 1)
            for c in range(count_cols - 1)
        ],
    )
    below = shift(below, "row", -1)
    size = 2 * high
    strip = (size + INFO, LANES)
    partial = (3, half, length)
    deposits = [(blocks + 1, size, LANES), (3, length, length)] + info_space(1)
    ext, keep, send, inner, middle, outer = call(
        first_kernel,
        [extended, partial, partial, strip, (size, LANES), strip],
        deposits,
        [ext, right, below, corner, probe_now, measured, tables, info],
        aliases={0: 0},
    )
    last_row, last_col = count_rows // 2, count_cols // 2
    edge = (2 * (blocks + 1) * length + 3 * INFO, LANES)
    padded = (blocks + 3, high + 2 * length, LANES)

    from_inner = swap(inner, "col", 0)
    from_outer = swap(outer, "col", 1)
    total, inner, outer, infos = call(
        strips_kernel,
        [(blocks + 1, size, LANES), edge, edge, (3, INFO, LANES)],
        [],
        [inner, middle, outer, from_inner, from_outer],
    )
    part = keep + flip(send, "row", 1)
    part = quad(part, "row", 2)
    part, inner, outer = tie(part, inner, outer)
    from_inner = swap(inner, "row", 0)
    from_outer = swap(outer, "row", 1)
    part = butterfly(part, "col", 1, last_col)
    part, from_inner = tie(part, from_inner)
    part = butterfly(part, "col", last_col)
    new_half = stepped(own, part)
    tile, patches, infos = call(
        object_kernel,
        [(2, blocks, tall, LANES), (slots, 2, length, length), (9, INFO, LANES)],
        [extended, padded, (length, length)] + info_space(9),
        [ext, probe_now, total, infos, from_inner, from_outer],
    )
    new_half, patches = tie(new_half, patches)
    new_other = flip(new_half, "row", 1)

    keep, send, left, middle, right = call(
        second_kernel,
        [partial, partial, (size, LANES), (size, LANES), (size, LANES)],
        deposits,
        [patches, new_half, new_other, measured, tables, info],
    )
    padded = (blocks + 2, tall + 2 * length, LANES)
    (light,) = call(
        functools.partial(light_kernel, slots),
        [(blocks, tall, LANES)],
        [padded, (length, length)] + info_space(9),
        [infos, new_half, new_other],
    )
    from_left = shift(right, "col", 1)
    part = keep + flip(send, "row", 1)
    part = butterfly(part, "row", 2, last_row)
    part = butterfly(part, "row", last_row)
    part, light = tie(part, light)
    left, bottom = call(
        push_kernel, [(size, LANES), (blocks, 2 * length, LANES)], [], [left, middle, from_left]
    )
    from_above = shift(bottom, "row", 1)
    part = butterfly(part, "col", 1, last_col)
    part = butterfly(part, "col", last_col)
    last_half = stepped(new_half, part)
    last_other = flip(last_half, "row", 1)
    return call(
        final_kernel,
        [(2, tall, wide), (2, length, length)],
        [],
        [tile, light, left, middle, from_above, last_half, last_other],
    )


def solution(mesh):
    placed = (
        P(None, "row", "col"),
        P(),
        P("row", "col", None, None, None),
        P("row", "col", None),
        P("row", "col", None),
        P("row", "col"),
    )
    return jax.shard_map(
        local, mesh=mesh, in_specs=placed, out_specs=(P(None, "row", "col"), P()), check_vma=False
    )
```

```python
import functools
import math

import jax
import jax.numpy as jnp
import numpy as np
from jax import lax
from jax.experimental import pallas as pl
from jax.experimental.pallas import tpu as pltpu
from jax.sharding import PartitionSpec as P

STEP_SIZE = 0.25
PROBE_STEP = 1.0
REGULARIZER = 1.0
COUNT_SCALE = 1.0 / 1024.0
LANES = 128
INFO = 8
VMEM_BYTES = 12 * 1024 * 1024


def dft_parts(length):
    points = np.arange(length)
    angles = (points[:, None] * points[None, :] % length) * (2.0 * math.pi / length)
    cosine = np.cos(angles) / math.sqrt(length)
    sine = np.sin(angles) / math.sqrt(length)
    forward = np.block([[cosine, -sine], [sine, cosine]]).astype(np.float32)
    parts = []
    for table in (forward, forward.T):
        high = table.astype(jnp.bfloat16)
        low = (table - high.astype(np.float32)).astype(jnp.bfloat16)
        parts += [high, low]
    return np.stack(parts)


def split(values):
    high = values.astype(jnp.bfloat16)
    low = (values - high.astype(jnp.float32)).astype(jnp.bfloat16)
    return high, low


def dot(left, right):
    return jnp.dot(left, right, preferred_element_type=jnp.float32)


def right_table(values, table_high, table_low):
    high, low = split(values)
    return dot(high, table_high) + (dot(high, table_low) + dot(low, table_high))


def left_table(table_high, table_low, values):
    high, low = split(values)
    return dot(table_high, high) + (dot(table_low, high) + dot(table_high, low))


def parity(axis):
    return lax.axis_index(axis) % 2


def slot_place(info_ref, index, slot, slots):
    row = info_ref[index, 0, slot].astype(jnp.int32)
    col = info_ref[index, 0, slots + slot].astype(jnp.int32)
    return row, col, info_ref[index, 0, 2 * slots + slot]


def lane_index(length):
    return lax.broadcasted_iota(jnp.int32, (length, LANES), 1)


def take_patch(ext_ref, channel, row, col, length):
    block = col // LANES
    shift = col % LANES
    turn = (LANES - shift) % LANES
    first = pltpu.roll(ext_ref[channel, block, pl.ds(row, length), :], turn, 1)
    second = pltpu.roll(ext_ref[channel, block + 1, pl.ds(row, length), :], turn, 1)
    return jnp.where(lane_index(length) < LANES - shift, first, second)


def add_patch(acc_ref, row, col, values, length):
    block = col // LANES
    shift = col % LANES
    turned = pltpu.roll(values, shift, 1)
    late = lane_index(length) >= shift
    window = pl.ds(row, length)
    acc_ref[block, window, :] += jnp.where(late, turned, 0.0)
    acc_ref[block + 1, window, :] += jnp.where(late, 0.0, turned)


def add_light(light_ref, power_ref, row, col, weight, length):
    row, col = row + length, col + length
    inside = (row > 0) & (row < light_ref.shape[1] - length) & (col > 0) & (col < (light_ref.shape[0] - 1) * LANES)

    @pl.when(inside & (weight > 0.0))
    def _():
        add_patch(light_ref, row, col, power_ref[...], length)


def add_tiles(light_ref, power_ref, info_ref, tiles, tall, wide, slots, length):
    across = 1 - 2 * parity("col")
    down = 1 - 2 * parity("row")
    places = [(0, 0), (0, across), (0, -across)]
    places += [(down, step) for step in (-1, 0, 1)] + [(-down, step) for step in (-1, 0, 1)]
    for index in tiles:
        row_step, col_step = places[index]
        for s in range(slots):
            row, col, weight = slot_place(info_ref, index, s, slots)
            add_light(light_ref, power_ref, row + row_step * tall, col + col_step * wide, weight, length)


def fill_info(rows_ref, cols_ref, counts_ref, slots):
    lanes = lax.broadcasted_iota(jnp.int32, (INFO, LANES), 1)
    info = jnp.zeros((INFO, LANES), jnp.float32)
    count = counts_ref[0, 0]
    upper = lax.axis_index("row") < lax.axis_size("row") // 2
    for s in range(slots):
        inside = jnp.where(upper, s < count, s >= slots - count)
        weight = jnp.where(inside, 1.0, 0.0).astype(jnp.float32)
        info = jnp.where(lanes == s, rows_ref[0, 0, s].astype(jnp.float32), info)
        info = jnp.where(lanes == slots + s, cols_ref[0, 0, s].astype(jnp.float32), info)
        info = jnp.where(lanes == 2 * slots + s, weight, info)
    return info


def position_terms(patches, probe_real, probe_imag, measured_ref, tables_ref, weights, slots, length):
    forward_high, forward_low = tables_ref[0], tables_ref[1]
    backward_high, backward_low = tables_ref[2], tables_ref[3]
    exits = []
    for patch_real, patch_imag in patches:
        exits.append(
            jnp.concatenate(
                [
                    probe_real * patch_real - probe_imag * patch_imag,
                    probe_real * patch_imag + probe_imag * patch_real,
                ],
                axis=1,
            )
        )
    mid = right_table(jnp.concatenate(exits, axis=0), forward_high, forward_low)
    mid = jnp.concatenate(
        [
            jnp.concatenate(
                [
                    mid[s * length : (s + 1) * length, :length],
                    mid[s * length : (s + 1) * length, length:],
                ],
                axis=0,
            )
            for s in range(slots)
        ],
        axis=1,
    )
    freq = left_table(backward_high, backward_low, mid)
    scaled = []
    for s in range(slots):
        freq_real = freq[:length, s * length : (s + 1) * length]
        freq_imag = freq[length:, s * length : (s + 1) * length]
        measured = measured_ref[s].astype(jnp.float32)
        residual = freq_real * freq_real + freq_imag * freq_imag - COUNT_SCALE * measured
        scaled.append(jnp.concatenate([residual * freq_real, residual * freq_imag], axis=0))
    mid = left_table(forward_high, forward_low, jnp.concatenate(scaled, axis=1))
    mid = jnp.concatenate(
        [
            jnp.concatenate(
                [
                    mid[:length, s * length : (s + 1) * length],
                    mid[length:, s * length : (s + 1) * length],
                ],
                axis=1,
            )
            for s in range(slots)
        ],
        axis=0,
    )
    back = right_table(mid, backward_high, backward_low)
    updates = []
    for s in range(slots):
        rows = slice(s * length, (s + 1) * length)
        updates.append((back[rows, :length] * weights[s], back[rows, length:] * weights[s]))
    return updates


def finish_terms(patches, updates, probe_real, probe_imag, places, keep_ref, send_ref, dep_ref, sum_ref, length):
    slots = len(patches)
    grad_real = jnp.zeros((length, length), jnp.float32)
    grad_imag = grad_real
    light = grad_real
    for s in range(slots):
        (patch_real, patch_imag), (back_real, back_imag) = patches[s], updates[s]
        grad_real += patch_real * back_real + patch_imag * back_imag
        grad_imag += patch_real * back_imag - patch_imag * back_real
        light += places[s][2] * (patch_real * patch_real + patch_imag * patch_imag)
    sum_ref[0] = grad_real
    sum_ref[1] = grad_imag
    sum_ref[2] = light
    half = length // 2
    side = parity("row")
    keep_ref[...] = sum_ref[:, pl.ds(pl.multiple_of(side * half, half), half), :]
    send_ref[...] = sum_ref[:, pl.ds(pl.multiple_of((1 - side) * half, half), half), :]
    dep_ref[...] = jnp.zeros_like(dep_ref)
    high = dep_ref.shape[1] // 2
    for s in range(slots):
        back_real, back_imag = updates[s]
        row, col, _ = places[s]
        add_patch(dep_ref, row, col, probe_real * back_real + probe_imag * back_imag, length)
        add_patch(dep_ref, row + high, col, probe_real * back_imag - probe_imag * back_real, length)


def start_all(pairs, sems):
    copies = [pltpu.make_async_copy(source, target, sems.at[i]) for i, (source, target) in enumerate(pairs)]
    for copy in copies:
        copy.start()
    return copies


def wait_all(copies):
    for copy in copies:
        copy.wait()


def halo_kernel(field_ref, ext_ref, right_out, below_out, corner_out, sems):
    length = corner_out.shape[1]
    blocks = ext_ref.shape[1] - 1
    tall = field_ref.shape[1]
    pairs = [
        (field_ref.at[:, :, pl.ds(0, length)], right_out),
        (field_ref.at[:, pl.ds(0, length), :], below_out),
        (field_ref.at[:, pl.ds(0, length), pl.ds(0, length)], corner_out),
    ]
    for block in range(blocks):
        for channel in range(2):
            pairs.append(
                (
                    field_ref.at[channel, :, pl.ds(block * LANES, LANES)],
                    ext_ref.at[channel, block, pl.ds(0, tall), :],
                )
            )
    wait_all(start_all(pairs, sems))


def load_kernel(
    probe_ref, measured_ref, tables_ref, rows_ref, cols_ref, counts_ref,
    probe_out, half_out, measured_out, tables_out, info_out, rows_at, cols_at, counts_at, sems,
):
    half = half_out.shape[1]
    start = pl.multiple_of(parity("row") * half, half)
    pairs = [
        (rows_ref, rows_at),
        (cols_ref, cols_at),
        (counts_ref, counts_at),
        (probe_ref, probe_out),
        (probe_ref.at[:, pl.ds(start, half), :], half_out),
        (measured_ref, measured_out),
        (tables_ref, tables_out),
    ]
    copies = start_all(pairs, sems)
    wait_all(copies[:3])
    info_out[...] = fill_info(rows_at, cols_at, counts_at, rows_at.shape[2])
    wait_all(copies[3:])


def split_sides(inner_out, outer_out, dep_ref):
    size = dep_ref.shape[1]
    side = parity("col")
    inner_out[:size] = dep_ref[2 - 2 * side]
    outer_out[:size] = dep_ref[2 * side]


def first_kernel(
    start_ref, right_ref, below_ref, corner_ref, probe_ref, measured_ref, tables_ref, info_ref,
    ext_ref, keep_ref, send_ref, inner_out, middle_out, outer_out, dep_ref, sum_ref, info_at, sems,
):
    copies = start_all([(info_ref, info_at.at[0])], sems)
    length = probe_ref.shape[1]
    slots = measured_ref.shape[0]
    tall = right_ref.shape[1]
    blocks = below_ref.shape[2] // LANES
    for channel in range(2):
        for block in range(blocks):
            lanes = slice(block * LANES, (block + 1) * LANES)
            ext_ref[channel, block, tall:, :] = below_ref[channel, :, lanes]
        ext_ref[channel, blocks, :tall, :] = right_ref[channel]
        ext_ref[channel, blocks, tall:, :] = corner_ref[channel]
    probe_real, probe_imag = probe_ref[0], probe_ref[1]
    wait_all(copies)
    places = [slot_place(info_at, 0, s, slots) for s in range(slots)]
    patches = [
        [take_patch(ext_ref, channel, places[s][0], places[s][1], length) for channel in range(2)] for s in range(slots)
    ]
    weights = [place[2] for place in places]
    updates = position_terms(
        patches, probe_real, probe_imag, measured_ref, tables_ref, weights, slots, length
    )
    finish_terms(patches, updates, probe_real, probe_imag, places, keep_ref, send_ref, dep_ref, sum_ref, length)
    size = dep_ref.shape[1]
    middle_out[...] = dep_ref[1]
    split_sides(inner_out, outer_out, dep_ref)
    inner_out[size:] = info_ref[...]
    outer_out[size:] = info_ref[...]


def strips_kernel(
    inner_ref, middle_ref, outer_ref, from_inner, from_outer, total_out, inner_out, outer_out, infos_out
):
    size = middle_ref.shape[0]
    high = size // 2
    length = (inner_out.shape[0] - 3 * INFO) // 6
    tall = high - length
    side = parity("col")
    total_out[2 - 2 * side] = inner_ref[:size] + from_inner[:size]
    total_out[1] = middle_ref[...]
    total_out[2 * side] = outer_ref[:size] + from_outer[:size]
    side_row = parity("row")
    for block in range(3):
        for channel in range(2):
            rows = slice((2 * block + channel) * length, (2 * block + channel + 1) * length)
            start = channel * high + tall - side_row * tall
            inner_out[rows] = total_out[block, pl.ds(pl.multiple_of(start, 8), length), :]
            start = channel * high + side_row * tall
            outer_out[rows] = total_out[block, pl.ds(pl.multiple_of(start, 8), length), :]
    own, inner, outer = inner_ref[size:], from_inner[size:], from_outer[size:]
    infos_out[0], infos_out[1], infos_out[2] = own, inner, outer
    left = jnp.where(side == 0, outer, inner)
    right = jnp.where(side == 0, inner, outer)
    for index, info in enumerate((left, own, right)):
        rows = slice(6 * length + index * INFO, 6 * length + (index + 1) * INFO)
        inner_out[rows] = info
        outer_out[rows] = info


def update_rows(new_ref, ext_ref, light_ref, total_ref, extra, block, start, stop, length, inside):
    high = ext_ref.shape[2]
    scale = STEP_SIZE / (light_ref[block + 1, start + length : stop + length, :] + REGULARIZER)
    if inside is not None:
        scale = scale * inside
    for channel in range(2):
        total = total_ref[block, channel * high + start : channel * high + stop]
        if extra is not None:
            total = total + extra(2 * block + channel)
        new_ref[channel, block, start:stop, :] = ext_ref[channel, block, start:stop, :] - scale * total


def inside_mesh(axis):
    return jnp.where(lax.axis_index(axis) < lax.axis_size(axis) - 1, 1.0, 0.0).astype(jnp.float32)


def near_light_kernel(
    slots, tall, ext_ref, infos_ref, probe_ref, total_ref, new_ref, light_out, power_ref, info_at, sems
):
    copies = start_all([(infos_ref, info_at)], sems)
    length = power_ref.shape[0]
    power_ref[...] = probe_ref[0] * probe_ref[0] + probe_ref[1] * probe_ref[1]
    light_out[...] = jnp.zeros_like(light_out)
    wait_all(copies)
    wide = (light_out.shape[0] - 3) * LANES
    add_tiles(light_out, power_ref, info_at, range(3), tall, wide, slots, length)
    blocks = ext_ref.shape[1] - 1
    for block in range(blocks + 1):
        inside = inside_mesh("col") if block == blocks else None
        update_rows(new_ref, ext_ref, light_out, total_ref, None, block, length, tall, length, inside)


def object_kernel(
    slots, ext_ref, light_in, probe_ref, total_ref, infos_ref, from_inner, from_outer,
    new_ref, light_ref, info_out, power_ref, info_at, sems,
):
    length = power_ref.shape[0]
    high = ext_ref.shape[2]
    tall = high - length
    blocks = ext_ref.shape[1] - 1
    edge = 6 * length
    info_out[0:3] = infos_ref[...]
    for index in range(3):
        info_out[3 + index] = from_inner[edge + index * INFO : edge + (index + 1) * INFO]
        info_out[6 + index] = from_outer[edge + index * INFO : edge + (index + 1) * INFO]
    copies = start_all([(info_out, info_at)], sems)
    power_ref[...] = probe_ref[0] * probe_ref[0] + probe_ref[1] * probe_ref[1]
    wait_all(copies)
    add_tiles(light_ref, power_ref, info_at, range(3, 9), tall, blocks * LANES, slots, length)
    even = parity("row") == 0

    def rows_of(part, index):
        return part[index * length : (index + 1) * length]

    def from_above(index):
        return jnp.where(even, rows_of(from_outer, index), rows_of(from_inner, index))

    def from_below(index):
        return jnp.where(even, rows_of(from_inner, index), rows_of(from_outer, index))

    for block in range(blocks + 1):
        inside = inside_mesh("col") if block == blocks else None
        update_rows(new_ref, ext_ref, light_ref, total_ref, from_above, block, 0, length, length, inside)
        last = inside_mesh("row") if inside is None else inside * inside_mesh("row")
        update_rows(new_ref, ext_ref, light_ref, total_ref, from_below, block, tall, high, length, last)


def patch_kernel(ext_ref, info_ref, patches_out, info_at, sems):
    copies = start_all([(info_ref, info_at.at[0])], sems)
    slots, _, length, _ = patches_out.shape
    wait_all(copies)
    for s in range(slots):
        row, col, _ = slot_place(info_at, 0, s, slots)
        for channel in range(2):
            patches_out[s, channel] = take_patch(ext_ref, channel, row, col, length)


def assemble_probe(half_ref, other_ref, side):
    first = side == 0
    return [
        jnp.concatenate(
            [
                jnp.where(first, half_ref[channel], other_ref[channel]),
                jnp.where(first, other_ref[channel], half_ref[channel]),
            ],
            axis=0,
        )
        for channel in range(2)
    ]


def second_kernel(
    patches_ref, half_ref, other_ref, measured_ref, tables_ref, info_ref,
    keep_ref, send_ref, body_out, bottom_out, dep_ref, sum_ref, info_at, sems,
):
    copies = start_all([(info_ref, info_at.at[0])], sems)
    slots = measured_ref.shape[0]
    length = measured_ref.shape[1]
    probe_real, probe_imag = assemble_probe(half_ref, other_ref, parity("row"))
    patches = [[patches_ref[s, channel] for channel in range(2)] for s in range(slots)]
    wait_all(copies)
    places = [slot_place(info_at, 0, s, slots) for s in range(slots)]
    weights = [place[2] for place in places]
    updates = position_terms(
        patches, probe_real, probe_imag, measured_ref, tables_ref, weights, slots, length
    )
    finish_terms(patches, updates, probe_real, probe_imag, places, keep_ref, send_ref, dep_ref, sum_ref, length)
    high = dep_ref.shape[1] // 2
    tall = body_out.shape[1] // 2
    for channel in range(2):
        start = channel * high
        body_out[:, channel * tall : (channel + 1) * tall] = dep_ref[:, start : start + tall, :]
        bottom_out[:, channel * length : (channel + 1) * length] = dep_ref[:, start + tall : start + high, :]


def light_kernel(slots, infos_ref, half_ref, other_ref, light_out, light_ref, power_ref, info_at, sems):
    copies = start_all([(infos_ref, info_at)], sems)
    length = power_ref.shape[0]
    tall = light_out.shape[1]
    blocks = light_out.shape[0]
    probe_real, probe_imag = assemble_probe(half_ref, other_ref, parity("row"))
    power_ref[...] = probe_real * probe_real + probe_imag * probe_imag
    light_ref[...] = jnp.zeros_like(light_ref)
    wait_all(copies)
    add_tiles(light_ref, power_ref, info_at, range(9), tall, blocks * LANES, slots, length)
    light_out[...] = STEP_SIZE / (light_ref[1 : 1 + blocks, length : length + tall, :] + REGULARIZER)


def push_kernel(body_ref, from_above, right_out):
    tall = body_ref.shape[1] // 2
    length = from_above.shape[1] // 2
    last = body_ref.shape[0] - 1
    for channel in range(2):
        start = channel * tall
        right_out[start : start + length] = (
            body_ref[last, start : start + length] + from_above[last, channel * length : (channel + 1) * length]
        )
        right_out[start + length : start + tall] = body_ref[last, start + length : start + tall]


def final_kernel(tile_ref, light_ref, body_ref, from_above, from_left, half_ref, other_ref, object_out, probe_out):
    tall = body_ref.shape[1] // 2
    length = from_above.shape[1] // 2
    for block in range(light_ref.shape[0]):
        lanes = slice(block * LANES, (block + 1) * LANES)
        for channel in range(2):
            for start, stop in ((0, length), (length, tall)):
                rows = slice(channel * tall + start, channel * tall + stop)
                total = body_ref[block, rows]
                if start == 0:
                    total = total + from_above[block, channel * length : (channel + 1) * length]
                if block == 0:
                    total = total + from_left[rows]
                object_out[channel, start:stop, lanes] = (
                    tile_ref[channel, block, start:stop, :] - light_ref[block, start:stop, :] * total
                )
    probe_out[0], probe_out[1] = assemble_probe(half_ref, other_ref, parity("row"))


def shift(value, axis, steps):
    count = lax.axis_size(axis)
    pairs = [(source, source + steps) for source in range(count) if 0 <= source + steps < count]
    return lax.ppermute(value, axis, pairs)


def swap(value, axis, first):
    count = lax.axis_size(axis)
    pairs = []
    for low in range(first, count - 1, 2):
        pairs += [(low, low + 1), (low + 1, low)]
    return lax.ppermute(value, axis, pairs)


def flip(value, axis, mask):
    count = lax.axis_size(axis)
    return lax.ppermute(value, axis, [(source, source ^ mask) for source in range(count)])


def tie(*values):
    return lax.optimization_barrier(values)


def butterfly(total, axis, first, stop=None):
    bit = first
    while bit < (stop or lax.axis_size(axis)):
        total = total + flip(total, axis, bit)
        bit *= 2
    return total


def quad(total, axis, first):
    bit = first
    while 2 * bit < lax.axis_size(axis):
        one, two, three = (flip(total, axis, bit * mask) for mask in (1, 2, 3))
        total = (total + one) + (two + three)
        bit *= 4
    return butterfly(total, axis, bit)


def stepped(half, total):
    return half - PROBE_STEP * total[:2] / (total[2] + REGULARIZER)


def shape_of(spec):
    return spec if isinstance(spec, jax.ShapeDtypeStruct) else jax.ShapeDtypeStruct(spec, jnp.float32)


def call(kernel, outs, scratch, args, aliases={}, space=pltpu.VMEM):
    vmem = pl.BlockSpec(memory_space=pltpu.VMEM)
    return pl.pallas_call(
        kernel,
        out_shape=[shape_of(spec) for spec in outs],
        in_specs=[pl.BlockSpec(memory_space=space)] * len(args),
        out_specs=[vmem] * len(outs),
        scratch_shapes=[pltpu.VMEM(shape, jnp.float32) if isinstance(shape, tuple) else shape for shape in scratch],
        compiler_params=pltpu.CompilerParams(vmem_limit_bytes=VMEM_BYTES),
        input_output_aliases=aliases,
    )(*args)


def local(object_field, probe_field, intensities, off_rows, off_cols, counts):
    tall, wide = object_field.shape[1:]
    length = probe_field.shape[1]
    slots = off_rows.shape[2]
    half = length // 2
    high = tall + length
    blocks = wide // LANES
    tables = jnp.asarray(dft_parts(length))
    measured = intensities.reshape(slots, length, length)
    count_rows, count_cols = lax.axis_size("row"), lax.axis_size("col")

    def info_space(tiles):
        return [pltpu.SMEM((tiles, INFO, LANES), jnp.float32), pltpu.SemaphoreType.DMA((1,))]

    extended = (2, blocks + 1, high, LANES)
    ext, right, below, corner = call(
        halo_kernel,
        [extended, (2, tall, length), (2, length, wide), (2, length, length)],
        [pltpu.SemaphoreType.DMA((3 + 2 * blocks,))],
        [object_field],
        space=pl.ANY,
    )
    probe_now, own, measured, tables, info = call(
        load_kernel,
        [
            (2, length, length),
            (2, half, length),
            jax.ShapeDtypeStruct(measured.shape, measured.dtype),
            jax.ShapeDtypeStruct(tables.shape, tables.dtype),
            (INFO, LANES),
        ],
        [
            pltpu.SMEM(off_rows.shape, jnp.int32),
            pltpu.SMEM(off_cols.shape, jnp.int32),
            pltpu.SMEM(counts.shape, jnp.int32),
            pltpu.SemaphoreType.DMA((7,)),
        ],
        [probe_field, measured, tables, off_rows, off_cols, counts],
        space=pl.ANY,
    )
    right = shift(right, "col", -1)
    corner = lax.ppermute(
        corner,
        ("row", "col"),
        [
            ((r + 1) * count_cols + c + 1, r * count_cols + c)
            for r in range(count_rows - 1)
            for c in range(count_cols - 1)
        ],
    )
    below = shift(below, "row", -1)
    size = 2 * high
    strip = (size + INFO, LANES)
    partial = (3, half, length)
    deposits = [(blocks + 1, size, LANES), (3, length, length)] + info_space(1)
    ext, keep, send, inner, middle, outer = call(
        first_kernel,
        [extended, partial, partial, strip, (size, LANES), strip],
        deposits,
        [ext, right, below, corner, probe_now, measured, tables, info],
        aliases={0: 0},
    )
    last_row, last_col = count_rows // 2, count_cols // 2
    edge = (2 * (blocks + 1) * length + 3 * INFO, LANES)
    padded = (blocks + 3, high + 2 * length, LANES)

    from_inner = swap(inner, "col", 0)
    from_outer = swap(outer, "col", 1)
    total, inner, outer, infos = call(
        strips_kernel,
        [(blocks + 1, size, LANES), edge, edge, (3, INFO, LANES)],
        [],
        [inner, middle, outer, from_inner, from_outer],
    )
    part = keep + flip(send, "row", 1)
    part = quad(part, "row", 2)
    ext, light = call(
        functools.partial(near_light_kernel, slots, tall),
        [extended, padded],
        [(length, length)] + info_space(3),
        [ext, infos, probe_now, total],
        aliases={0: 0},
    )
    part, inner, outer = tie(part, inner, outer)
    from_inner = swap(inner, "row", 0)
    from_outer = swap(outer, "row", 1)
    part = butterfly(part, "col", 1, last_col)
    part, from_inner, light = tie(part, from_inner, light)
    part = butterfly(part, "col", last_col)
    new_half = stepped(own, part)
    tile, _, infos = call(
        functools.partial(object_kernel, slots),
        [extended, padded, (9, INFO, LANES)],
        [(length, length)] + info_space(9),
        [ext, light, probe_now, total, infos, from_inner, from_outer],
        aliases={0: 0, 1: 1},
    )
    new_half, tile = tie(new_half, tile)
    (patches,) = call(patch_kernel, [(slots, 2, length, length)], info_space(1), [tile, info])
    new_other = flip(new_half, "row", 1)

    body_shape = (blocks + 1, 2 * tall, LANES)
    bottom_shape = (blocks + 1, 2 * length, LANES)
    keep, send, body, bottom = call(
        second_kernel,
        [partial, partial, body_shape, bottom_shape],
        deposits,
        [patches, new_half, new_other, measured, tables, info],
    )
    padded = (blocks + 2, tall + 2 * length, LANES)
    (light,) = call(
        functools.partial(light_kernel, slots),
        [(blocks, tall, LANES)],
        [padded, (length, length)] + info_space(9),
        [infos, new_half, new_other],
    )
    from_above = shift(bottom, "row", 1)
    (right,) = call(push_kernel, [(2 * tall, LANES)], [], [body, from_above])
    part = keep + flip(send, "row", 1)
    part = butterfly(part, "col", 1, last_col)
    part = butterfly(part, "col", last_col)
    from_left = shift(right, "col", 1)
    part = butterfly(part, "row", 2, last_row)
    part = butterfly(part, "row", last_row)
    last_half = stepped(new_half, part)
    last_other = flip(last_half, "row", 1)
    return call(
        final_kernel,
        [(2, tall, wide), (2, length, length)],
        [],
        [tile, light, body, from_above, from_left, last_half, last_other],
    )


def solution(mesh):
    placed = (
        P(None, "row", "col"),
        P(),
        P("row", "col", None, None, None),
        P("row", "col", None),
        P("row", "col", None),
        P("row", "col"),
    )
    return jax.shard_map(
        local, mesh=mesh, in_specs=placed, out_specs=(P(None, "row", "col"), P()), check_vma=False
    )
```

```python
import functools
import math

import jax
import jax.numpy as jnp
import numpy as np
from jax import lax
from jax.experimental import pallas as pl
from jax.experimental.pallas import tpu as pltpu
from jax.sharding import PartitionSpec as P

STEP_SIZE = 0.25
PROBE_STEP = 1.0
REGULARIZER = 1.0
COUNT_SCALE = 1.0 / 1024.0
LANES = 128
INFO = 8
VMEM_BYTES = 12 * 1024 * 1024


def dft_parts(length):
    points = np.arange(length)
    angles = (points[:, None] * points[None, :] % length) * (2.0 * math.pi / length)
    cosine = np.cos(angles) / math.sqrt(length)
    sine = np.sin(angles) / math.sqrt(length)
    forward = np.block([[cosine, -sine], [sine, cosine]]).astype(np.float32)
    parts = []
    for table in (forward, forward.T):
        high = table.astype(jnp.bfloat16)
        low = (table - high.astype(np.float32)).astype(jnp.bfloat16)
        parts += [high, low]
    return np.stack(parts)


def split(values):
    high = values.astype(jnp.bfloat16)
    low = (values - high.astype(jnp.float32)).astype(jnp.bfloat16)
    return high, low


def dot(left, right):
    return jnp.dot(left, right, preferred_element_type=jnp.float32)


def right_table(values, table_high, table_low):
    high, low = split(values)
    return dot(high, table_high) + (dot(high, table_low) + dot(low, table_high))


def left_table(table_high, table_low, values):
    high, low = split(values)
    rows = table_high.shape[0]
    both = dot(jnp.concatenate([table_high, table_low], axis=0), high)
    return both[:rows] + (both[rows:] + dot(table_high, low))


def parity(axis):
    return lax.axis_index(axis) % 2


def slot_place(info_ref, index, slot, slots):
    row = info_ref[index, 0, slot].astype(jnp.int32)
    col = info_ref[index, 0, slots + slot].astype(jnp.int32)
    return row, col, info_ref[index, 0, 2 * slots + slot]


def lane_index(length):
    return lax.broadcasted_iota(jnp.int32, (length, LANES), 1)


def take_patch(ext_ref, channel, row, col, length):
    block = col // LANES
    shift = col % LANES
    turn = (LANES - shift) % LANES
    first = pltpu.roll(ext_ref[channel, block, pl.ds(row, length), :], turn, 1)
    second = pltpu.roll(ext_ref[channel, block + 1, pl.ds(row, length), :], turn, 1)
    return jnp.where(lane_index(length) < LANES - shift, first, second)


def add_patch(acc_ref, row, col, values, length):
    block = col // LANES
    shift = col % LANES
    turned = pltpu.roll(values, shift, 1)
    late = lane_index(length) >= shift
    window = pl.ds(row, length)
    acc_ref[block, window, :] += jnp.where(late, turned, 0.0)
    acc_ref[block + 1, window, :] += jnp.where(late, 0.0, turned)


def add_light(light_ref, power_ref, row, col, weight, length):
    row, col = row + length, col + length
    inside = (row > 0) & (row < light_ref.shape[1] - length) & (col > 0) & (col < (light_ref.shape[0] - 1) * LANES)

    @pl.when(inside & (weight > 0.0))
    def _():
        add_patch(light_ref, row, col, power_ref[...], length)


def add_tiles(light_ref, power_ref, info_ref, tiles, tall, wide, slots, length):
    across = 1 - 2 * parity("col")
    down = 1 - 2 * parity("row")
    places = [(0, 0), (0, across), (0, -across)]
    places += [(down, step) for step in (-1, 0, 1)] + [(-down, step) for step in (-1, 0, 1)]
    for index in tiles:
        row_step, col_step = places[index]
        for s in range(slots):
            row, col, weight = slot_place(info_ref, index, s, slots)
            add_light(light_ref, power_ref, row + row_step * tall, col + col_step * wide, weight, length)


def fill_info(rows_ref, cols_ref, counts_ref, slots):
    lanes = lax.broadcasted_iota(jnp.int32, (INFO, LANES), 1)
    info = jnp.zeros((INFO, LANES), jnp.float32)
    count = counts_ref[0, 0]
    upper = lax.axis_index("row") < lax.axis_size("row") // 2
    for s in range(slots):
        inside = jnp.where(upper, s < count, s >= slots - count)
        weight = jnp.where(inside, 1.0, 0.0).astype(jnp.float32)
        info = jnp.where(lanes == s, rows_ref[0, 0, s].astype(jnp.float32), info)
        info = jnp.where(lanes == slots + s, cols_ref[0, 0, s].astype(jnp.float32), info)
        info = jnp.where(lanes == 2 * slots + s, weight, info)
    return info


def position_terms(patches, probe_real, probe_imag, measured_ref, tables_ref, weights, slots, length):
    forward_high, forward_low = tables_ref[0], tables_ref[1]
    backward_high, backward_low = tables_ref[2], tables_ref[3]
    exits = []
    for patch_real, patch_imag in patches:
        exits.append(
            jnp.concatenate(
                [
                    probe_real * patch_real - probe_imag * patch_imag,
                    probe_real * patch_imag + probe_imag * patch_real,
                ],
                axis=1,
            )
        )
    mid = right_table(jnp.concatenate(exits, axis=0), forward_high, forward_low)
    mid = jnp.concatenate(
        [
            jnp.concatenate(
                [
                    mid[s * length : (s + 1) * length, :length],
                    mid[s * length : (s + 1) * length, length:],
                ],
                axis=0,
            )
            for s in range(slots)
        ],
        axis=1,
    )
    freq = left_table(backward_high, backward_low, mid)
    scaled = []
    for s in range(slots):
        freq_real = freq[:length, s * length : (s + 1) * length]
        freq_imag = freq[length:, s * length : (s + 1) * length]
        measured = measured_ref[s].astype(jnp.float32)
        residual = freq_real * freq_real + freq_imag * freq_imag - COUNT_SCALE * measured
        scaled.append(jnp.concatenate([residual * freq_real, residual * freq_imag], axis=0))
    mid = left_table(forward_high, forward_low, jnp.concatenate(scaled, axis=1))
    mid = jnp.concatenate(
        [
            jnp.concatenate(
                [
                    mid[:length, s * length : (s + 1) * length],
                    mid[length:, s * length : (s + 1) * length],
                ],
                axis=1,
            )
            for s in range(slots)
        ],
        axis=0,
    )
    back = right_table(mid, backward_high, backward_low)
    updates = []
    for s in range(slots):
        rows = slice(s * length, (s + 1) * length)
        updates.append((back[rows, :length] * weights[s], back[rows, length:] * weights[s]))
    return updates


def probe_sums(patches, updates, weights, keep_ref, send_ref, sum_ref, length):
    slots = len(patches)
    grad_real = jnp.zeros((length, length), jnp.float32)
    grad_imag = grad_real
    light = grad_real
    for s in range(slots):
        (patch_real, patch_imag), (back_real, back_imag) = patches[s], updates[s]
        grad_real += patch_real * back_real + patch_imag * back_imag
        grad_imag += patch_real * back_imag - patch_imag * back_real
        light += weights[s] * (patch_real * patch_real + patch_imag * patch_imag)
    sum_ref[0] = grad_real
    sum_ref[1] = grad_imag
    sum_ref[2] = light
    half = length // 2
    side = parity("row")
    keep_ref[...] = sum_ref[:, pl.ds(pl.multiple_of(side * half, half), half), :]
    send_ref[...] = sum_ref[:, pl.ds(pl.multiple_of((1 - side) * half, half), half), :]


def deposit(updates, probe_real, probe_imag, places, dep_ref, length):
    dep_ref[...] = jnp.zeros_like(dep_ref)
    high = dep_ref.shape[1] // 2
    for s in range(len(updates)):
        back_real, back_imag = updates[s]
        row, col, _ = places[s]
        add_patch(dep_ref, row, col, probe_real * back_real + probe_imag * back_imag, length)
        add_patch(dep_ref, row + high, col, probe_real * back_imag - probe_imag * back_real, length)


def start_all(pairs, sems):
    copies = [pltpu.make_async_copy(source, target, sems.at[i]) for i, (source, target) in enumerate(pairs)]
    for copy in copies:
        copy.start()
    return copies


def wait_all(copies):
    for copy in copies:
        copy.wait()


def halo_kernel(field_ref, ext_ref, right_out, below_out, corner_out, sems):
    length = corner_out.shape[1]
    blocks = ext_ref.shape[1] - 1
    tall = field_ref.shape[1]
    pairs = [
        (field_ref.at[:, :, pl.ds(0, length)], right_out),
        (field_ref.at[:, pl.ds(0, length), :], below_out),
        (field_ref.at[:, pl.ds(0, length), pl.ds(0, length)], corner_out),
    ]
    for block in range(blocks):
        for channel in range(2):
            pairs.append(
                (
                    field_ref.at[channel, :, pl.ds(block * LANES, LANES)],
                    ext_ref.at[channel, block, pl.ds(0, tall), :],
                )
            )
    wait_all(start_all(pairs, sems))


def load_kernel(
    probe_ref, measured_ref, tables_ref, rows_ref, cols_ref, counts_ref,
    probe_out, half_out, measured_out, tables_out, info_out, rows_at, cols_at, counts_at, sems,
):
    half = half_out.shape[1]
    start = pl.multiple_of(parity("row") * half, half)
    pairs = [
        (rows_ref, rows_at),
        (cols_ref, cols_at),
        (counts_ref, counts_at),
        (probe_ref, probe_out),
        (probe_ref.at[:, pl.ds(start, half), :], half_out),
        (measured_ref, measured_out),
        (tables_ref, tables_out),
    ]
    copies = start_all(pairs, sems)
    wait_all(copies[:3])
    info_out[...] = fill_info(rows_at, cols_at, counts_at, rows_at.shape[2])
    wait_all(copies[3:])


def split_sides(inner_out, outer_out, dep_ref):
    size = dep_ref.shape[1]
    side = parity("col")
    inner_out[:size] = dep_ref[2 - 2 * side]
    outer_out[:size] = dep_ref[2 * side]


def first_kernel(
    start_ref, right_ref, below_ref, corner_ref, probe_ref, measured_ref, tables_ref, info_ref,
    ext_ref, keep_ref, send_ref, inner_out, middle_out, outer_out, dep_ref, sum_ref, info_at, sems,
):
    copies = start_all([(info_ref, info_at.at[0])], sems)
    length = probe_ref.shape[1]
    slots = measured_ref.shape[0]
    tall = right_ref.shape[1]
    blocks = below_ref.shape[2] // LANES
    for channel in range(2):
        for block in range(blocks):
            lanes = slice(block * LANES, (block + 1) * LANES)
            ext_ref[channel, block, tall:, :] = below_ref[channel, :, lanes]
        ext_ref[channel, blocks, :tall, :] = right_ref[channel]
        ext_ref[channel, blocks, tall:, :] = corner_ref[channel]
    probe_real, probe_imag = probe_ref[0], probe_ref[1]
    wait_all(copies)
    places = [slot_place(info_at, 0, s, slots) for s in range(slots)]
    patches = [
        [take_patch(ext_ref, channel, places[s][0], places[s][1], length) for channel in range(2)] for s in range(slots)
    ]
    weights = [place[2] for place in places]
    updates = position_terms(
        patches, probe_real, probe_imag, measured_ref, tables_ref, weights, slots, length
    )
    probe_sums(patches, updates, weights, keep_ref, send_ref, sum_ref, length)
    deposit(updates, probe_real, probe_imag, places, dep_ref, length)
    size = dep_ref.shape[1]
    middle_out[...] = dep_ref[1]
    split_sides(inner_out, outer_out, dep_ref)
    inner_out[size:] = info_ref[...]
    outer_out[size:] = info_ref[...]


def strips_kernel(
    inner_ref, middle_ref, outer_ref, from_inner, from_outer, total_out, inner_out, outer_out, infos_out
):
    size = middle_ref.shape[0]
    high = size // 2
    length = (inner_out.shape[0] - 3 * INFO) // 6
    tall = high - length
    side = parity("col")
    total_out[2 - 2 * side] = inner_ref[:size] + from_inner[:size]
    total_out[1] = middle_ref[...]
    total_out[2 * side] = outer_ref[:size] + from_outer[:size]
    side_row = parity("row")
    for block in range(3):
        for channel in range(2):
            rows = slice((2 * block + channel) * length, (2 * block + channel + 1) * length)
            start = channel * high + tall - side_row * tall
            inner_out[rows] = total_out[block, pl.ds(pl.multiple_of(start, 8), length), :]
            start = channel * high + side_row * tall
            outer_out[rows] = total_out[block, pl.ds(pl.multiple_of(start, 8), length), :]
    own, inner, outer = inner_ref[size:], from_inner[size:], from_outer[size:]
    infos_out[0], infos_out[1], infos_out[2] = own, inner, outer
    left = jnp.where(side == 0, outer, inner)
    right = jnp.where(side == 0, inner, outer)
    for index, info in enumerate((left, own, right)):
        rows = slice(6 * length + index * INFO, 6 * length + (index + 1) * INFO)
        inner_out[rows] = info
        outer_out[rows] = info


def update_rows(new_ref, ext_ref, light_ref, total_ref, extra, block, start, stop, length, inside):
    high = ext_ref.shape[2]
    scale = STEP_SIZE / (light_ref[block + 1, start + length : stop + length, :] + REGULARIZER)
    if inside is not None:
        scale = scale * inside
    for channel in range(2):
        total = total_ref[block, channel * high + start : channel * high + stop]
        if extra is not None:
            total = total + extra(2 * block + channel)
        new_ref[channel, block, start:stop, :] = ext_ref[channel, block, start:stop, :] - scale * total


def inside_mesh(axis):
    return jnp.where(lax.axis_index(axis) < lax.axis_size(axis) - 1, 1.0, 0.0).astype(jnp.float32)


def near_light_kernel(
    slots, tall, ext_ref, infos_ref, probe_ref, total_ref, new_ref, light_out, power_ref, info_at, sems
):
    copies = start_all([(infos_ref, info_at)], sems)
    length = power_ref.shape[0]
    power_ref[...] = probe_ref[0] * probe_ref[0] + probe_ref[1] * probe_ref[1]
    light_out[...] = jnp.zeros_like(light_out)
    wait_all(copies)
    wide = (light_out.shape[0] - 3) * LANES
    add_tiles(light_out, power_ref, info_at, range(3), tall, wide, slots, length)
    blocks = ext_ref.shape[1] - 1
    for block in range(blocks + 1):
        inside = inside_mesh("col") if block == blocks else None
        update_rows(new_ref, ext_ref, light_out, total_ref, None, block, length, tall, length, inside)


def object_kernel(
    slots, outer, ext_ref, light_in, probe_ref, total_ref, strip_ref, new_ref, light_ref, info_out, power_ref, info_at, sems
):
    length = power_ref.shape[0]
    high = ext_ref.shape[2]
    tall = high - length
    blocks = ext_ref.shape[1] - 1
    edge = 6 * length
    for index in range(3):
        info_out[index] = strip_ref[edge + index * INFO : edge + (index + 1) * INFO]
    copies = start_all([(info_out, info_at.at[pl.ds(3 + 3 * outer, 3)])], sems)
    power_ref[...] = probe_ref[0] * probe_ref[0] + probe_ref[1] * probe_ref[1]
    side = parity("row")
    below = side if outer else 1 - side
    start = below * tall
    inside_row = jnp.where(below == 1, inside_mesh("row"), 1.0)
    wait_all(copies)
    add_tiles(light_ref, power_ref, info_at, range(3 + 3 * outer, 6 + 3 * outer), tall, blocks * LANES, slots, length)
    window = pl.ds(pl.multiple_of(start, 8), length)
    for block in range(blocks + 1):
        light = light_ref[block + 1, pl.ds(pl.multiple_of(start + length, 8), length), :]
        inside = inside_row * inside_mesh("col") if block == blocks else inside_row
        scale = inside * (STEP_SIZE / (light + REGULARIZER))
        for channel in range(2):
            index = 2 * block + channel
            total = total_ref[block, pl.ds(pl.multiple_of(start + channel * high, 8), length), :]
            total = total + strip_ref[index * length : (index + 1) * length]
            new_ref[channel, block, window, :] = ext_ref[channel, block, window, :] - scale * total


def patch_kernel(ext_ref, info_ref, patches_out, info_at, sems):
    copies = start_all([(info_ref, info_at.at[0])], sems)
    slots, _, length, _ = patches_out.shape
    wait_all(copies)
    for s in range(slots):
        row, col, _ = slot_place(info_at, 0, s, slots)
        for channel in range(2):
            patches_out[s, channel] = take_patch(ext_ref, channel, row, col, length)


def assemble_probe(half_ref, other_ref, side):
    first = side == 0
    return [
        jnp.concatenate(
            [
                jnp.where(first, half_ref[channel], other_ref[channel]),
                jnp.where(first, other_ref[channel], half_ref[channel]),
            ],
            axis=0,
        )
        for channel in range(2)
    ]


def second_kernel(
    patches_ref, half_ref, other_ref, measured_ref, tables_ref, info_ref,
    keep_ref, send_ref, updates_out, sum_ref, info_at, sems,
):
    copies = start_all([(info_ref, info_at.at[0])], sems)
    slots = measured_ref.shape[0]
    length = measured_ref.shape[1]
    probe_real, probe_imag = assemble_probe(half_ref, other_ref, parity("row"))
    patches = [[patches_ref[s, channel] for channel in range(2)] for s in range(slots)]
    wait_all(copies)
    weights = [slot_place(info_at, 0, s, slots)[2] for s in range(slots)]
    updates = position_terms(
        patches, probe_real, probe_imag, measured_ref, tables_ref, weights, slots, length
    )
    probe_sums(patches, updates, weights, keep_ref, send_ref, sum_ref, length)
    for s in range(slots):
        updates_out[s, 0], updates_out[s, 1] = updates[s]


def deposit_kernel(updates_ref, half_ref, other_ref, info_ref, body_out, bottom_out, dep_ref, info_at, sems):
    copies = start_all([(info_ref, info_at.at[0])], sems)
    slots, _, length, _ = updates_ref.shape
    probe_real, probe_imag = assemble_probe(half_ref, other_ref, parity("row"))
    wait_all(copies)
    places = [slot_place(info_at, 0, s, slots) for s in range(slots)]
    updates = [(updates_ref[s, 0], updates_ref[s, 1]) for s in range(slots)]
    deposit(updates, probe_real, probe_imag, places, dep_ref, length)
    high = dep_ref.shape[1] // 2
    tall = body_out.shape[1] // 2
    for channel in range(2):
        start = channel * high
        body_out[:, channel * tall : (channel + 1) * tall] = dep_ref[:, start : start + tall, :]
        bottom_out[:, channel * length : (channel + 1) * length] = dep_ref[:, start + tall : start + high, :]


def light_kernel(
    slots, near_ref, inner_ref, outer_ref, half_ref, other_ref, light_out, light_ref, power_ref, info_at, sems
):
    parts = (near_ref, inner_ref, outer_ref)
    copies = start_all([(part, info_at.at[pl.ds(3 * index, 3)]) for index, part in enumerate(parts)], sems)
    length = power_ref.shape[0]
    tall = light_out.shape[1]
    blocks = light_out.shape[0]
    probe_real, probe_imag = assemble_probe(half_ref, other_ref, parity("row"))
    power_ref[...] = probe_real * probe_real + probe_imag * probe_imag
    light_ref[...] = jnp.zeros_like(light_ref)
    wait_all(copies)
    add_tiles(light_ref, power_ref, info_at, range(9), tall, blocks * LANES, slots, length)
    light_out[...] = STEP_SIZE / (light_ref[1 : 1 + blocks, length : length + tall, :] + REGULARIZER)


def push_kernel(body_ref, from_above, right_out):
    tall = body_ref.shape[1] // 2
    length = from_above.shape[1] // 2
    last = body_ref.shape[0] - 1
    for channel in range(2):
        start = channel * tall
        right_out[start : start + length] = (
            body_ref[last, start : start + length] + from_above[last, channel * length : (channel + 1) * length]
        )
        right_out[start + length : start + tall] = body_ref[last, start + length : start + tall]


def final_kernel(tile_ref, light_ref, body_ref, from_above, from_left, half_ref, other_ref, object_out, probe_out):
    tall = body_ref.shape[1] // 2
    length = from_above.shape[1] // 2
    for block in range(light_ref.shape[0]):
        lanes = slice(block * LANES, (block + 1) * LANES)
        for channel in range(2):
            for start, stop in ((0, length), (length, tall)):
                rows = slice(channel * tall + start, channel * tall + stop)
                total = body_ref[block, rows]
                if start == 0:
                    total = total + from_above[block, channel * length : (channel + 1) * length]
                if block == 0:
                    total = total + from_left[rows]
                object_out[channel, start:stop, lanes] = (
                    tile_ref[channel, block, start:stop, :] - light_ref[block, start:stop, :] * total
                )
    probe_out[0], probe_out[1] = assemble_probe(half_ref, other_ref, parity("row"))


def shift(value, axis, steps):
    count = lax.axis_size(axis)
    pairs = [(source, source + steps) for source in range(count) if 0 <= source + steps < count]
    return lax.ppermute(value, axis, pairs)


def swap(value, axis, first):
    count = lax.axis_size(axis)
    pairs = []
    for low in range(first, count - 1, 2):
        pairs += [(low, low + 1), (low + 1, low)]
    return lax.ppermute(value, axis, pairs)


def flip(value, axis, mask):
    count = lax.axis_size(axis)
    return lax.ppermute(value, axis, [(source, source ^ mask) for source in range(count)])


def tie(*values):
    return lax.optimization_barrier(values)


def butterfly(total, axis, first, stop=None):
    bit = first
    while bit < (stop or lax.axis_size(axis)):
        total = total + flip(total, axis, bit)
        bit *= 2
    return total


def quad(total, axis, first):
    bit = first
    while 2 * bit < lax.axis_size(axis):
        one, two, three = (flip(total, axis, bit * mask) for mask in (1, 2, 3))
        total = (total + one) + (two + three)
        bit *= 4
    return butterfly(total, axis, bit)


def stepped(half, total):
    return half - PROBE_STEP * total[:2] / (total[2] + REGULARIZER)


def shape_of(spec):
    return spec if isinstance(spec, jax.ShapeDtypeStruct) else jax.ShapeDtypeStruct(spec, jnp.float32)


def call(kernel, outs, scratch, args, aliases={}, space=pltpu.VMEM):
    vmem = pl.BlockSpec(memory_space=pltpu.VMEM)
    return pl.pallas_call(
        kernel,
        out_shape=[shape_of(spec) for spec in outs],
        in_specs=[pl.BlockSpec(memory_space=space)] * len(args),
        out_specs=[vmem] * len(outs),
        scratch_shapes=[pltpu.VMEM(shape, jnp.float32) if isinstance(shape, tuple) else shape for shape in scratch],
        compiler_params=pltpu.CompilerParams(vmem_limit_bytes=VMEM_BYTES),
        input_output_aliases=aliases,
    )(*args)


def local(object_field, probe_field, intensities, off_rows, off_cols, counts):
    tall, wide = object_field.shape[1:]
    length = probe_field.shape[1]
    slots = off_rows.shape[2]
    half = length // 2
    high = tall + length
    blocks = wide // LANES
    tables = jnp.asarray(dft_parts(length))
    measured = intensities.reshape(slots, length, length)
    count_rows, count_cols = lax.axis_size("row"), lax.axis_size("col")

    def info_space(tiles):
        return [pltpu.SMEM((tiles, INFO, LANES), jnp.float32), pltpu.SemaphoreType.DMA((3,))]

    extended = (2, blocks + 1, high, LANES)
    ext, right, below, corner = call(
        halo_kernel,
        [extended, (2, tall, length), (2, length, wide), (2, length, length)],
        [pltpu.SemaphoreType.DMA((3 + 2 * blocks,))],
        [object_field],
        space=pl.ANY,
    )
    probe_now, own, measured, tables, info = call(
        load_kernel,
        [
            (2, length, length),
            (2, half, length),
            jax.ShapeDtypeStruct(measured.shape, measured.dtype),
            jax.ShapeDtypeStruct(tables.shape, tables.dtype),
            (INFO, LANES),
        ],
        [
            pltpu.SMEM(off_rows.shape, jnp.int32),
            pltpu.SMEM(off_cols.shape, jnp.int32),
            pltpu.SMEM(counts.shape, jnp.int32),
            pltpu.SemaphoreType.DMA((7,)),
        ],
        [probe_field, measured, tables, off_rows, off_cols, counts],
        space=pl.ANY,
    )
    right = shift(right, "col", -1)
    corner = lax.ppermute(
        corner,
        ("row", "col"),
        [
            ((r + 1) * count_cols + c + 1, r * count_cols + c)
            for r in range(count_rows - 1)
            for c in range(count_cols - 1)
        ],
    )
    below = shift(below, "row", -1)
    size = 2 * high
    strip = (size + INFO, LANES)
    partial = (3, half, length)
    deposits = [(blocks + 1, size, LANES), (3, length, length)] + info_space(1)
    ext, keep, send, inner, middle, outer = call(
        first_kernel,
        [extended, partial, partial, strip, (size, LANES), strip],
        deposits,
        [ext, right, below, corner, probe_now, measured, tables, info],
        aliases={0: 0},
    )
    last_row, last_col = count_rows // 2, count_cols // 2
    edge = (2 * (blocks + 1) * length + 3 * INFO, LANES)
    padded = (blocks + 3, high + 2 * length, LANES)

    from_inner = swap(inner, "col", 0)
    from_outer = swap(outer, "col", 1)
    total, inner, outer, infos = call(
        strips_kernel,
        [(blocks + 1, size, LANES), edge, edge, (3, INFO, LANES)],
        [],
        [inner, middle, outer, from_inner, from_outer],
    )
    part = keep + flip(send, "row", 1)
    part = quad(part, "row", 2)
    ext, light = call(
        functools.partial(near_light_kernel, slots, tall),
        [extended, padded],
        [(length, length)] + info_space(3),
        [ext, infos, probe_now, total],
        aliases={0: 0},
    )
    part, inner, outer = tie(part, inner, outer)
    from_inner = swap(inner, "row", 0)
    from_outer = swap(outer, "row", 1)
    row_infos = []

    def update(ext, light, strip, outer):
        ext, light, info_rows = call(
            functools.partial(object_kernel, slots, outer),
            [extended, padded, (3, INFO, LANES)],
            [(length, length)] + info_space(9),
            [ext, light, probe_now, total, strip],
            aliases={0: 0, 1: 1},
        )
        row_infos.append(info_rows)
        return ext, light

    part = butterfly(part, "col", 1, last_col)
    part, from_inner, light = tie(part, from_inner, light)
    ext, light = update(ext, light, from_inner, 0)
    part = butterfly(part, "col", last_col)
    new_half = stepped(own, part)
    tile, _ = update(ext, light, from_outer, 1)
    new_half, tile = tie(new_half, tile)
    (patches,) = call(patch_kernel, [(slots, 2, length, length)], info_space(1), [tile, info])
    new_other = flip(new_half, "row", 1)

    body_shape = (blocks + 1, 2 * tall, LANES)
    bottom_shape = (blocks + 1, 2 * length, LANES)
    keep, send, updates = call(
        second_kernel,
        [partial, partial, (slots, 2, length, length)],
        [(3, length, length)] + info_space(1),
        [patches, new_half, new_other, measured, tables, info],
    )
    body, bottom = call(
        deposit_kernel,
        [body_shape, bottom_shape],
        [(blocks + 1, size, LANES)] + info_space(1),
        [updates, new_half, new_other, info],
    )
    padded = (blocks + 2, tall + 2 * length, LANES)
    (light,) = call(
        functools.partial(light_kernel, slots),
        [(blocks, tall, LANES)],
        [padded, (length, length)] + info_space(9),
        [infos, *row_infos, new_half, new_other],
    )
    from_above = shift(bottom, "row", 1)
    (right,) = call(push_kernel, [(2 * tall, LANES)], [], [body, from_above])
    part = keep + flip(send, "row", 1)
    part, bottom = tie(part, bottom)
    part = butterfly(part, "col", 1, last_col)
    part = butterfly(part, "col", last_col)
    from_left = shift(right, "col", 1)
    part = butterfly(part, "row", 2, last_row)
    part = butterfly(part, "row", last_row)
    last_half = stepped(new_half, part)
    last_other = flip(last_half, "row", 1)
    return call(
        final_kernel,
        [(2, tall, wide), (2, length, length)],
        [],
        [tile, light, body, from_above, from_left, last_half, last_other],
    )


def solution(mesh):
    placed = (
        P(None, "row", "col"),
        P(),
        P("row", "col", None, None, None),
        P("row", "col", None),
        P("row", "col", None),
        P("row", "col"),
    )
    return jax.shard_map(
        local, mesh=mesh, in_specs=placed, out_specs=(P(None, "row", "col"), P()), check_vma=False
    )
```

```python
import functools
import math

import jax
import jax.numpy as jnp
import numpy as np
from jax import lax
from jax.experimental import pallas as pl
from jax.experimental.pallas import tpu as pltpu
from jax.sharding import PartitionSpec as P

STEP_SIZE = 0.25
PROBE_STEP = 1.0
REGULARIZER = 1.0
COUNT_SCALE = 1.0 / 1024.0
LANES = 128
INFO = 8
VMEM_BYTES = 12 * 1024 * 1024


def dft_parts(length):
    points = np.arange(length)
    angles = (points[:, None] * points[None, :] % length) * (2.0 * math.pi / length)
    cosine = np.cos(angles) / math.sqrt(length)
    sine = np.sin(angles) / math.sqrt(length)
    forward = np.block([[cosine, -sine], [sine, cosine]]).astype(np.float32)
    parts = []
    for table in (forward, forward.T):
        high = table.astype(jnp.bfloat16)
        low = (table - high.astype(np.float32)).astype(jnp.bfloat16)
        parts += [high, low]
    return np.stack(parts)


def split(values):
    high = values.astype(jnp.bfloat16)
    low = (values - high.astype(jnp.float32)).astype(jnp.bfloat16)
    return high, low


def dot(left, right):
    return jnp.dot(left, right, preferred_element_type=jnp.float32)


def right_table(values, table_high, table_low):
    high, low = split(values)
    return dot(high, table_high) + (dot(high, table_low) + dot(low, table_high))


def left_table(table_high, table_low, values):
    high, low = split(values)
    rows = table_high.shape[0]
    both = dot(jnp.concatenate([table_high, table_low], axis=0), high)
    return both[:rows] + (both[rows:] + dot(table_high, low))


def parity(axis):
    return lax.axis_index(axis) % 2


def slot_place(info_ref, index, slot, slots):
    row = info_ref[index, 0, slot].astype(jnp.int32)
    col = info_ref[index, 0, slots + slot].astype(jnp.int32)
    return row, col, info_ref[index, 0, 2 * slots + slot]


def lane_index(length):
    return lax.broadcasted_iota(jnp.int32, (length, LANES), 1)


def take_patch(ext_ref, channel, row, col, length):
    block = col // LANES
    shift = col % LANES
    turn = (LANES - shift) % LANES
    first = pltpu.roll(ext_ref[channel, block, pl.ds(row, length), :], turn, 1)
    second = pltpu.roll(ext_ref[channel, block + 1, pl.ds(row, length), :], turn, 1)
    return jnp.where(lane_index(length) < LANES - shift, first, second)


def add_patch(acc_ref, row, col, values, length):
    block = col // LANES
    shift = col % LANES
    turned = pltpu.roll(values, shift, 1)
    late = lane_index(length) >= shift
    window = pl.ds(row, length)
    acc_ref[block, window, :] += jnp.where(late, turned, 0.0)
    acc_ref[block + 1, window, :] += jnp.where(late, 0.0, turned)


def add_light(light_ref, power_ref, row, col, weight, length):
    row, col = row + length, col + length
    inside = (row > 0) & (row < light_ref.shape[1] - length) & (col > 0) & (col < (light_ref.shape[0] - 1) * LANES)

    @pl.when(inside & (weight > 0.0))
    def _():
        add_patch(light_ref, row, col, power_ref[...], length)


def add_tile(light_ref, power_ref, info_ref, index, down, across, tall, wide, slots, length):
    for s in range(slots):
        row, col, weight = slot_place(info_ref, index, s, slots)
        add_light(light_ref, power_ref, row + down * tall, col + across * wide, weight, length)


def add_tiles(light_ref, power_ref, info_ref, tiles, tall, wide, slots, length):
    across = 1 - 2 * parity("col")
    down = 1 - 2 * parity("row")
    places = [(0, 0), (0, across), (0, -across)]
    places += [(down, step) for step in (-1, 0, 1)] + [(-down, step) for step in (-1, 0, 1)]
    for index in tiles:
        add_tile(light_ref, power_ref, info_ref, index, *places[index], tall, wide, slots, length)


def fill_info(rows_ref, cols_ref, counts_ref, slots):
    lanes = lax.broadcasted_iota(jnp.int32, (INFO, LANES), 1)
    info = jnp.zeros((INFO, LANES), jnp.float32)
    count = counts_ref[0, 0]
    upper = lax.axis_index("row") < lax.axis_size("row") // 2
    for s in range(slots):
        inside = jnp.where(upper, s < count, s >= slots - count)
        weight = jnp.where(inside, 1.0, 0.0).astype(jnp.float32)
        info = jnp.where(lanes == s, rows_ref[0, 0, s].astype(jnp.float32), info)
        info = jnp.where(lanes == slots + s, cols_ref[0, 0, s].astype(jnp.float32), info)
        info = jnp.where(lanes == 2 * slots + s, weight, info)
    return info


def position_terms(patches, probe_real, probe_imag, measured_ref, tables_ref, weights, slots, length):
    forward_high, forward_low = tables_ref[0], tables_ref[1]
    backward_high, backward_low = tables_ref[2], tables_ref[3]
    exits = []
    for patch_real, patch_imag in patches:
        exits.append(
            jnp.concatenate(
                [
                    probe_real * patch_real - probe_imag * patch_imag,
                    probe_real * patch_imag + probe_imag * patch_real,
                ],
                axis=1,
            )
        )
    mid = right_table(jnp.concatenate(exits, axis=0), forward_high, forward_low)
    mid = jnp.concatenate(
        [
            jnp.concatenate(
                [
                    mid[s * length : (s + 1) * length, :length],
                    mid[s * length : (s + 1) * length, length:],
                ],
                axis=0,
            )
            for s in range(slots)
        ],
        axis=1,
    )
    freq = left_table(backward_high, backward_low, mid)
    scaled = []
    for s in range(slots):
        freq_real = freq[:length, s * length : (s + 1) * length]
        freq_imag = freq[length:, s * length : (s + 1) * length]
        measured = measured_ref[s].astype(jnp.float32)
        residual = freq_real * freq_real + freq_imag * freq_imag - COUNT_SCALE * measured
        scaled.append(jnp.concatenate([residual * freq_real, residual * freq_imag], axis=0))
    mid = left_table(forward_high, forward_low, jnp.concatenate(scaled, axis=1))
    mid = jnp.concatenate(
        [
            jnp.concatenate(
                [
                    mid[:length, s * length : (s + 1) * length],
                    mid[length:, s * length : (s + 1) * length],
                ],
                axis=1,
            )
            for s in range(slots)
        ],
        axis=0,
    )
    back = right_table(mid, backward_high, backward_low)
    updates = []
    for s in range(slots):
        rows = slice(s * length, (s + 1) * length)
        updates.append((back[rows, :length] * weights[s], back[rows, length:] * weights[s]))
    return updates


def probe_sums(patches, updates, weights, keep_ref, send_ref, sum_ref, length):
    slots = len(patches)
    grad_real = jnp.zeros((length, length), jnp.float32)
    grad_imag = grad_real
    light = grad_real
    for s in range(slots):
        (patch_real, patch_imag), (back_real, back_imag) = patches[s], updates[s]
        grad_real += patch_real * back_real + patch_imag * back_imag
        grad_imag += patch_real * back_imag - patch_imag * back_real
        light += weights[s] * (patch_real * patch_real + patch_imag * patch_imag)
    sum_ref[0] = grad_real
    sum_ref[1] = grad_imag
    sum_ref[2] = light
    half = length // 2
    side = parity("row")
    keep_ref[...] = sum_ref[:, pl.ds(pl.multiple_of(side * half, half), half), :]
    send_ref[...] = sum_ref[:, pl.ds(pl.multiple_of((1 - side) * half, half), half), :]


def deposit(updates, probe_real, probe_imag, places, dep_ref, length):
    dep_ref[...] = jnp.zeros_like(dep_ref)
    high = dep_ref.shape[1] // 2
    for s in range(len(updates)):
        back_real, back_imag = updates[s]
        row, col, _ = places[s]
        add_patch(dep_ref, row, col, probe_real * back_real + probe_imag * back_imag, length)
        add_patch(dep_ref, row + high, col, probe_real * back_imag - probe_imag * back_real, length)


def start_all(pairs, sems):
    copies = [pltpu.make_async_copy(source, target, sems.at[i]) for i, (source, target) in enumerate(pairs)]
    for copy in copies:
        copy.start()
    return copies


def wait_all(copies):
    for copy in copies:
        copy.wait()


def halo_kernel(field_ref, ext_ref, right_out, below_out, corner_out, sems):
    length = corner_out.shape[1]
    blocks = ext_ref.shape[1] - 1
    tall = field_ref.shape[1]
    pairs = [
        (field_ref.at[:, :, pl.ds(0, length)], right_out),
        (field_ref.at[:, pl.ds(0, length), :], below_out),
        (field_ref.at[:, pl.ds(0, length), pl.ds(0, length)], corner_out),
    ]
    for block in range(blocks):
        for channel in range(2):
            pairs.append(
                (
                    field_ref.at[channel, :, pl.ds(block * LANES, LANES)],
                    ext_ref.at[channel, block, pl.ds(0, tall), :],
                )
            )
    wait_all(start_all(pairs, sems))


def load_kernel(
    probe_ref, measured_ref, tables_ref, rows_ref, cols_ref, counts_ref,
    probe_out, half_out, measured_out, tables_out, info_out, rows_at, cols_at, counts_at, sems,
):
    half = half_out.shape[1]
    start = pl.multiple_of(parity("row") * half, half)
    pairs = [
        (rows_ref, rows_at),
        (cols_ref, cols_at),
        (counts_ref, counts_at),
        (probe_ref, probe_out),
        (probe_ref.at[:, pl.ds(start, half), :], half_out),
        (measured_ref, measured_out),
        (tables_ref, tables_out),
    ]
    copies = start_all(pairs, sems)
    wait_all(copies[:3])
    info_out[...] = fill_info(rows_at, cols_at, counts_at, rows_at.shape[2])
    wait_all(copies[3:])


def split_sides(inner_out, outer_out, dep_ref):
    size = dep_ref.shape[1]
    side = parity("col")
    inner_out[:size] = dep_ref[2 - 2 * side]
    outer_out[:size] = dep_ref[2 * side]


def first_kernel(
    start_ref, right_ref, below_ref, corner_ref, probe_ref, measured_ref, tables_ref, info_ref,
    ext_ref, keep_ref, send_ref, inner_out, middle_out, outer_out, dep_ref, sum_ref, info_at, sems,
):
    copies = start_all([(info_ref, info_at.at[0])], sems)
    length = probe_ref.shape[1]
    slots = measured_ref.shape[0]
    tall = right_ref.shape[1]
    blocks = below_ref.shape[2] // LANES
    for channel in range(2):
        for block in range(blocks):
            lanes = slice(block * LANES, (block + 1) * LANES)
            ext_ref[channel, block, tall:, :] = below_ref[channel, :, lanes]
        ext_ref[channel, blocks, :tall, :] = right_ref[channel]
        ext_ref[channel, blocks, tall:, :] = corner_ref[channel]
    probe_real, probe_imag = probe_ref[0], probe_ref[1]
    wait_all(copies)
    places = [slot_place(info_at, 0, s, slots) for s in range(slots)]
    patches = [
        [take_patch(ext_ref, channel, places[s][0], places[s][1], length) for channel in range(2)] for s in range(slots)
    ]
    weights = [place[2] for place in places]
    updates = position_terms(
        patches, probe_real, probe_imag, measured_ref, tables_ref, weights, slots, length
    )
    probe_sums(patches, updates, weights, keep_ref, send_ref, sum_ref, length)
    deposit(updates, probe_real, probe_imag, places, dep_ref, length)
    size = dep_ref.shape[1]
    middle_out[...] = dep_ref[1]
    split_sides(inner_out, outer_out, dep_ref)
    inner_out[size:] = info_ref[...]
    outer_out[size:] = info_ref[...]


def strips_kernel(
    inner_ref, middle_ref, outer_ref, from_inner, from_outer, total_out, inner_out, outer_out, infos_out
):
    size = middle_ref.shape[0]
    high = size // 2
    length = (inner_out.shape[0] - 3 * INFO) // 6
    tall = high - length
    side = parity("col")
    total_out[2 - 2 * side] = inner_ref[:size] + from_inner[:size]
    total_out[1] = middle_ref[...]
    total_out[2 * side] = outer_ref[:size] + from_outer[:size]
    side_row = parity("row")
    for block in range(3):
        for channel in range(2):
            rows = slice((2 * block + channel) * length, (2 * block + channel + 1) * length)
            start = channel * high + tall - side_row * tall
            inner_out[rows] = total_out[block, pl.ds(pl.multiple_of(start, 8), length), :]
            start = channel * high + side_row * tall
            outer_out[rows] = total_out[block, pl.ds(pl.multiple_of(start, 8), length), :]
    own, inner, outer = inner_ref[size:], from_inner[size:], from_outer[size:]
    infos_out[0], infos_out[1], infos_out[2] = own, inner, outer
    left = jnp.where(side == 0, outer, inner)
    right = jnp.where(side == 0, inner, outer)
    for index, info in enumerate((left, own, right)):
        rows = slice(6 * length + index * INFO, 6 * length + (index + 1) * INFO)
        inner_out[rows] = info
        outer_out[rows] = info


def update_rows(new_ref, ext_ref, light_ref, total_ref, extra, block, start, stop, length, inside):
    high = ext_ref.shape[2]
    scale = STEP_SIZE / (light_ref[block + 1, start + length : stop + length, :] + REGULARIZER)
    if inside is not None:
        scale = scale * inside
    for channel in range(2):
        total = total_ref[block, channel * high + start : channel * high + stop]
        if extra is not None:
            total = total + extra(2 * block + channel)
        new_ref[channel, block, start:stop, :] = ext_ref[channel, block, start:stop, :] - scale * total


def inside_mesh(axis):
    return jnp.where(lax.axis_index(axis) < lax.axis_size(axis) - 1, 1.0, 0.0).astype(jnp.float32)


def near_light_kernel(
    slots, tall, ext_ref, infos_ref, probe_ref, total_ref, new_ref, light_out, power_ref, info_at, sems
):
    copies = start_all([(infos_ref, info_at)], sems)
    length = power_ref.shape[0]
    power_ref[...] = probe_ref[0] * probe_ref[0] + probe_ref[1] * probe_ref[1]
    light_out[...] = jnp.zeros_like(light_out)
    wait_all(copies)
    wide = (light_out.shape[0] - 3) * LANES
    add_tiles(light_out, power_ref, info_at, range(3), tall, wide, slots, length)
    blocks = ext_ref.shape[1] - 1
    for block in range(blocks + 1):
        inside = inside_mesh("col") if block == blocks else None
        update_rows(new_ref, ext_ref, light_out, total_ref, None, block, length, tall, length, inside)


def object_kernel(
    slots, outer, ext_ref, light_in, probe_ref, total_ref, strip_ref, new_ref, light_ref, info_out, power_ref, info_at, sems
):
    length = power_ref.shape[0]
    high = ext_ref.shape[2]
    tall = high - length
    blocks = ext_ref.shape[1] - 1
    edge = 6 * length
    for index in range(3):
        info_out[index] = strip_ref[edge + index * INFO : edge + (index + 1) * INFO]
    copies = start_all([(info_out, info_at.at[pl.ds(3 + 3 * outer, 3)])], sems)
    power_ref[...] = probe_ref[0] * probe_ref[0] + probe_ref[1] * probe_ref[1]
    side = parity("row")
    below = side if outer else 1 - side
    start = below * tall
    inside_row = jnp.where(below == 1, inside_mesh("row"), 1.0)
    wait_all(copies)
    add_tiles(light_ref, power_ref, info_at, range(3 + 3 * outer, 6 + 3 * outer), tall, blocks * LANES, slots, length)
    window = pl.ds(pl.multiple_of(start, 8), length)
    for block in range(blocks + 1):
        light = light_ref[block + 1, pl.ds(pl.multiple_of(start + length, 8), length), :]
        inside = inside_row * inside_mesh("col") if block == blocks else inside_row
        scale = inside * (STEP_SIZE / (light + REGULARIZER))
        for channel in range(2):
            index = 2 * block + channel
            total = total_ref[block, pl.ds(pl.multiple_of(start + channel * high, 8), length), :]
            total = total + strip_ref[index * length : (index + 1) * length]
            new_ref[channel, block, window, :] = ext_ref[channel, block, window, :] - scale * total


def patch_kernel(ext_ref, info_ref, patches_out, info_at, sems):
    copies = start_all([(info_ref, info_at.at[0])], sems)
    slots, _, length, _ = patches_out.shape
    wait_all(copies)
    for s in range(slots):
        row, col, _ = slot_place(info_at, 0, s, slots)
        for channel in range(2):
            patches_out[s, channel] = take_patch(ext_ref, channel, row, col, length)


def assemble_probe(half_ref, other_ref, side):
    first = side == 0
    return [
        jnp.concatenate(
            [
                jnp.where(first, half_ref[channel], other_ref[channel]),
                jnp.where(first, other_ref[channel], half_ref[channel]),
            ],
            axis=0,
        )
        for channel in range(2)
    ]


def second_kernel(
    patches_ref, half_ref, other_ref, measured_ref, tables_ref, info_ref,
    keep_ref, send_ref, updates_out, sum_ref, info_at, sems,
):
    copies = start_all([(info_ref, info_at.at[0])], sems)
    slots = measured_ref.shape[0]
    length = measured_ref.shape[1]
    probe_real, probe_imag = assemble_probe(half_ref, other_ref, parity("row"))
    patches = [[patches_ref[s, channel] for channel in range(2)] for s in range(slots)]
    wait_all(copies)
    weights = [slot_place(info_at, 0, s, slots)[2] for s in range(slots)]
    updates = position_terms(
        patches, probe_real, probe_imag, measured_ref, tables_ref, weights, slots, length
    )
    probe_sums(patches, updates, weights, keep_ref, send_ref, sum_ref, length)
    for s in range(slots):
        updates_out[s, 0], updates_out[s, 1] = updates[s]


def deposit_kernel(updates_ref, half_ref, other_ref, info_ref, body_out, bottom_out, dep_ref, info_at, sems):
    copies = start_all([(info_ref, info_at.at[0])], sems)
    slots, _, length, _ = updates_ref.shape
    probe_real, probe_imag = assemble_probe(half_ref, other_ref, parity("row"))
    wait_all(copies)
    places = [slot_place(info_at, 0, s, slots) for s in range(slots)]
    updates = [(updates_ref[s, 0], updates_ref[s, 1]) for s in range(slots)]
    deposit(updates, probe_real, probe_imag, places, dep_ref, length)
    high = dep_ref.shape[1] // 2
    tall = body_out.shape[1] // 2
    for channel in range(2):
        start = channel * high
        body_out[:, channel * tall : (channel + 1) * tall] = dep_ref[:, start : start + tall, :]
        bottom_out[:, channel * length : (channel + 1) * length] = dep_ref[:, start + tall : start + high, :]


def light_kernel(
    slots, near_ref, inner_ref, outer_ref, half_ref, other_ref, light_out, light_ref, power_ref, info_at, sems
):
    parts = (near_ref, inner_ref, outer_ref)
    copies = start_all([(part, info_at.at[pl.ds(3 * index, 3)]) for index, part in enumerate(parts)], sems)
    length = power_ref.shape[0]
    tall = light_out.shape[1]
    blocks = light_out.shape[0]
    probe_real, probe_imag = assemble_probe(half_ref, other_ref, parity("row"))
    power_ref[...] = probe_real * probe_real + probe_imag * probe_imag
    light_ref[...] = jnp.zeros_like(light_ref)
    wait_all(copies)
    left, above = 2 - parity("col"), 6 - 3 * parity("row")
    for index, down, across in ((0, 0, 0), (left, 0, -1), (above, -1, -1), (above + 1, -1, 0)):
        add_tile(light_ref, power_ref, info_at, index, down, across, tall, blocks * LANES, slots, length)
    light_out[...] = STEP_SIZE / (light_ref[1 : 1 + blocks, length : length + tall, :] + REGULARIZER)


def push_kernel(body_ref, from_above, right_out):
    tall = body_ref.shape[1] // 2
    length = from_above.shape[1] // 2
    last = body_ref.shape[0] - 1
    for channel in range(2):
        start = channel * tall
        right_out[start : start + length] = (
            body_ref[last, start : start + length] + from_above[last, channel * length : (channel + 1) * length]
        )
        right_out[start + length : start + tall] = body_ref[last, start + length : start + tall]


def final_kernel(tile_ref, light_ref, body_ref, from_above, from_left, half_ref, other_ref, object_out, probe_out):
    tall = body_ref.shape[1] // 2
    length = from_above.shape[1] // 2
    for block in range(light_ref.shape[0]):
        lanes = slice(block * LANES, (block + 1) * LANES)
        for channel in range(2):
            for start, stop in ((0, length), (length, tall)):
                rows = slice(channel * tall + start, channel * tall + stop)
                total = body_ref[block, rows]
                if start == 0:
                    total = total + from_above[block, channel * length : (channel + 1) * length]
                if block == 0:
                    total = total + from_left[rows]
                object_out[channel, start:stop, lanes] = (
                    tile_ref[channel, block, start:stop, :] - light_ref[block, start:stop, :] * total
                )
    probe_out[0], probe_out[1] = assemble_probe(half_ref, other_ref, parity("row"))


def shift(value, axis, steps):
    count = lax.axis_size(axis)
    pairs = [(source, source + steps) for source in range(count) if 0 <= source + steps < count]
    return lax.ppermute(value, axis, pairs)


def swap(value, axis, first):
    count = lax.axis_size(axis)
    pairs = []
    for low in range(first, count - 1, 2):
        pairs += [(low, low + 1), (low + 1, low)]
    return lax.ppermute(value, axis, pairs)


def flip(value, axis, mask):
    count = lax.axis_size(axis)
    return lax.ppermute(value, axis, [(source, source ^ mask) for source in range(count)])


def tie(*values):
    return lax.optimization_barrier(values)


def butterfly(total, axis, first, stop=None):
    bit = first
    while bit < (stop or lax.axis_size(axis)):
        total = total + flip(total, axis, bit)
        bit *= 2
    return total


def quad(total, axis, first):
    bit = first
    while 2 * bit < lax.axis_size(axis):
        one, two, three = (flip(total, axis, bit * mask) for mask in (1, 2, 3))
        total = (total + one) + (two + three)
        bit *= 4
    return butterfly(total, axis, bit)


def stepped(half, total):
    return half - PROBE_STEP * total[:2] / (total[2] + REGULARIZER)


def shape_of(spec):
    return spec if isinstance(spec, jax.ShapeDtypeStruct) else jax.ShapeDtypeStruct(spec, jnp.float32)


def call(kernel, outs, scratch, args, aliases={}, space=pltpu.VMEM):
    vmem = pl.BlockSpec(memory_space=pltpu.VMEM)
    return pl.pallas_call(
        kernel,
        out_shape=[shape_of(spec) for spec in outs],
        in_specs=[pl.BlockSpec(memory_space=space)] * len(args),
        out_specs=[vmem] * len(outs),
        scratch_shapes=[pltpu.VMEM(shape, jnp.float32) if isinstance(shape, tuple) else shape for shape in scratch],
        compiler_params=pltpu.CompilerParams(vmem_limit_bytes=VMEM_BYTES),
        input_output_aliases=aliases,
    )(*args)


def local(object_field, probe_field, intensities, off_rows, off_cols, counts):
    tall, wide = object_field.shape[1:]
    length = probe_field.shape[1]
    slots = off_rows.shape[2]
    half = length // 2
    high = tall + length
    blocks = wide // LANES
    tables = jnp.asarray(dft_parts(length))
    measured = intensities.reshape(slots, length, length)
    count_rows, count_cols = lax.axis_size("row"), lax.axis_size("col")

    def info_space(tiles):
        return [pltpu.SMEM((tiles, INFO, LANES), jnp.float32), pltpu.SemaphoreType.DMA((3,))]

    extended = (2, blocks + 1, high, LANES)
    ext, right, below, corner = call(
        halo_kernel,
        [extended, (2, tall, length), (2, length, wide), (2, length, length)],
        [pltpu.SemaphoreType.DMA((3 + 2 * blocks,))],
        [object_field],
        space=pl.ANY,
    )
    probe_now, own, measured, tables, info = call(
        load_kernel,
        [
            (2, length, length),
            (2, half, length),
            jax.ShapeDtypeStruct(measured.shape, measured.dtype),
            jax.ShapeDtypeStruct(tables.shape, tables.dtype),
            (INFO, LANES),
        ],
        [
            pltpu.SMEM(off_rows.shape, jnp.int32),
            pltpu.SMEM(off_cols.shape, jnp.int32),
            pltpu.SMEM(counts.shape, jnp.int32),
            pltpu.SemaphoreType.DMA((7,)),
        ],
        [probe_field, measured, tables, off_rows, off_cols, counts],
        space=pl.ANY,
    )
    right = shift(right, "col", -1)
    corner = lax.ppermute(
        corner,
        ("row", "col"),
        [
            ((r + 1) * count_cols + c + 1, r * count_cols + c)
            for r in range(count_rows - 1)
            for c in range(count_cols - 1)
        ],
    )
    below = shift(below, "row", -1)
    size = 2 * high
    strip = (size + INFO, LANES)
    partial = (3, half, length)
    deposits = [(blocks + 1, size, LANES), (3, length, length)] + info_space(1)
    ext, keep, send, inner, middle, outer = call(
        first_kernel,
        [extended, partial, partial, strip, (size, LANES), strip],
        deposits,
        [ext, right, below, corner, probe_now, measured, tables, info],
        aliases={0: 0},
    )
    last_row, last_col = count_rows // 2, count_cols // 2
    edge = (2 * (blocks + 1) * length + 3 * INFO, LANES)
    padded = (blocks + 3, high + 2 * length, LANES)

    from_inner = swap(inner, "col", 0)
    from_outer = swap(outer, "col", 1)
    total, inner, outer, infos = call(
        strips_kernel,
        [(blocks + 1, size, LANES), edge, edge, (3, INFO, LANES)],
        [],
        [inner, middle, outer, from_inner, from_outer],
    )
    part = keep + flip(send, "row", 1)
    part = quad(part, "row", 2)
    ext, light = call(
        functools.partial(near_light_kernel, slots, tall),
        [extended, padded],
        [(length, length)] + info_space(3),
        [ext, infos, probe_now, total],
        aliases={0: 0},
    )
    part, inner, outer = tie(part, inner, outer)
    from_inner = swap(inner, "row", 0)
    from_outer = swap(outer, "row", 1)
    row_infos = []

    def update(ext, light, strip, outer):
        ext, light, info_rows = call(
            functools.partial(object_kernel, slots, outer),
            [extended, padded, (3, INFO, LANES)],
            [(length, length)] + info_space(9),
            [ext, light, probe_now, total, strip],
            aliases={0: 0, 1: 1},
        )
        row_infos.append(info_rows)
        return ext, light

    part = butterfly(part, "col", 1, last_col)
    part, from_inner, light = tie(part, from_inner, light)
    ext, light = update(ext, light, from_inner, 0)
    part = butterfly(part, "col", last_col)
    new_half = stepped(own, part)
    tile, _ = update(ext, light, from_outer, 1)
    new_half, tile = tie(new_half, tile)
    (patches,) = call(patch_kernel, [(slots, 2, length, length)], info_space(1), [tile, info])
    new_other = flip(new_half, "row", 1)

    body_shape = (blocks + 1, 2 * tall, LANES)
    bottom_shape = (blocks + 1, 2 * length, LANES)
    keep, send, updates = call(
        second_kernel,
        [partial, partial, (slots, 2, length, length)],
        [(3, length, length)] + info_space(1),
        [patches, new_half, new_other, measured, tables, info],
    )
    body, bottom = call(
        deposit_kernel,
        [body_shape, bottom_shape],
        [(blocks + 1, size, LANES)] + info_space(1),
        [updates, new_half, new_other, info],
    )
    padded = (blocks + 2, tall + 2 * length, LANES)
    (light,) = call(
        functools.partial(light_kernel, slots),
        [(blocks, tall, LANES)],
        [padded, (length, length)] + info_space(9),
        [infos, *row_infos, new_half, new_other],
    )
    from_above = shift(bottom, "row", 1)
    (right,) = call(push_kernel, [(2 * tall, LANES)], [], [body, from_above])
    part = keep + flip(send, "row", 1)
    part, bottom = tie(part, bottom)
    part = butterfly(part, "col", 1, last_col)
    part = butterfly(part, "col", last_col)
    from_left = shift(right, "col", 1)
    part = butterfly(part, "row", 2, last_row)
    part, light = tie(part, light)
    part = butterfly(part, "row", last_row)
    last_half = stepped(new_half, part)
    last_other = flip(last_half, "row", 1)
    return call(
        final_kernel,
        [(2, tall, wide), (2, length, length)],
        [],
        [tile, light, body, from_above, from_left, last_half, last_other],
    )


def solution(mesh):
    placed = (
        P(None, "row", "col"),
        P(),
        P("row", "col", None, None, None),
        P("row", "col", None),
        P("row", "col", None),
        P("row", "col"),
    )
    return jax.shard_map(
        local, mesh=mesh, in_specs=placed, out_specs=(P(None, "row", "col"), P()), check_vma=False
    )
```

```python
import functools
import math

import jax
import jax.numpy as jnp
import numpy as np
from jax import lax
from jax.experimental import pallas as pl
from jax.experimental.pallas import tpu as pltpu
from jax.sharding import PartitionSpec as P

STEP_SIZE = 0.25
PROBE_STEP = 1.0
REGULARIZER = 1.0
COUNT_SCALE = 1.0 / 1024.0
LANES = 128
INFO = 8
VMEM_BYTES = 12 * 1024 * 1024


def dft_parts(length):
    points = np.arange(length)
    angles = (points[:, None] * points[None, :] % length) * (2.0 * math.pi / length)
    cosine = np.cos(angles) / math.sqrt(length)
    sine = np.sin(angles) / math.sqrt(length)
    forward = np.block([[cosine, -sine], [sine, cosine]]).astype(np.float32)
    parts = []
    for table in (forward, forward.T):
        high = table.astype(jnp.bfloat16)
        low = (table - high.astype(np.float32)).astype(jnp.bfloat16)
        parts += [high, low]
    return np.stack(parts)


def split(values):
    high = values.astype(jnp.bfloat16)
    low = (values - high.astype(jnp.float32)).astype(jnp.bfloat16)
    return high, low


def dot(left, right):
    return jnp.dot(left, right, preferred_element_type=jnp.float32)


def right_table(values, table_high, table_low):
    high, low = split(values)
    return dot(high, table_high) + (dot(high, table_low) + dot(low, table_high))


def left_table(table_high, table_low, values):
    high, low = split(values)
    rows = table_high.shape[0]
    both = dot(jnp.concatenate([table_high, table_low], axis=0), high)
    return both[:rows] + (both[rows:] + dot(table_high, low))


def parity(axis):
    return lax.axis_index(axis) % 2


def slot_place(info_ref, index, slot, slots):
    row = info_ref[index, 0, slot].astype(jnp.int32)
    col = info_ref[index, 0, slots + slot].astype(jnp.int32)
    return row, col, info_ref[index, 0, 2 * slots + slot]


def lane_index(length):
    return lax.broadcasted_iota(jnp.int32, (length, LANES), 1)


def take_patch(ext_ref, channel, row, col, length):
    block = col // LANES
    shift = col % LANES
    turn = (LANES - shift) % LANES
    first = pltpu.roll(ext_ref[channel, block, pl.ds(row, length), :], turn, 1)
    second = pltpu.roll(ext_ref[channel, block + 1, pl.ds(row, length), :], turn, 1)
    return jnp.where(lane_index(length) < LANES - shift, first, second)


def add_patch(acc_ref, row, col, values, length):
    block = col // LANES
    shift = col % LANES
    turned = pltpu.roll(values, shift, 1)
    late = lane_index(length) >= shift
    window = pl.ds(row, length)
    acc_ref[block, window, :] += jnp.where(late, turned, 0.0)
    acc_ref[block + 1, window, :] += jnp.where(late, 0.0, turned)


def add_light(light_ref, power_ref, row, col, weight, length):
    row, col = row + length, col + length
    inside = (row > 0) & (row < light_ref.shape[1] - length) & (col > 0) & (col < (light_ref.shape[0] - 1) * LANES)

    @pl.when(inside & (weight > 0.0))
    def _():
        add_patch(light_ref, row, col, power_ref[...], length)


def add_tile(light_ref, power_ref, info_ref, index, down, across, tall, wide, slots, length):
    for s in range(slots):
        row, col, weight = slot_place(info_ref, index, s, slots)
        add_light(light_ref, power_ref, row + down * tall, col + across * wide, weight, length)


def add_tiles(light_ref, power_ref, info_ref, tiles, tall, wide, slots, length):
    across = 1 - 2 * parity("col")
    down = 1 - 2 * parity("row")
    places = [(0, 0), (0, across), (0, -across)]
    places += [(down, step) for step in (-1, 0, 1)] + [(-down, step) for step in (-1, 0, 1)]
    for index in tiles:
        add_tile(light_ref, power_ref, info_ref, index, *places[index], tall, wide, slots, length)


def fill_info(rows_ref, cols_ref, counts_ref, slots):
    lanes = lax.broadcasted_iota(jnp.int32, (INFO, LANES), 1)
    info = jnp.zeros((INFO, LANES), jnp.float32)
    count = counts_ref[0, 0]
    upper = lax.axis_index("row") < lax.axis_size("row") // 2
    for s in range(slots):
        inside = jnp.where(upper, s < count, s >= slots - count)
        weight = jnp.where(inside, 1.0, 0.0).astype(jnp.float32)
        info = jnp.where(lanes == s, rows_ref[0, 0, s].astype(jnp.float32), info)
        info = jnp.where(lanes == slots + s, cols_ref[0, 0, s].astype(jnp.float32), info)
        info = jnp.where(lanes == 2 * slots + s, weight, info)
    return info


def position_terms(patches, probe_real, probe_imag, measured_ref, tables_ref, weights, slots, length):
    forward_high, forward_low = tables_ref[0], tables_ref[1]
    backward_high, backward_low = tables_ref[2], tables_ref[3]
    exits = []
    for patch_real, patch_imag in patches:
        exits.append(
            jnp.concatenate(
                [
                    probe_real * patch_real - probe_imag * patch_imag,
                    probe_real * patch_imag + probe_imag * patch_real,
                ],
                axis=1,
            )
        )
    mid = right_table(jnp.concatenate(exits, axis=0), forward_high, forward_low)
    mid = jnp.concatenate(
        [
            jnp.concatenate(
                [
                    mid[s * length : (s + 1) * length, :length],
                    mid[s * length : (s + 1) * length, length:],
                ],
                axis=0,
            )
            for s in range(slots)
        ],
        axis=1,
    )
    freq = left_table(backward_high, backward_low, mid)
    scaled = []
    for s in range(slots):
        freq_real = freq[:length, s * length : (s + 1) * length]
        freq_imag = freq[length:, s * length : (s + 1) * length]
        measured = measured_ref[s].astype(jnp.float32)
        residual = freq_real * freq_real + freq_imag * freq_imag - COUNT_SCALE * measured
        scaled.append(jnp.concatenate([residual * freq_real, residual * freq_imag], axis=0))
    mid = left_table(forward_high, forward_low, jnp.concatenate(scaled, axis=1))
    mid = jnp.concatenate(
        [
            jnp.concatenate(
                [
                    mid[:length, s * length : (s + 1) * length],
                    mid[length:, s * length : (s + 1) * length],
                ],
                axis=1,
            )
            for s in range(slots)
        ],
        axis=0,
    )
    back = right_table(mid, backward_high, backward_low)
    updates = []
    for s in range(slots):
        rows = slice(s * length, (s + 1) * length)
        updates.append((back[rows, :length] * weights[s], back[rows, length:] * weights[s]))
    return updates


def probe_sums(patches, updates, weights, keep_ref, send_ref, sum_ref, length):
    slots = len(patches)
    grad_real = jnp.zeros((length, length), jnp.float32)
    grad_imag = grad_real
    light = grad_real
    for s in range(slots):
        (patch_real, patch_imag), (back_real, back_imag) = patches[s], updates[s]
        grad_real += patch_real * back_real + patch_imag * back_imag
        grad_imag += patch_real * back_imag - patch_imag * back_real
        light += weights[s] * (patch_real * patch_real + patch_imag * patch_imag)
    sum_ref[0] = grad_real
    sum_ref[1] = grad_imag
    sum_ref[2] = light
    half = length // 2
    side = parity("row")
    keep_ref[...] = sum_ref[:, pl.ds(pl.multiple_of(side * half, half), half), :]
    send_ref[...] = sum_ref[:, pl.ds(pl.multiple_of((1 - side) * half, half), half), :]


def deposit(updates, probe_real, probe_imag, places, dep_ref, length):
    dep_ref[...] = jnp.zeros_like(dep_ref)
    high = dep_ref.shape[1] // 2
    for s in range(len(updates)):
        back_real, back_imag = updates[s]
        row, col, _ = places[s]
        add_patch(dep_ref, row, col, probe_real * back_real + probe_imag * back_imag, length)
        add_patch(dep_ref, row + high, col, probe_real * back_imag - probe_imag * back_real, length)


def start_all(pairs, sems):
    copies = [pltpu.make_async_copy(source, target, sems.at[i]) for i, (source, target) in enumerate(pairs)]
    for copy in copies:
        copy.start()
    return copies


def wait_all(copies):
    for copy in copies:
        copy.wait()


def halo_kernel(field_ref, ext_ref, right_out, below_out, corner_out, sems):
    length = corner_out.shape[1]
    blocks = ext_ref.shape[1] - 1
    tall = field_ref.shape[1]
    pairs = [
        (field_ref.at[:, :, pl.ds(0, length)], right_out),
        (field_ref.at[:, pl.ds(0, length), :], below_out),
        (field_ref.at[:, pl.ds(0, length), pl.ds(0, length)], corner_out),
    ]
    for block in range(blocks):
        for channel in range(2):
            pairs.append(
                (
                    field_ref.at[channel, :, pl.ds(block * LANES, LANES)],
                    ext_ref.at[channel, block, pl.ds(0, tall), :],
                )
            )
    wait_all(start_all(pairs, sems))


def load_kernel(
    probe_ref, measured_ref, tables_ref, rows_ref, cols_ref, counts_ref,
    probe_out, half_out, measured_out, tables_out, info_out, rows_at, cols_at, counts_at, sems,
):
    half = half_out.shape[1]
    start = pl.multiple_of(parity("row") * half, half)
    pairs = [
        (rows_ref, rows_at),
        (cols_ref, cols_at),
        (counts_ref, counts_at),
        (probe_ref, probe_out),
        (probe_ref.at[:, pl.ds(start, half), :], half_out),
        (measured_ref, measured_out),
        (tables_ref, tables_out),
    ]
    copies = start_all(pairs, sems)
    wait_all(copies[:3])
    info_out[...] = fill_info(rows_at, cols_at, counts_at, rows_at.shape[2])
    wait_all(copies[3:])


def split_sides(inner_out, outer_out, dep_ref):
    size = dep_ref.shape[1]
    side = parity("col")
    inner_out[:size] = dep_ref[2 - 2 * side]
    outer_out[:size] = dep_ref[2 * side]


def first_kernel(
    start_ref, right_ref, below_ref, corner_ref, probe_ref, measured_ref, tables_ref, info_ref,
    ext_ref, keep_ref, send_ref, inner_out, middle_out, outer_out, dep_ref, sum_ref, info_at, sems,
):
    copies = start_all([(info_ref, info_at.at[0])], sems)
    length = probe_ref.shape[1]
    slots = measured_ref.shape[0]
    tall = right_ref.shape[1]
    blocks = below_ref.shape[2] // LANES
    for channel in range(2):
        for block in range(blocks):
            lanes = slice(block * LANES, (block + 1) * LANES)
            ext_ref[channel, block, tall:, :] = below_ref[channel, :, lanes]
        ext_ref[channel, blocks, :tall, :] = right_ref[channel]
        ext_ref[channel, blocks, tall:, :] = corner_ref[channel]
    probe_real, probe_imag = probe_ref[0], probe_ref[1]
    wait_all(copies)
    places = [slot_place(info_at, 0, s, slots) for s in range(slots)]
    patches = [
        [take_patch(ext_ref, channel, places[s][0], places[s][1], length) for channel in range(2)] for s in range(slots)
    ]
    weights = [place[2] for place in places]
    updates = position_terms(
        patches, probe_real, probe_imag, measured_ref, tables_ref, weights, slots, length
    )
    probe_sums(patches, updates, weights, keep_ref, send_ref, sum_ref, length)
    deposit(updates, probe_real, probe_imag, places, dep_ref, length)
    size = dep_ref.shape[1]
    middle_out[...] = dep_ref[1]
    split_sides(inner_out, outer_out, dep_ref)
    inner_out[size:] = info_ref[...]
    outer_out[size:] = info_ref[...]


def strips_kernel(
    inner_ref, middle_ref, outer_ref, from_inner, from_outer, total_out, inner_out, outer_out, infos_out
):
    size = middle_ref.shape[0]
    high = size // 2
    length = (inner_out.shape[0] - 3 * INFO) // 6
    tall = high - length
    side = parity("col")
    total_out[2 - 2 * side] = inner_ref[:size] + from_inner[:size]
    total_out[1] = middle_ref[...]
    total_out[2 * side] = outer_ref[:size] + from_outer[:size]
    side_row = parity("row")
    for block in range(3):
        for channel in range(2):
            rows = slice((2 * block + channel) * length, (2 * block + channel + 1) * length)
            start = channel * high + tall - side_row * tall
            inner_out[rows] = total_out[block, pl.ds(pl.multiple_of(start, 8), length), :]
            start = channel * high + side_row * tall
            outer_out[rows] = total_out[block, pl.ds(pl.multiple_of(start, 8), length), :]
    own, inner, outer = inner_ref[size:], from_inner[size:], from_outer[size:]
    infos_out[0], infos_out[1], infos_out[2] = own, inner, outer
    left = jnp.where(side == 0, outer, inner)
    right = jnp.where(side == 0, inner, outer)
    for index, info in enumerate((left, own, right)):
        rows = slice(6 * length + index * INFO, 6 * length + (index + 1) * INFO)
        inner_out[rows] = info
        outer_out[rows] = info


def update_rows(new_ref, ext_ref, light_ref, total_ref, extra, block, start, stop, length, inside):
    high = ext_ref.shape[2]
    scale = STEP_SIZE / (light_ref[block + 1, start + length : stop + length, :] + REGULARIZER)
    if inside is not None:
        scale = scale * inside
    for channel in range(2):
        total = total_ref[block, channel * high + start : channel * high + stop]
        if extra is not None:
            total = total + extra(2 * block + channel)
        new_ref[channel, block, start:stop, :] = ext_ref[channel, block, start:stop, :] - scale * total


def inside_mesh(axis):
    return jnp.where(lax.axis_index(axis) < lax.axis_size(axis) - 1, 1.0, 0.0).astype(jnp.float32)


def near_light_kernel(
    slots, tall, ext_ref, infos_ref, probe_ref, total_ref, new_ref, light_out, power_ref, info_at, sems
):
    copies = start_all([(infos_ref, info_at)], sems)
    length = power_ref.shape[0]
    power_ref[...] = probe_ref[0] * probe_ref[0] + probe_ref[1] * probe_ref[1]
    light_out[...] = jnp.zeros_like(light_out)
    wait_all(copies)
    wide = (light_out.shape[0] - 3) * LANES
    add_tiles(light_out, power_ref, info_at, range(3), tall, wide, slots, length)
    blocks = ext_ref.shape[1] - 1
    for block in range(blocks + 1):
        inside = inside_mesh("col") if block == blocks else None
        update_rows(new_ref, ext_ref, light_out, total_ref, None, block, length, tall, length, inside)


def object_kernel(
    slots, outer, ext_ref, light_in, probe_ref, total_ref, strip_ref, new_ref, light_ref, info_out, power_ref, info_at, sems
):
    length = power_ref.shape[0]
    high = ext_ref.shape[2]
    tall = high - length
    blocks = ext_ref.shape[1] - 1
    edge = 6 * length
    for index in range(3):
        info_out[index] = strip_ref[edge + index * INFO : edge + (index + 1) * INFO]
    copies = start_all([(info_out, info_at.at[pl.ds(3 + 3 * outer, 3)])], sems)
    power_ref[...] = probe_ref[0] * probe_ref[0] + probe_ref[1] * probe_ref[1]
    side = parity("row")
    below = side if outer else 1 - side
    start = below * tall
    inside_row = jnp.where(below == 1, inside_mesh("row"), 1.0)
    wait_all(copies)
    add_tiles(light_ref, power_ref, info_at, range(3 + 3 * outer, 6 + 3 * outer), tall, blocks * LANES, slots, length)
    window = pl.ds(pl.multiple_of(start, 8), length)
    for block in range(blocks + 1):
        light = light_ref[block + 1, pl.ds(pl.multiple_of(start + length, 8), length), :]
        inside = inside_row * inside_mesh("col") if block == blocks else inside_row
        scale = inside * (STEP_SIZE / (light + REGULARIZER))
        for channel in range(2):
            index = 2 * block + channel
            total = total_ref[block, pl.ds(pl.multiple_of(start + channel * high, 8), length), :]
            total = total + strip_ref[index * length : (index + 1) * length]
            new_ref[channel, block, window, :] = ext_ref[channel, block, window, :] - scale * total


def patch_kernel(ext_ref, info_ref, patches_out, info_at, sems):
    copies = start_all([(info_ref, info_at.at[0])], sems)
    slots, _, length, _ = patches_out.shape
    wait_all(copies)
    for s in range(slots):
        row, col, _ = slot_place(info_at, 0, s, slots)
        for channel in range(2):
            patches_out[s, channel] = take_patch(ext_ref, channel, row, col, length)


def assemble_probe(half_ref, other_ref, side):
    first = side == 0
    return [
        jnp.concatenate(
            [
                jnp.where(first, half_ref[channel], other_ref[channel]),
                jnp.where(first, other_ref[channel], half_ref[channel]),
            ],
            axis=0,
        )
        for channel in range(2)
    ]


def second_kernel(
    patches_ref, half_ref, other_ref, measured_ref, tables_ref, info_ref,
    keep_ref, send_ref, updates_out, sum_ref, info_at, sems,
):
    copies = start_all([(info_ref, info_at.at[0])], sems)
    slots = measured_ref.shape[0]
    length = measured_ref.shape[1]
    probe_real, probe_imag = assemble_probe(half_ref, other_ref, parity("row"))
    patches = [[patches_ref[s, channel] for channel in range(2)] for s in range(slots)]
    wait_all(copies)
    weights = [slot_place(info_at, 0, s, slots)[2] for s in range(slots)]
    updates = position_terms(
        patches, probe_real, probe_imag, measured_ref, tables_ref, weights, slots, length
    )
    probe_sums(patches, updates, weights, keep_ref, send_ref, sum_ref, length)
    for s in range(slots):
        updates_out[s, 0], updates_out[s, 1] = updates[s]


def deposit_kernel(updates_ref, half_ref, other_ref, info_ref, body_out, bottom_out, dep_ref, info_at, sems):
    copies = start_all([(info_ref, info_at.at[0])], sems)
    slots, _, length, _ = updates_ref.shape
    probe_real, probe_imag = assemble_probe(half_ref, other_ref, parity("row"))
    wait_all(copies)
    places = [slot_place(info_at, 0, s, slots) for s in range(slots)]
    updates = [(updates_ref[s, 0], updates_ref[s, 1]) for s in range(slots)]
    deposit(updates, probe_real, probe_imag, places, dep_ref, length)
    high = dep_ref.shape[1] // 2
    tall = body_out.shape[1] // 2
    for channel in range(2):
        start = channel * high
        body_out[:, channel * tall : (channel + 1) * tall] = dep_ref[:, start : start + tall, :]
        bottom_out[:, channel * length : (channel + 1) * length] = dep_ref[:, start + tall : start + high, :]


def light_kernel(
    slots, near_ref, inner_ref, outer_ref, half_ref, other_ref, light_out, light_ref, power_ref, info_at, sems
):
    parts = (near_ref, inner_ref, outer_ref)
    copies = start_all([(part, info_at.at[pl.ds(3 * index, 3)]) for index, part in enumerate(parts)], sems)
    length = power_ref.shape[0]
    tall = light_out.shape[1]
    blocks = light_out.shape[0]
    probe_real, probe_imag = assemble_probe(half_ref, other_ref, parity("row"))
    power_ref[...] = probe_real * probe_real + probe_imag * probe_imag
    light_ref[...] = jnp.zeros_like(light_ref)
    wait_all(copies)
    left, above = 2 - parity("col"), 6 - 3 * parity("row")
    for index, down, across in ((0, 0, 0), (left, 0, -1), (above, -1, -1), (above + 1, -1, 0)):
        add_tile(light_ref, power_ref, info_at, index, down, across, tall, blocks * LANES, slots, length)
    light_out[...] = STEP_SIZE / (light_ref[1 : 1 + blocks, length : length + tall, :] + REGULARIZER)


def push_kernel(body_ref, from_above, right_out):
    tall = body_ref.shape[1] // 2
    length = from_above.shape[1] // 2
    last = body_ref.shape[0] - 1
    for channel in range(2):
        start = channel * tall
        right_out[start : start + length] = (
            body_ref[last, start : start + length] + from_above[last, channel * length : (channel + 1) * length]
        )
        right_out[start + length : start + tall] = body_ref[last, start + length : start + tall]


def final_kernel(tile_ref, light_ref, body_ref, from_above, from_left, half_ref, other_ref, object_out, probe_out):
    tall = body_ref.shape[1] // 2
    length = from_above.shape[1] // 2
    for block in range(light_ref.shape[0]):
        lanes = slice(block * LANES, (block + 1) * LANES)
        for channel in range(2):
            for start, stop in ((0, length), (length, tall)):
                rows = slice(channel * tall + start, channel * tall + stop)
                total = body_ref[block, rows]
                if start == 0:
                    total = total + from_above[block, channel * length : (channel + 1) * length]
                if block == 0:
                    total = total + from_left[rows]
                object_out[channel, start:stop, lanes] = (
                    tile_ref[channel, block, start:stop, :] - light_ref[block, start:stop, :] * total
                )
    probe_out[0], probe_out[1] = assemble_probe(half_ref, other_ref, parity("row"))


def shift(value, axis, steps):
    count = lax.axis_size(axis)
    pairs = [(source, source + steps) for source in range(count) if 0 <= source + steps < count]
    return lax.ppermute(value, axis, pairs)


def swap(value, axis, first):
    count = lax.axis_size(axis)
    pairs = []
    for low in range(first, count - 1, 2):
        pairs += [(low, low + 1), (low + 1, low)]
    return lax.ppermute(value, axis, pairs)


def flip(value, axis, mask):
    count = lax.axis_size(axis)
    return lax.ppermute(value, axis, [(source, source ^ mask) for source in range(count)])


def tie(*values):
    return lax.optimization_barrier(values)


def butterfly(total, axis, first, stop=None):
    bit = first
    while bit < (stop or lax.axis_size(axis)):
        total = total + flip(total, axis, bit)
        bit *= 2
    return total


def quad(total, axis, first):
    bit = first
    while 2 * bit < lax.axis_size(axis):
        one, two, three = (flip(total, axis, bit * mask) for mask in (1, 2, 3))
        total = (total + one) + (two + three)
        bit *= 4
    return butterfly(total, axis, bit)


def stepped(half, total):
    return half - PROBE_STEP * total[:2] / (total[2] + REGULARIZER)


def shape_of(spec):
    return spec if isinstance(spec, jax.ShapeDtypeStruct) else jax.ShapeDtypeStruct(spec, jnp.float32)


def call(kernel, outs, scratch, args, aliases={}, space=pltpu.VMEM):
    vmem = pl.BlockSpec(memory_space=pltpu.VMEM)
    return pl.pallas_call(
        kernel,
        out_shape=[shape_of(spec) for spec in outs],
        in_specs=[pl.BlockSpec(memory_space=space)] * len(args),
        out_specs=[vmem] * len(outs),
        scratch_shapes=[pltpu.VMEM(shape, jnp.float32) if isinstance(shape, tuple) else shape for shape in scratch],
        compiler_params=pltpu.CompilerParams(vmem_limit_bytes=VMEM_BYTES),
        input_output_aliases=aliases,
    )(*args)


def local(object_field, probe_field, intensities, off_rows, off_cols, counts):
    tall, wide = object_field.shape[1:]
    length = probe_field.shape[1]
    slots = off_rows.shape[2]
    half = length // 2
    high = tall + length
    blocks = wide // LANES
    tables = jnp.asarray(dft_parts(length))
    measured = intensities.reshape(slots, length, length)
    count_rows, count_cols = lax.axis_size("row"), lax.axis_size("col")

    def info_space(tiles):
        return [pltpu.SMEM((tiles, INFO, LANES), jnp.float32), pltpu.SemaphoreType.DMA((3,))]

    extended = (2, blocks + 1, high, LANES)
    ext, right, below, corner = call(
        halo_kernel,
        [extended, (2, tall, length), (2, length, wide), (2, length, length)],
        [pltpu.SemaphoreType.DMA((3 + 2 * blocks,))],
        [object_field],
        space=pl.ANY,
    )
    probe_now, own, measured, tables, info = call(
        load_kernel,
        [
            (2, length, length),
            (2, half, length),
            jax.ShapeDtypeStruct(measured.shape, measured.dtype),
            jax.ShapeDtypeStruct(tables.shape, tables.dtype),
            (INFO, LANES),
        ],
        [
            pltpu.SMEM(off_rows.shape, jnp.int32),
            pltpu.SMEM(off_cols.shape, jnp.int32),
            pltpu.SMEM(counts.shape, jnp.int32),
            pltpu.SemaphoreType.DMA((7,)),
        ],
        [probe_field, measured, tables, off_rows, off_cols, counts],
        space=pl.ANY,
    )
    right = shift(right, "col", -1)
    corner = lax.ppermute(
        corner,
        ("row", "col"),
        [
            ((r + 1) * count_cols + c + 1, r * count_cols + c)
            for r in range(count_rows - 1)
            for c in range(count_cols - 1)
        ],
    )
    below = shift(below, "row", -1)
    size = 2 * high
    strip = (size + INFO, LANES)
    partial = (3, half, length)
    deposits = [(blocks + 1, size, LANES), (3, length, length)] + info_space(1)
    ext, keep, send, inner, middle, outer = call(
        first_kernel,
        [extended, partial, partial, strip, (size, LANES), strip],
        deposits,
        [ext, right, below, corner, probe_now, measured, tables, info],
        aliases={0: 0},
    )
    last_row, last_col = count_rows // 2, count_cols // 2
    edge = (2 * (blocks + 1) * length + 3 * INFO, LANES)
    padded = (blocks + 3, high + 2 * length, LANES)

    from_inner = swap(inner, "col", 0)
    from_outer = swap(outer, "col", 1)
    total, inner, outer, infos = call(
        strips_kernel,
        [(blocks + 1, size, LANES), edge, edge, (3, INFO, LANES)],
        [],
        [inner, middle, outer, from_inner, from_outer],
    )
    part = keep + flip(send, "row", 1)
    part = quad(part, "row", 2)
    ext, light = call(
        functools.partial(near_light_kernel, slots, tall),
        [extended, padded],
        [(length, length)] + info_space(3),
        [ext, infos, probe_now, total],
        aliases={0: 0},
    )
    part, inner, outer = tie(part, inner, outer)
    from_inner = swap(inner, "row", 0)
    from_outer = swap(outer, "row", 1)
    row_infos = []

    def update(ext, light, strip, outer):
        ext, light, info_rows = call(
            functools.partial(object_kernel, slots, outer),
            [extended, padded, (3, INFO, LANES)],
            [(length, length)] + info_space(9),
            [ext, light, probe_now, total, strip],
            aliases={0: 0, 1: 1},
        )
        row_infos.append(info_rows)
        return ext, light

    part = butterfly(part, "col", last_col)
    part, from_inner, light = tie(part, from_inner, light)
    ext, light = update(ext, light, from_inner, 0)
    part = butterfly(part, "col", 1, last_col)
    new_half = stepped(own, part)
    tile, _ = update(ext, light, from_outer, 1)
    new_half, tile = tie(new_half, tile)
    (patches,) = call(patch_kernel, [(slots, 2, length, length)], info_space(1), [tile, info])
    new_other = flip(new_half, "row", 1)

    body_shape = (blocks + 1, 2 * tall, LANES)
    bottom_shape = (blocks + 1, 2 * length, LANES)
    keep, send, updates = call(
        second_kernel,
        [partial, partial, (slots, 2, length, length)],
        [(3, length, length)] + info_space(1),
        [patches, new_half, new_other, measured, tables, info],
    )
    body, bottom = call(
        deposit_kernel,
        [body_shape, bottom_shape],
        [(blocks + 1, size, LANES)] + info_space(1),
        [updates, new_half, new_other, info],
    )
    padded = (blocks + 2, tall + 2 * length, LANES)
    (light,) = call(
        functools.partial(light_kernel, slots),
        [(blocks, tall, LANES)],
        [padded, (length, length)] + info_space(9),
        [infos, *row_infos, new_half, new_other],
    )
    from_above = shift(bottom, "row", 1)
    (right,) = call(push_kernel, [(2 * tall, LANES)], [], [body, from_above])
    part = keep + flip(send, "row", 1)
    part, bottom = tie(part, bottom)
    part = butterfly(part, "col", 1, last_col)
    part = butterfly(part, "col", last_col)
    from_left = shift(right, "col", 1)
    part = butterfly(part, "row", 2, last_row)
    part = butterfly(part, "row", last_row)
    last_half = stepped(new_half, part)
    last_other = flip(last_half, "row", 1)
    return call(
        final_kernel,
        [(2, tall, wide), (2, length, length)],
        [],
        [tile, light, body, from_above, from_left, last_half, last_other],
    )


def solution(mesh):
    placed = (
        P(None, "row", "col"),
        P(),
        P("row", "col", None, None, None),
        P("row", "col", None),
        P("row", "col", None),
        P("row", "col"),
    )
    return jax.shard_map(
        local, mesh=mesh, in_specs=placed, out_specs=(P(None, "row", "col"), P()), check_vma=False
    )
```
